32 devices in a mesh: dp: 8 (over z, y), tensor: 4 (over x, core).
Axes of the slice: x: 2, y: 2, z: 4, core: 2. Of those that a mesh axis runs over, the one named last changes fastest.
Arguments:
- tokens: bfloat16 [8192, 2048], P('dp', 'tensor'), may hold values from -6 to 6
- segments: int32 [8, 1024], P('dp'), may hold values from 0 to 3, never falling along the last dimension, each value on 1 to 512 neighbouring positions
- cotangent: bfloat16 [8192, 2048], P('dp', 'tensor'), may hold values from -6 to 6
- w_query: bfloat16 [2048, 2048], P(None, 'tensor'), may hold values from -1 to 1
- w_key: bfloat16 [2048, 2048], P(None, 'tensor'), may hold values from -1 to 1
- w_value: bfloat16 [2048, 2048], P(None, 'tensor'), may hold values from -0.125 to 0.125
- w_out: bfloat16 [2048, 2048], P('tensor'), may hold values from -0.125 to 0.125
- w_gate: bfloat16 [2048, 8192], P(None, 'tensor'), may hold values from -0.125 to 0.125
- w_up: bfloat16 [2048, 8192], P(None, 'tensor'), may hold values from -0.125 to 0.125
- w_down: bfloat16 [8192, 2048], P('tensor'), may hold values from -0.0625 to 0.0625
- gain_query: float32 [2048], P('tensor'), may hold values from 0.1 to 1.9
- gain_key: float32 [2048], P('tensor'), may hold values from 0.1 to 1.9
- gain_attn: float32 [2048], replicated, may hold values from 0.1 to 1.9
- gain_mlp: float32 [2048], replicated, may hold values from 0.1 to 1.9
Outputs:
- output: bfloat16 [8192, 2048], P('dp', 'tensor')
- input_grad: bfloat16 [8192, 2048], P('dp', 'tensor')
- w_query_grad: float32 [2048, 2048], P(None, 'tensor')
- w_key_grad: float32 [2048, 2048], P(None, 'tensor')
- w_value_grad: float32 [2048, 2048], P(None, 'tensor')
- w_out_grad: float32 [2048, 2048], P('tensor')
- w_gate_grad: float32 [2048, 8192], P(None, 'tensor')
- w_up_grad: float32 [2048, 8192], P(None, 'tensor')
- w_down_grad: float32 [8192, 2048], P('tensor')
- gain_query_grad: float32 [2048], P('tensor')
- gain_key_grad: float32 [2048], P('tensor')
- gain_attn_grad: float32 [2048], replicated
- gain_mlp_grad: float32 [2048], replicated
The draws below stay inside these ranges and needn't reach their ends.
Inputs may be any that keep to these rules, and one draw needn't show every extreme that they name: `segments`: along each sequence the segment numbers never fall; a document is a run of equal numbers, at most 512 tokens long, and some document has exactly that length.
All inputs are finite; a program needn't handle non-finite values.
Results may differ from the reference program's by a relative error of at most 0.025.
Values may be sent and summed in bfloat16 or wider, within the bound.
No kernel may reach another device: no remote copies, remote signals or barrier semaphores. Data moves between devices by JAX's collectives and lax.ppermute only.
A program may use at most 256 MiB of HBM per device.

```python
import math
import jax
import jax.numpy as jnp
import numpy as np
from jax import lax

D = 2048
HEADS = 16
HD = 128
FF = 8192
SEQ_LEN = 1024
SEQS = 8
TOKENS = 8192


def draw_tokens(key, part):
    base_key = jax.random.fold_in(jax.random.fold_in(key, 11), 0)
    values = jax.random.normal(base_key, (TOKENS, D), jnp.float32)
    return jnp.clip(values, -6.0, 6.0).astype(jnp.bfloat16)


def draw_w_query(key, part):
    values = jnp.clip(jax.random.normal(jax.random.fold_in(key, 21), (D, D), jnp.float32), -6.0, 6.0) * D ** (-0.5)
    return values.astype(jnp.bfloat16)


def draw_w_key(key, part):
    values = jnp.clip(jax.random.normal(jax.random.fold_in(key, 22), (D, D), jnp.float32), -6.0, 6.0) * D ** (-0.5)
    return values.astype(jnp.bfloat16)


def steps_of(rng, dims, pieces, low, largest):
    gain = 1.0
    for axis_at, shards_of in pieces:
        heights = jax.random.uniform(jax.random.fold_in(jax.random.fold_in(rng, 6), axis_at), (shards_of,), jnp.float32, low / len(pieces), largest / len(pieces))
        gain = gain * jnp.repeat(jnp.exp(heights), dims[axis_at] // shards_of).reshape((-1,) + (1,) * (len(dims) - 1 - axis_at))
    return gain


def length_profile(count, total, limit, skew):
    weights = [(1 << 20) // math.isqrt(rank ** skew) + 1 for rank in range(2, count + 1)]
    spare, counts = total - limit - (count - 1), [1] * (count - 1)
    while spare > 0:
        candidates = [i for i in range(count - 1) if counts[i] < limit]
        whole, left = sum([weights[i] for i in candidates]), spare
        for i in candidates:
            more = min(limit - counts[i], max(1, left * weights[i] // whole), spare)
            counts[i] = counts[i] + more
            spare = spare - more
    return np.array([limit] + counts)


def uneven_parts(rng, number_of, total, reach, lean):
    if number_of == 2:
        one = jax.random.randint(rng, (), max(1, total - reach), min(reach, total - 1) + 1)
        return jnp.stack([one, total - one])
    sizes = jnp.asarray(length_profile(number_of, total, reach, lean), jnp.int32)
    twos = (number_of - 1) // 2
    source_of, taker = sizes[1:1 + 2 * twos:2], sizes[2:2 + 2 * twos:2]
    room = jnp.minimum(source_of - 1, reach - taker)
    shifted = jax.random.randint(jax.random.fold_in(rng, 1), (twos,), 0, 1 << 20) % (room + 1)
    sizes = sizes.at[1:1 + 2 * twos:2].set(source_of - shifted).at[2:2 + 2 * twos:2].set(taker + shifted)
    return sizes[jax.random.permutation(jax.random.fold_in(rng, 2), number_of)]


def normal_values(own_key, dims, deviation, reach, cuts=(), kind=jnp.bfloat16):
    array = jax.random.normal(own_key, dims, jnp.float32) * deviation
    if len(cuts) > 0:
        array = steps_of(own_key, dims, cuts, -0.22, 0.18) * array
    return jnp.clip(array, min=-reach, max=reach).astype(kind)


def setup_inputs(seed: int = 0) -> dict:
    seeds = jax.random.split(jax.random.key(seed), 15)
    return {
        "tokens": draw_tokens(jax.random.fold_in(seeds[14], 71), 0),
        "segments": jax.vmap(lambda own: jnp.searchsorted(jnp.cumsum(uneven_parts(own, 4, SEQ_LEN, SEQ_LEN // 2, 0)), jnp.arange(SEQ_LEN), side="right"))(jax.random.split(seeds[1], SEQS)).reshape((SEQS, SEQ_LEN)).astype(jnp.int32),
        "cotangent": normal_values(seeds[2], (TOKENS, D), 1.0, 6.0, ((0, 8), (1, 4))),
        "w_query": draw_w_query(jax.random.fold_in(seeds[14], 71), 0),
        "w_key": draw_w_key(jax.random.fold_in(seeds[14], 71), 0),
        "w_value": normal_values(seeds[5], (D, D), D ** -0.5, 0.125, ((1, 4),)),
        "w_out": normal_values(seeds[6], (D, D), D ** -0.5, 0.125, ((0, 4),)),
        "w_gate": normal_values(seeds[7], (D, FF), D ** -0.5, 0.125, ((1, 4),)),
        "w_up": normal_values(seeds[8], (D, FF), D ** -0.5, 0.125, ((1, 4),)),
        "w_down": normal_values(seeds[9], (FF, D), FF ** -0.5, 0.0625, ((0, 4),)),
        "gain_query": jnp.clip(1.0 + 0.18 * jax.random.normal(seeds[10], (D,), jnp.float32), 0.1, 1.9),
        "gain_key": jnp.clip(1.0 + 0.18 * jax.random.normal(seeds[11], (D,), jnp.float32), 0.1, 1.9),
        "gain_attn": jnp.clip(1.0 + 0.18 * jax.random.normal(seeds[12], (D,), jnp.float32), 0.1, 1.9),
        "gain_mlp": jnp.clip(1.0 + 0.18 * jax.random.normal(seeds[13], (D,), jnp.float32), 0.1, 1.9),
    }


epsilon = 1e-06
rope_base = 500000.0

@jax.custom_vjp
def low(v):
    return lax.optimization_barrier(v.astype(jnp.bfloat16)).astype(jnp.float32)

@jax.custom_vjp
def low_back(v):
    return v

def low_keep(v):
    return (low(v), None)

def low_pass(kept, grad):
    return (grad,)

def back_keep(v):
    return (v, None)

def back_low(kept, grad):
    return (low(grad),)
low.defvjp(low_keep, low_pass)
low_back.defvjp(back_keep, back_low)

def product(left, right):
    return jnp.dot(left, right, precision=lax.Precision.HIGHEST)

def norm_rows(values, gains):
    return values * lax.rsqrt(lax.optimization_barrier(jnp.mean(values * values, axis=-1, keepdims=True)) + epsilon) * gains

def rotate(values, cosine, sine_table):
    half_dim = values.shape[-1] // 2
    turned = jnp.concatenate([-values[..., half_dim:], values[..., :half_dim]], axis=-1)
    return values * cosine + turned * sine_table

def tables(segments):
    length = segments.shape[-1]
    places = jnp.broadcast_to(jnp.arange(length, dtype=jnp.int32), segments.shape)
    starts = jnp.concatenate([jnp.ones(segments.shape[:-1] + (1,), dtype=bool), segments[..., 1:] != segments[..., :-1]], axis=-1)
    firsts = lax.cummax(jnp.where(starts, places, 0), axis=segments.ndim - 1)
    offsets = (places - firsts).astype(jnp.float32)
    freqs = jnp.power(rope_base, -jnp.arange(0, HD, 2).astype(jnp.float32) / HD)
    angles = offsets[..., None] * freqs
    angles = jnp.concatenate([angles, angles], axis=-1)
    return (jnp.cos(angles), jnp.sin(angles))

def attend(queries, keys_in, values_in, doc_ids):
    length = doc_ids.shape[0]
    places = jnp.arange(length)
    allowed = (doc_ids[:, None] == doc_ids[None, :]) & (places[:, None] >= places[None, :])
    scores = low_back(jnp.einsum('qhd,khd->hqk', queries, keys_in, precision=lax.Precision.HIGHEST) * HD ** (-0.5))
    scores = jnp.where(allowed[None], scores, -1e+30)
    weights = low(jax.nn.softmax(scores, axis=-1))
    return jnp.einsum('hqk,khd->qhd', weights, values_in, precision=lax.Precision.HIGHEST)

def attend_bundle(bundle):
    return attend(bundle[0], bundle[1], bundle[2], bundle[3])

def forward(inputs, w_query, w_key, w_value, w_out, w_gate, w_up, w_down, gain_query, gain_key, gain_attn, gain_mlp, cosine, sine_table, segments):
    seq_count = segments.shape[0]
    query_proj = low_back(product(inputs, w_query))
    key_proj = low_back(product(inputs, w_key))
    value_proj = low(low_back(product(inputs, w_value)))
    query_norm = norm_rows(query_proj, gain_query).reshape(seq_count, -1, HEADS, HD)
    key_norm = norm_rows(key_proj, gain_key).reshape(seq_count, -1, HEADS, HD)
    query_rot = low(rotate(query_norm, cosine[:, :, None], sine_table[:, :, None]))
    key_rot = low(rotate(key_norm, cosine[:, :, None], sine_table[:, :, None]))
    value_heads = value_proj.reshape(seq_count, -1, HEADS, HD)
    mixed_out = lax.map(jax.checkpoint(attend_bundle), (query_rot, key_rot, value_heads, segments))
    mixed_out = low(low_back(mixed_out.reshape(inputs.shape[0], -1)))
    attn_out = low_back(product(mixed_out, w_out))
    hidden = inputs + norm_rows(attn_out, gain_attn)
    hidden_low = low(hidden)
    gate_proj = low_back(product(hidden_low, w_gate))
    up_proj = low_back(product(hidden_low, w_up))
    act_low = low(jax.nn.silu(gate_proj) * up_proj)
    branch = low_back(product(act_low, w_down))
    return hidden + norm_rows(branch, gain_mlp)

def reference(tokens, segments, cotangent, w_query, w_key, w_value, w_out, w_gate, w_up, w_down, gain_query, gain_key, gain_attn, gain_mlp):
    cosine, sine_table = tables(segments)

    def run(inputs, wq_f, wk_f, wv_f, wo_f, wg_f, wu_f, wd_f, gq_f, gk_f, ga_f, gm_f):
        return forward(inputs, wq_f, wk_f, wv_f, wo_f, wg_f, wu_f, wd_f, gq_f, gk_f, ga_f, gm_f, cosine, sine_table, segments)
    result, pull = jax.vjp(run, tokens.astype(jnp.float32), w_query.astype(jnp.float32), w_key.astype(jnp.float32), w_value.astype(jnp.float32), w_out.astype(jnp.float32), w_gate.astype(jnp.float32), w_up.astype(jnp.float32), w_down.astype(jnp.float32), gain_query.astype(jnp.float32), gain_key.astype(jnp.float32), gain_attn.astype(jnp.float32), gain_mlp.astype(jnp.float32))
    grads = pull(cotangent.astype(jnp.float32))
    return (result.astype(jnp.bfloat16), grads[0].astype(jnp.bfloat16), grads[1], grads[2], grads[3], grads[4], grads[5], grads[6], grads[7], grads[8], grads[9], grads[10], grads[11])
```

```python
import jax
import jax.numpy as jnp
from jax import lax
from jax.experimental import pallas as pl
from jax.experimental.pallas import tpu as pltpu
from jax.sharding import PartitionSpec as P

HD = 128


epsilon = 1e-06
rope_base = 500000.0


def tables(segments):
    length = segments.shape[-1]
    places = jnp.broadcast_to(jnp.arange(length, dtype=jnp.int32), segments.shape)
    starts = jnp.concatenate(
        [jnp.ones(segments.shape[:-1] + (1,), dtype=bool), segments[..., 1:] != segments[..., :-1]],
        axis=-1,
    )
    firsts = lax.cummax(jnp.where(starts, places, 0), axis=segments.ndim - 1)
    offsets = (places - firsts).astype(jnp.float32)
    freqs = jnp.power(rope_base, -jnp.arange(0, HD, 2).astype(jnp.float32) / HD)
    angles = offsets[..., None] * freqs
    angles = jnp.concatenate([angles, angles], axis=-1)
    return (jnp.cos(angles), jnp.sin(angles))


def rotate(values, cosine, sine_table):
    half_dim = values.shape[-1] // 2
    turned = jnp.concatenate([-values[..., half_dim:], values[..., :half_dim]], axis=-1)
    return values * cosine + turned * sine_table


def rotate_back(gradient, cosine, sine_table):
    half_dim = gradient.shape[-1] // 2
    scaled = gradient * sine_table
    return gradient * cosine + jnp.concatenate(
        [scaled[..., half_dim:], -scaled[..., :half_dim]], axis=-1
    )


def column_sum(partial_value):
    return lax.psum_scatter(
        partial_value.astype(jnp.bfloat16), "tensor", scatter_dimension=1, tiled=True
    ).astype(jnp.float32)


def general_body(
    tokens,
    segments,
    cotangent,
    w_query,
    w_key,
    w_value,
    w_out,
    w_gate,
    w_up,
    w_down,
    gain_query,
    gain_key,
    gain_attn,
    gain_mlp,
):
    full_width = w_query.shape[0]
    row_count = tokens.shape[0]
    narrow = tokens.shape[1]
    local_width = w_query.shape[1]
    heads_here = local_width // HD
    tensor_rank = lax.axis_index("tensor")
    col_start = tensor_rank * narrow
    block_rows = min(512, row_count)
    block_count = row_count // block_rows
    score_scale = HD ** (-0.5)
    cosine, sine_table = tables(segments)
    cosine = cosine[0][:, None, :]
    sine_table = sine_table[0][:, None, :]
    doc_ids = segments[0]
    position = jnp.arange(row_count)
    gain_mlp_cols = lax.dynamic_slice_in_dim(gain_mlp, col_start, narrow, 0)
    whole_x, whole_dy = (
        lax.all_gather(tokens, "tensor", axis=1, tiled=True),
        lax.all_gather(cotangent, "tensor", axis=1, tiled=True),
    )
    query_proj = jnp.dot(whole_x, w_query, preferred_element_type=jnp.float32)
    key_proj = jnp.dot(whole_x, w_key, preferred_element_type=jnp.float32)
    value_proj = jnp.dot(whole_x, w_value, preferred_element_type=jnp.float32)
    query_sq, key_sq = lax.psum(
        (jnp.sum(query_proj * query_proj, 1), jnp.sum(key_proj * key_proj, 1)), "tensor"
    )
    query_scale = lax.rsqrt(query_sq / full_width + epsilon)[:, None]
    key_scale = lax.rsqrt(key_sq / full_width + epsilon)[:, None]
    query_rot = rotate(
        (query_proj * query_scale * gain_query).reshape(row_count, heads_here, HD),
        cosine,
        sine_table,
    ).astype(jnp.bfloat16)
    key_rot = rotate(
        (key_proj * key_scale * gain_key).reshape(row_count, heads_here, HD), cosine, sine_table
    ).astype(jnp.bfloat16)
    value_low = value_proj.astype(jnp.bfloat16).reshape(row_count, heads_here, HD)

    def scores_for(row_start):
        query_block = lax.dynamic_slice_in_dim(query_rot, row_start, block_rows, 0)
        ahead_rows = row_start + jnp.arange(block_rows)
        block_docs = lax.dynamic_slice_in_dim(doc_ids, row_start, block_rows, 0)
        allowed = (block_docs[:, None] == doc_ids[None, :]) & (
            ahead_rows[:, None] >= position[None, :]
        )
        scores = (
            jnp.einsum("qhd,khd->hqk", query_block, key_rot, preferred_element_type=jnp.float32)
            * score_scale
        )
        return (query_block, jnp.where(allowed[None], scores, -1e30))

    def attend_block(block_index):
        query_block, scores = scores_for(block_index * block_rows)
        row_max = jnp.max(scores, -1, keepdims=True)
        exp_terms = jnp.exp(scores - row_max)
        row_total = jnp.sum(exp_terms, -1, keepdims=True)
        weights = (exp_terms / row_total).astype(jnp.bfloat16)
        mixed_block = jnp.einsum(
            "hqk,khd->qhd", weights, value_low, preferred_element_type=jnp.float32
        )
        return (mixed_block, (row_max + jnp.log(row_total))[..., 0])

    mixed_out, log_sums = lax.map(attend_block, jnp.arange(block_count))
    mixed_low = mixed_out.reshape(row_count, local_width).astype(jnp.bfloat16)
    attn_part = jnp.dot(mixed_low, w_out, preferred_element_type=jnp.float32)
    attn_total = lax.psum(attn_part.astype(jnp.bfloat16), "tensor").astype(jnp.float32)
    attn_scale = lax.rsqrt(
        jnp.sum(attn_total * attn_total, 1, keepdims=True) / full_width + epsilon
    )
    hidden = whole_x.astype(jnp.float32) + attn_total * attn_scale * gain_attn
    hidden_low = hidden.astype(jnp.bfloat16)
    hidden_cols = lax.dynamic_slice_in_dim(hidden, col_start, narrow, 1)
    gate_proj = jnp.dot(hidden_low, w_gate, preferred_element_type=jnp.float32)
    up_proj = jnp.dot(hidden_low, w_up, preferred_element_type=jnp.float32)
    gate_silu = jax.nn.silu(gate_proj)
    act_low = (gate_silu * up_proj).astype(jnp.bfloat16)
    branch_part = jnp.dot(act_low, w_down, preferred_element_type=jnp.float32)
    branch = lax.psum(branch_part.astype(jnp.bfloat16), "tensor").astype(jnp.float32)
    branch_scale = lax.rsqrt(jnp.sum(branch * branch, 1, keepdims=True) / full_width + epsilon)
    branch_own = lax.dynamic_slice_in_dim(branch, col_start, narrow, 1)
    output = (hidden_cols + branch_own * branch_scale * gain_mlp_cols).astype(jnp.bfloat16)
    dy_full = whole_dy.astype(jnp.float32)
    gained = gain_mlp * dy_full
    row_inner = jnp.sum(gained * branch, 1, keepdims=True)
    branch_low = (
        branch_scale * gained - branch * branch_scale**3 / full_width * row_inner
    ).astype(jnp.bfloat16)
    owner_mask = jnp.arange(full_width) // narrow == tensor_rank
    gain_mlp_part = jnp.where(owner_mask, jnp.sum(dy_full * branch * branch_scale, 0), 0.0)
    down_wgrad = jnp.einsum("tf,td->fd", act_low, branch_low, preferred_element_type=jnp.float32)
    act_grad = jnp.einsum("td,fd->tf", branch_low, w_down, preferred_element_type=jnp.float32)
    sigma = jax.nn.sigmoid(gate_proj)
    gate_low = (act_grad * up_proj * sigma * (1.0 + gate_proj * (1.0 - sigma))).astype(jnp.bfloat16)
    up_low = (act_grad * gate_silu).astype(jnp.bfloat16)
    gate_wgrad = jnp.einsum("td,tf->df", hidden_low, gate_low, preferred_element_type=jnp.float32)
    up_wgrad = jnp.einsum("td,tf->df", hidden_low, up_low, preferred_element_type=jnp.float32)
    hidden_part = jnp.einsum(
        "tf,df->td", gate_low, w_gate, preferred_element_type=jnp.float32
    ) + jnp.einsum("tf,df->td", up_low, w_up, preferred_element_type=jnp.float32)
    hidden_sum, gain_mlp_grad = (
        lax.psum(hidden_part.astype(jnp.bfloat16), "tensor").astype(jnp.float32),
        lax.psum(gain_mlp_part.astype(jnp.bfloat16), "tensor").astype(jnp.float32),
    )
    hidden_grad = dy_full + hidden_sum
    gained_attn = gain_attn * hidden_grad
    attn_inner = jnp.sum(gained_attn * attn_total, 1, keepdims=True)
    attn_low = (
        attn_scale * gained_attn - attn_total * attn_scale**3 / full_width * attn_inner
    ).astype(jnp.bfloat16)
    gain_attn_grad = jnp.sum(hidden_grad * attn_total * attn_scale, 0)
    grad_own = lax.dynamic_slice_in_dim(hidden_grad, col_start, narrow, 1)
    out_wgrad = jnp.einsum("tc,td->cd", mixed_low, attn_low, preferred_element_type=jnp.float32)
    mixed_grad = (
        jnp.einsum("td,cd->tc", attn_low, w_out, preferred_element_type=jnp.float32)
        .astype(jnp.bfloat16)
        .reshape(row_count, heads_here, HD)
    )

    def attend_back(carry, block_index):
        key_acc, value_acc = carry
        row_start = block_index * block_rows
        query_block, scores = scores_for(row_start)
        grad_block = lax.dynamic_slice_in_dim(mixed_grad, row_start, block_rows, 0)
        probs = jnp.exp(scores - log_sums[block_index][..., None])
        probs_low = probs.astype(jnp.bfloat16)
        prob_grad = jnp.einsum(
            "qhd,khd->hqk", grad_block, value_low, preferred_element_type=jnp.float32
        )
        row_dot = jnp.sum(probs * prob_grad, -1, keepdims=True)
        score_low = (probs * (prob_grad - row_dot)).astype(jnp.bfloat16)
        query_part = (
            jnp.einsum("hqk,khd->qhd", score_low, key_rot, preferred_element_type=jnp.float32)
            * score_scale
        )
        key_acc = (
            key_acc
            + jnp.einsum("hqk,qhd->khd", score_low, query_block, preferred_element_type=jnp.float32)
            * score_scale
        )
        value_acc = value_acc + jnp.einsum(
            "hqk,qhd->khd", probs_low, grad_block, preferred_element_type=jnp.float32
        )
        return ((key_acc, value_acc), query_part)

    zero_acc = jnp.zeros((row_count, heads_here, HD), jnp.float32)
    (key_grad, value_grad), query_grad = lax.scan(
        attend_back, (zero_acc, zero_acc), jnp.arange(block_count)
    )
    query_grad = query_grad.reshape(row_count, heads_here, HD)
    query_normed_grad = rotate_back(query_grad, cosine, sine_table).reshape(row_count, local_width)
    key_normed_grad = rotate_back(key_grad, cosine, sine_table).reshape(row_count, local_width)
    gain_query_grad = jnp.sum(query_normed_grad * query_proj * query_scale, 0)
    gain_key_grad = jnp.sum(key_normed_grad * key_proj * key_scale, 0)
    query_gained = gain_query * query_normed_grad
    key_gained = gain_key * key_normed_grad
    query_dot, key_dot = lax.psum(
        (jnp.sum(query_gained * query_proj, 1), jnp.sum(key_gained * key_proj, 1)), "tensor"
    )
    query_low = (
        query_scale * query_gained - query_proj * query_scale**3 / full_width * query_dot[:, None]
    ).astype(jnp.bfloat16)
    key_low = (
        key_scale * key_gained - key_proj * key_scale**3 / full_width * key_dot[:, None]
    ).astype(jnp.bfloat16)
    value_grad_low = value_grad.reshape(row_count, local_width).astype(jnp.bfloat16)
    query_wgrad = jnp.einsum("td,tc->dc", whole_x, query_low, preferred_element_type=jnp.float32)
    key_wgrad = jnp.einsum("td,tc->dc", whole_x, key_low, preferred_element_type=jnp.float32)
    value_wgrad = jnp.einsum(
        "td,tc->dc", whole_x, value_grad_low, preferred_element_type=jnp.float32
    )
    input_part = jnp.einsum("tc,dc->td", query_low, w_query, preferred_element_type=jnp.float32)
    input_part = input_part + jnp.einsum(
        "tc,dc->td", key_low, w_key, preferred_element_type=jnp.float32
    )
    input_part = input_part + jnp.einsum(
        "tc,dc->td", value_grad_low, w_value, preferred_element_type=jnp.float32
    )
    input_grad = (column_sum(input_part) + grad_own).astype(jnp.bfloat16)
    pieces = (
        lax.psum_scatter(
            query_wgrad.astype(jnp.bfloat16), "dp", scatter_dimension=0, tiled=True
        ).astype(jnp.float32),
        lax.psum_scatter(
            key_wgrad.astype(jnp.bfloat16), "dp", scatter_dimension=0, tiled=True
        ).astype(jnp.float32),
        lax.psum_scatter(
            value_wgrad.astype(jnp.bfloat16), "dp", scatter_dimension=0, tiled=True
        ).astype(jnp.float32),
        lax.psum_scatter(
            out_wgrad.astype(jnp.bfloat16), "dp", scatter_dimension=1, tiled=True
        ).astype(jnp.float32),
        lax.psum_scatter(
            gate_wgrad.astype(jnp.bfloat16), "dp", scatter_dimension=0, tiled=True
        ).astype(jnp.float32),
        lax.psum_scatter(
            up_wgrad.astype(jnp.bfloat16), "dp", scatter_dimension=0, tiled=True
        ).astype(jnp.float32),
        lax.psum_scatter(
            down_wgrad.astype(jnp.bfloat16), "dp", scatter_dimension=1, tiled=True
        ).astype(jnp.float32),
        lax.psum_scatter(
            gain_query_grad.astype(jnp.bfloat16), "dp", scatter_dimension=0, tiled=True
        ).astype(jnp.float32),
        lax.psum_scatter(
            gain_key_grad.astype(jnp.bfloat16), "dp", scatter_dimension=0, tiled=True
        ).astype(jnp.float32),
        lax.psum_scatter(
            gain_attn_grad.astype(jnp.bfloat16), "dp", scatter_dimension=0, tiled=True
        ).astype(jnp.float32),
        lax.psum_scatter(
            gain_mlp_grad.astype(jnp.bfloat16), "dp", scatter_dimension=0, tiled=True
        ).astype(jnp.float32),
    )
    summed = (
        lax.all_gather(pieces[0].astype(jnp.bfloat16), "dp", axis=0, tiled=True).astype(
            jnp.float32
        ),
        lax.all_gather(pieces[1].astype(jnp.bfloat16), "dp", axis=0, tiled=True).astype(
            jnp.float32
        ),
        lax.all_gather(pieces[2].astype(jnp.bfloat16), "dp", axis=0, tiled=True).astype(
            jnp.float32
        ),
        lax.all_gather(pieces[3].astype(jnp.bfloat16), "dp", axis=1, tiled=True).astype(
            jnp.float32
        ),
        lax.all_gather(pieces[4].astype(jnp.bfloat16), "dp", axis=0, tiled=True).astype(
            jnp.float32
        ),
        lax.all_gather(pieces[5].astype(jnp.bfloat16), "dp", axis=0, tiled=True).astype(
            jnp.float32
        ),
        lax.all_gather(pieces[6].astype(jnp.bfloat16), "dp", axis=1, tiled=True).astype(
            jnp.float32
        ),
        lax.all_gather(pieces[7].astype(jnp.bfloat16), "dp", axis=0, tiled=True).astype(
            jnp.float32
        ),
        lax.all_gather(pieces[8].astype(jnp.bfloat16), "dp", axis=0, tiled=True).astype(
            jnp.float32
        ),
        lax.all_gather(pieces[9].astype(jnp.bfloat16), "dp", axis=0, tiled=True).astype(
            jnp.float32
        ),
        lax.all_gather(pieces[10].astype(jnp.bfloat16), "dp", axis=0, tiled=True).astype(
            jnp.float32
        ),
    )
    return (
        output,
        input_grad,
        summed[0],
        summed[1],
        summed[2],
        summed[3],
        summed[4],
        summed[5],
        summed[6],
        summed[7],
        summed[8],
        summed[9],
        summed[10],
    )


f32 = jnp.float32
bf16 = jnp.bfloat16

SWAP_Y = [(d, d ^ 1) for d in range(8)]
Z_IN = [(2 * a + y, 2 * b + y) for a, b in ((0, 1), (3, 2)) for y in (0, 1)]
Z_MID = [(2 * a + y, 2 * b + y) for a, b in ((1, 2), (2, 1)) for y in (0, 1)]
Z_OUT = [(2 * a + y, 2 * b + y) for a, b in ((1, 0), (2, 3)) for y in (0, 1)]
SWAP_CORE = [(t, t ^ 1) for t in range(4)]
SWAP_X = [(t, t ^ 2) for t in range(4)]


def over_dp(value, pairs):
    return lax.ppermute(value, "dp", pairs)


def to_core(value):
    return lax.ppermute(value, "tensor", SWAP_CORE)


def to_x(value):
    return lax.ppermute(value, "tensor", SWAP_X)


def low_add(left, right):
    return (left.astype(f32) + right.astype(f32)).astype(bf16)


def dot(left, right, left_axis=1, right_axis=0):
    return lax.dot_general(
        left, right, (((left_axis,), (right_axis,)), ((), ())), preferred_element_type=f32
    )


def part(value, index, size, axis):
    return lax.dynamic_slice_in_dim(value, index * size, size, axis)


def place(target, shape, block, row_block, col_block):
    rows, cols = block.shape
    tile = max(128, min(rows, (1 << 19) // cols))
    steps = rows // tile

    def kernel(where_ref, block_ref, *refs):
        refs[-1][...] = block_ref[...].astype(f32)

    spots = jnp.stack([jnp.int32(row_block) * steps, jnp.int32(col_block)])
    in_specs = [pl.BlockSpec((tile, cols), lambda i, where: (i, 0))]
    operands = [spots, block]
    aliases = {}
    if target is not None:
        in_specs.append(pl.BlockSpec(memory_space=pl.ANY))
        operands.append(target)
        aliases = {2: 0}
    return pl.pallas_call(
        kernel,
        out_shape=jax.ShapeDtypeStruct(shape, f32),
        grid_spec=pltpu.PrefetchScalarGridSpec(
            num_scalar_prefetch=1,
            grid=(steps,),
            in_specs=in_specs,
            out_specs=pl.BlockSpec((tile, cols), lambda i, where: (where[0] + i, where[1])),
        ),
        input_output_aliases=aliases,
        cost_estimate=pl.CostEstimate(
            flops=rows * cols, bytes_accessed=6 * rows * cols, transcendentals=0
        ),
        name="place",
    )(*operands)


def line_sum(own, outer):
    near = low_add(own, over_dp(own, Z_IN))
    total = low_add(near, over_dp(near, Z_MID))
    return jnp.where(outer, over_dp(total, Z_OUT), total)


def sum_middle(own, z_side, outer):
    half = own.shape[0] // 2
    came = over_dp(own, Z_IN)
    send = low_add(part(own, 1 - z_side, half, 0), part(came, 1 - z_side, half, 0))
    keep = low_add(part(own, z_side, half, 0), part(came, z_side, half, 0))
    keep = low_add(keep, over_dp(send, Z_MID))
    keep = low_add(keep, over_dp(keep, SWAP_Y))
    other = over_dp(keep, Z_MID)
    return (
        jnp.where(outer, over_dp(keep, Z_OUT), keep),
        jnp.where(outer, over_dp(other, Z_OUT), other),
    )


def sum_ends(own, z_side, outer):
    half = own.shape[0] // 2
    near = part(own, z_side, half, 0)
    far = part(own, 1 - z_side, half, 0)
    came = over_dp(far, Z_IN)
    came = over_dp(low_add(far, came), Z_MID)
    came = over_dp(low_add(near, came), Z_OUT)
    root = low_add(near, came)
    root = low_add(root, over_dp(root, SWAP_Y))
    first = over_dp(root, Z_IN)
    second = over_dp(first, Z_MID)
    third = over_dp(second, Z_OUT)
    return jnp.where(outer, root, first), jnp.where(outer, third, second)


def gather_columns(own, rank):
    rows, cols = own.shape
    across = to_x(own)
    pieces = (own, to_core(own), across, to_core(across))
    tile = rows // 4

    def kernel(rank_ref, *refs):
        which = pl.program_id(1)
        for k in range(4):
            @pl.when(which == k)
            def _(k=k):
                refs[4][...] = refs[k][...]

    return pl.pallas_call(
        kernel,
        out_shape=jax.ShapeDtypeStruct((rows, 4 * cols), own.dtype),
        grid_spec=pltpu.PrefetchScalarGridSpec(
            num_scalar_prefetch=1,
            grid=(rows // tile, 4),
            in_specs=[pl.BlockSpec((tile, cols), lambda i, k, rank: (i, 0))] * 4,
            out_specs=pl.BlockSpec((tile, cols), lambda i, k, rank: (i, rank[0] ^ k)),
        ),
        cost_estimate=pl.CostEstimate(
            flops=rows * cols, bytes_accessed=16 * rows * cols, transcendentals=0
        ),
        name="gather_columns",
    )(rank[None], *pieces)


def small_sum(value):
    value = value + to_core(value)
    return value + to_x(value)


def fast_body(
    tokens,
    segments,
    cotangent,
    w_query,
    w_key,
    w_value,
    w_out,
    w_gate,
    w_up,
    w_down,
    gain_query,
    gain_key,
    gain_attn,
    gain_mlp,
):
    full_width = w_query.shape[0]
    row_count, narrow = tokens.shape
    local_width = w_query.shape[1]
    units = w_gate.shape[1]
    heads_here = local_width // HD
    rank = lax.axis_index("tensor")
    core = rank % 2
    dp_rank = lax.axis_index("dp")
    y = dp_rank % 2
    z = dp_rank // 2
    z_side = z // 2
    outer = (z == 0) | (z == 3)
    score_scale = HD ** (-0.5)
    chunks = 2
    chunk = row_count // chunks
    half = chunk // 2

    cosine, sine_table = tables(segments)
    cosine = cosine[0][:, None, :]
    sine_table = sine_table[0][:, None, :]
    doc_ids = segments[0]
    position = jnp.arange(row_count)

    whole_x = gather_columns(tokens, rank)
    whole_dy = gather_columns(cotangent, rank)

    query_proj = dot(whole_x, w_query)
    key_proj = dot(whole_x, w_key)
    value_proj = dot(whole_x, w_value)
    squares = small_sum(
        jnp.stack([jnp.sum(query_proj * query_proj, 1), jnp.sum(key_proj * key_proj, 1)])
    )
    query_scale = lax.rsqrt(squares[0] / full_width + epsilon)[:, None]
    key_scale = lax.rsqrt(squares[1] / full_width + epsilon)[:, None]
    query_rot = rotate(
        (query_proj * query_scale * gain_query).reshape(row_count, heads_here, HD),
        cosine,
        sine_table,
    ).astype(bf16)
    key_rot = rotate(
        (key_proj * key_scale * gain_key).reshape(row_count, heads_here, HD), cosine, sine_table
    ).astype(bf16)
    value_low = value_proj.astype(bf16).reshape(row_count, heads_here, HD)

    def scores_for(j):
        last = (j + 1) * chunk
        rows = slice(j * chunk, last)
        allowed = (doc_ids[rows, None] == doc_ids[None, :last]) & (
            position[rows, None] >= position[None, :last]
        )
        scores = (
            jnp.einsum("qhd,khd->hqk", query_rot[rows], key_rot[:last], preferred_element_type=f32)
            * score_scale
        )
        return jnp.where(allowed[None], scores, -1e30)

    def own_rows(value, j):
        return lax.dynamic_slice_in_dim(value, j * chunk + core * half, half, 0)

    def tensor_sum(partial):
        partial = partial.astype(bf16)
        chip = low_add(partial[:half], to_core(partial[half:]))
        return chip.astype(f32) + to_x(chip).astype(f32)

    log_sums, mixed, hid, attn_total, attn_scale, hid_low = [], [], [], [], [], []
    for j in range(chunks):
        scores = scores_for(j)
        row_max = jnp.max(scores, -1, keepdims=True)
        exp_terms = jnp.exp(scores - row_max)
        row_total = jnp.sum(exp_terms, -1, keepdims=True)
        weights = (exp_terms / row_total).astype(bf16)
        mixed_block = jnp.einsum(
            "hqk,khd->qhd", weights, value_low[: (j + 1) * chunk], preferred_element_type=f32
        )
        log_sums.append(row_max + jnp.log(row_total))
        mixed_block = mixed_block.reshape(chunk, local_width).astype(bf16)
        mixed.append(
            jnp.concatenate(
                [part(mixed_block, core, half, 0), part(mixed_block, 1 - core, half, 0)], 0
            )
        )
        total = tensor_sum(dot(mixed[j], w_out))
        scale = lax.rsqrt(jnp.sum(total * total, 1, keepdims=True) / full_width + epsilon)
        hidden = own_rows(whole_x, j).astype(f32) + total * scale * gain_attn
        low = hidden.astype(bf16)
        attn_total.append(total)
        attn_scale.append(scale)
        hid.append(hidden)
        hid_low.append(jnp.concatenate([low, to_core(low)], 0))

    gate, up, act, branch_low, outs = [], [], [], [], []
    gain_mlp_grad = 0.0
    for j in range(chunks):
        gate.append(dot(hid_low[j], w_gate))
        up.append(dot(hid_low[j], w_up))
        act.append((jax.nn.silu(gate[j]) * up[j]).astype(bf16))
        branch = tensor_sum(dot(act[j], w_down))
        scale = lax.rsqrt(jnp.sum(branch * branch, 1, keepdims=True) / full_width + epsilon)
        normed = branch * scale
        outs.append((hid[j] + normed * gain_mlp).astype(bf16))
        dy_rows = own_rows(whole_dy, j).astype(f32)
        gained = gain_mlp * dy_rows
        inner = jnp.sum(gained * branch, 1, keepdims=True)
        low = (scale * gained - branch * scale**3 / full_width * inner).astype(bf16)
        branch_low.append(jnp.concatenate([low, to_core(low)], 0))
        gain_mlp_grad = gain_mlp_grad + jnp.sum(dy_rows * normed, 0)

    def own_columns(blocks, dtype):
        pieces = []
        for block in blocks:
            keep = lax.dynamic_slice_in_dim(block, rank * narrow, narrow, 1)
            give = lax.dynamic_slice_in_dim(block, (rank ^ 1) * narrow, narrow, 1)
            came = to_core(give)
            pieces.append(jnp.where(core == 0, keep, came))
            pieces.append(jnp.where(core == 0, came, keep))
        return jnp.concatenate(pieces, 0)

    output = own_columns(outs, bf16)

    whole_act = jnp.concatenate(act, 0)
    whole_branch_low = jnp.concatenate(branch_low, 0)
    whole_hid = jnp.concatenate(hid_low, 0)

    quarter = units // 4
    down_grad = None
    for k in range(4):
        block = dot(whole_act[:, k * quarter : (k + 1) * quarter], whole_branch_low, 0, 0)
        summed = (sum_middle if k % 2 == 0 else sum_ends)(block.astype(bf16), z_side, outer)
        for which, piece in ((z_side, summed[0]), (1 - z_side, summed[1])):
            down_grad = place(down_grad, (units, full_width), piece, 2 * k + which, 0)

    neighbour_hid = [over_dp(low[:half], SWAP_Y) for low in hid_low]
    neighbour_hid = jnp.concatenate(
        [piece for own in neighbour_hid for piece in (own, to_core(own))], 0
    )
    gate_low, up_low = [], []
    grad_sum = []
    for j in range(chunks):
        act_grad = dot(branch_low[j], w_down, 1, 1)
        sigma = jax.nn.sigmoid(gate[j])
        gate_low.append((act_grad * up[j] * sigma * (1.0 + gate[j] * (1.0 - sigma))).astype(bf16))
        up_low.append((act_grad * (gate[j] * sigma)).astype(bf16))
    whole_gate_low = jnp.concatenate(gate_low, 0)
    whole_up_low = jnp.concatenate(up_low, 0)
    mid = units // 2
    wide = []
    for low in (whole_gate_low, whole_up_low):
        keep = part(low, y, mid, 1)
        came = over_dp(part(low, 1 - y, mid, 1), SWAP_Y)
        grad = (dot(whole_hid, keep, 0, 0) + dot(neighbour_hid, came, 0, 0)).astype(bf16)
        result = None
        for k in range(2):
            rows = full_width // 2
            piece = line_sum(grad[k * rows : (k + 1) * rows], outer)
            result = place(result, (full_width, units), piece, k, y)
            result = place(result, (full_width, units), over_dp(piece, SWAP_Y), k, 1 - y)
        wide.append(result)
    gate_grad, up_grad = wide

    hidden_grad, attn_low = [], []
    gain_attn_grad = 0.0
    for j in range(chunks):
        partial = dot(gate_low[j], w_gate, 1, 1) + dot(up_low[j], w_up, 1, 1)
        grad = own_rows(whole_dy, j).astype(f32) + tensor_sum(partial)
        gained = gain_attn * grad
        inner = jnp.sum(gained * attn_total[j], 1, keepdims=True)
        scale = attn_scale[j]
        low = (scale * gained - attn_total[j] * scale**3 / full_width * inner).astype(bf16)
        gain_attn_grad = gain_attn_grad + jnp.sum(grad * attn_total[j] * scale, 0)
        hidden_grad.append(grad)
        attn_low.append(jnp.concatenate([low, to_core(low)], 0))
    grad_own = own_columns(hidden_grad, f32)
    whole_attn_low = jnp.concatenate(attn_low, 0)
    whole_mixed = jnp.concatenate(mixed, 0)

    def pair_grad(left, right):
        rows = left.shape[1] // 2
        shape = (left.shape[1], right.shape[1])
        came = over_dp(dot(part(left, 1 - y, rows, 1), right, 0, 0).astype(bf16), SWAP_Y)
        own = (dot(part(left, y, rows, 1), right, 0, 0) + came.astype(f32)).astype(bf16)
        piece = line_sum(own, outer)
        result = place(None, shape, piece, y, 0)
        return place(result, shape, over_dp(piece, SWAP_Y), 1 - y, 0)

    out_grad = pair_grad(whole_mixed, whole_attn_low)

    mixed_grad = dot(whole_attn_low, w_out, 1, 1).astype(bf16)
    ordered = []
    for j in range(chunks):
        block = mixed_grad[j * chunk : (j + 1) * chunk]
        ordered.append(part(block, core, half, 0))
        ordered.append(part(block, 1 - core, half, 0))
    mixed_grad = jnp.concatenate(ordered, 0).reshape(row_count, heads_here, HD)

    query_grads = []
    key_grad = jnp.zeros((row_count, heads_here, HD), f32)
    value_grad = jnp.zeros((row_count, heads_here, HD), f32)
    for j in range(chunks):
        last = (j + 1) * chunk
        rows = slice(j * chunk, last)
        scores = scores_for(j)
        grad_block = mixed_grad[rows]
        probs = jnp.exp(scores - log_sums[j])
        prob_grad = jnp.einsum(
            "qhd,khd->hqk", grad_block, value_low[:last], preferred_element_type=f32
        )
        row_dot = jnp.sum(probs * prob_grad, -1, keepdims=True)
        score_low = (probs * (prob_grad - row_dot)).astype(bf16)
        query_grads.append(
            jnp.einsum("hqk,khd->qhd", score_low, key_rot[:last], preferred_element_type=f32)
            * score_scale
        )
        key_part = (
            jnp.einsum("hqk,qhd->khd", score_low, query_rot[rows], preferred_element_type=f32)
            * score_scale
        )
        value_part = jnp.einsum(
            "hqk,qhd->khd", probs.astype(bf16), grad_block, preferred_element_type=f32
        )
        key_grad = key_grad + jnp.pad(key_part, ((0, row_count - last), (0, 0), (0, 0)))
        value_grad = value_grad + jnp.pad(value_part, ((0, row_count - last), (0, 0), (0, 0)))
    query_grad = jnp.concatenate(query_grads, 0)
    query_normed_grad = rotate_back(query_grad, cosine, sine_table).reshape(row_count, local_width)
    key_normed_grad = rotate_back(key_grad, cosine, sine_table).reshape(row_count, local_width)
    gain_query_grad = jnp.sum(query_normed_grad * query_proj * query_scale, 0)
    gain_key_grad = jnp.sum(key_normed_grad * key_proj * key_scale, 0)
    query_gained = gain_query * query_normed_grad
    key_gained = gain_key * key_normed_grad
    dots = small_sum(
        jnp.stack([jnp.sum(query_gained * query_proj, 1), jnp.sum(key_gained * key_proj, 1)])
    )
    query_low = (
        query_scale * query_gained - query_proj * query_scale**3 / full_width * dots[0][:, None]
    ).astype(bf16)
    key_low = (
        key_scale * key_gained - key_proj * key_scale**3 / full_width * dots[1][:, None]
    ).astype(bf16)
    value_grad_low = value_grad.reshape(row_count, local_width).astype(bf16)

    query_wgrad = pair_grad(whole_x, query_low)
    key_wgrad = pair_grad(whole_x, key_low)
    value_wgrad = pair_grad(whole_x, value_grad_low)

    def column_part(which):
        pieces = []
        for x in (0, 1):
            rows = (2 * x + which) * narrow
            total = 0.0
            for low, weight in ((query_low, w_query), (key_low, w_key), (value_grad_low, w_value)):
                total = total + dot(low, lax.dynamic_slice_in_dim(weight, rows, narrow, 0), 1, 1)
            pieces.append(total.astype(bf16))
        return pieces

    give, keep = column_part(1 - core), column_part(core)
    keep = [low_add(k, to_core(g)) for k, g in zip(keep, give)]
    x_here = rank // 2
    away = to_x(jnp.where(x_here == 0, keep[1], keep[0]))
    here = jnp.where(x_here == 0, keep[0], keep[1])
    input_grad = (here.astype(f32) + away.astype(f32) + grad_own).astype(bf16)

    wide_gains = jnp.stack([gain_mlp_grad, gain_attn_grad])
    wide_gains = wide_gains + to_core(wide_gains)
    mine = jnp.arange(full_width) // (full_width // 2) == rank // 2
    wide_gains = jnp.where(mine, wide_gains, 0.0)
    wide_gains = wide_gains + to_x(wide_gains)
    gains = jnp.concatenate([wide_gains.reshape(-1), gain_query_grad, gain_key_grad])
    gains = gains + over_dp(gains, SWAP_Y)
    gains = gains + over_dp(gains, Z_IN)
    gains = gains + over_dp(gains, Z_MID)
    gains = jnp.where(outer, over_dp(gains, Z_OUT), gains)
    return (
        output,
        input_grad,
        query_wgrad,
        key_wgrad,
        value_wgrad,
        out_grad,
        gate_grad,
        up_grad,
        down_grad,
        gains[2 * full_width : 2 * full_width + local_width],
        gains[2 * full_width + local_width :],
        gains[full_width : 2 * full_width],
        gains[:full_width],
    )


def solution(mesh):
    in_specs = (
        P("dp", "tensor"),
        P("dp", None),
        P("dp", "tensor"),
        P(None, "tensor"),
        P(None, "tensor"),
        P(None, "tensor"),
        P("tensor", None),
        P(None, "tensor"),
        P(None, "tensor"),
        P("tensor", None),
        P("tensor"),
        P("tensor"),
        P(),
        P(),
    )
    out_specs = (
        P("dp", "tensor"),
        P("dp", "tensor"),
        P(None, "tensor"),
        P(None, "tensor"),
        P(None, "tensor"),
        P("tensor", None),
        P(None, "tensor"),
        P(None, "tensor"),
        P("tensor", None),
        P("tensor"),
        P("tensor"),
        P(),
        P(),
    )
    body = fast_body if dict(mesh.shape) == {"dp": 8, "tensor": 4} else general_body
    return jax.shard_map(body, mesh=mesh, in_specs=in_specs, out_specs=out_specs, check_vma=False)
```

```python
import math

import jax
import jax.numpy as jnp
from jax import lax
from jax.experimental import pallas as pl
from jax.experimental.pallas import tpu as pltpu
from jax.sharding import PartitionSpec as P


HD = 128


epsilon = 1e-06
rope_base = 500000.0


def tables(segments):
    length = segments.shape[-1]
    places = jnp.broadcast_to(jnp.arange(length, dtype=jnp.int32), segments.shape)
    starts = jnp.concatenate(
        [jnp.ones(segments.shape[:-1] + (1,), dtype=bool), segments[..., 1:] != segments[..., :-1]],
        axis=-1,
    )
    firsts = lax.cummax(jnp.where(starts, places, 0), axis=segments.ndim - 1)
    offsets = (places - firsts).astype(jnp.float32)
    freqs = jnp.power(rope_base, -jnp.arange(0, HD, 2).astype(jnp.float32) / HD)
    angles = offsets[..., None] * freqs
    angles = jnp.concatenate([angles, angles], axis=-1)
    return (jnp.cos(angles), jnp.sin(angles))


def rotate(values, cosine, sine_table):
    half_dim = values.shape[-1] // 2
    turned = jnp.concatenate([-values[..., half_dim:], values[..., :half_dim]], axis=-1)
    return values * cosine + turned * sine_table


def rotate_back(gradient, cosine, sine_table):
    half_dim = gradient.shape[-1] // 2
    scaled = gradient * sine_table
    return gradient * cosine + jnp.concatenate(
        [scaled[..., half_dim:], -scaled[..., :half_dim]], axis=-1
    )


def column_sum(partial_value):
    return lax.psum_scatter(
        partial_value.astype(jnp.bfloat16), "tensor", scatter_dimension=1, tiled=True
    ).astype(jnp.float32)


def general_body(
    tokens,
    segments,
    cotangent,
    w_query,
    w_key,
    w_value,
    w_out,
    w_gate,
    w_up,
    w_down,
    gain_query,
    gain_key,
    gain_attn,
    gain_mlp,
):
    full_width = w_query.shape[0]
    row_count = tokens.shape[0]
    narrow = tokens.shape[1]
    local_width = w_query.shape[1]
    heads_here = local_width // HD
    tensor_rank = lax.axis_index("tensor")
    col_start = tensor_rank * narrow
    block_rows = min(512, row_count)
    block_count = row_count // block_rows
    score_scale = HD ** (-0.5)
    cosine, sine_table = tables(segments)
    cosine = cosine[0][:, None, :]
    sine_table = sine_table[0][:, None, :]
    doc_ids = segments[0]
    position = jnp.arange(row_count)
    gain_mlp_cols = lax.dynamic_slice_in_dim(gain_mlp, col_start, narrow, 0)
    whole_x, whole_dy = (
        lax.all_gather(tokens, "tensor", axis=1, tiled=True),
        lax.all_gather(cotangent, "tensor", axis=1, tiled=True),
    )
    query_proj = jnp.dot(whole_x, w_query, preferred_element_type=jnp.float32)
    key_proj = jnp.dot(whole_x, w_key, preferred_element_type=jnp.float32)
    value_proj = jnp.dot(whole_x, w_value, preferred_element_type=jnp.float32)
    query_sq, key_sq = lax.psum(
        (jnp.sum(query_proj * query_proj, 1), jnp.sum(key_proj * key_proj, 1)), "tensor"
    )
    query_scale = lax.rsqrt(query_sq / full_width + epsilon)[:, None]
    key_scale = lax.rsqrt(key_sq / full_width + epsilon)[:, None]
    query_rot = rotate(
        (query_proj * query_scale * gain_query).reshape(row_count, heads_here, HD),
        cosine,
        sine_table,
    ).astype(jnp.bfloat16)
    key_rot = rotate(
        (key_proj * key_scale * gain_key).reshape(row_count, heads_here, HD), cosine, sine_table
    ).astype(jnp.bfloat16)
    value_low = value_proj.astype(jnp.bfloat16).reshape(row_count, heads_here, HD)

    def scores_for(row_start):
        query_block = lax.dynamic_slice_in_dim(query_rot, row_start, block_rows, 0)
        ahead_rows = row_start + jnp.arange(block_rows)
        block_docs = lax.dynamic_slice_in_dim(doc_ids, row_start, block_rows, 0)
        allowed = (block_docs[:, None] == doc_ids[None, :]) & (
            ahead_rows[:, None] >= position[None, :]
        )
        scores = (
            jnp.einsum("qhd,khd->hqk", query_block, key_rot, preferred_element_type=jnp.float32)
            * score_scale
        )
        return (query_block, jnp.where(allowed[None], scores, -1e30))

    def attend_block(block_index):
        _, scores = scores_for(block_index * block_rows)
        row_max = jnp.max(scores, -1, keepdims=True)
        exp_terms = jnp.exp(scores - row_max)
        row_total = jnp.sum(exp_terms, -1, keepdims=True)
        weights = (exp_terms / row_total).astype(jnp.bfloat16)
        mixed_block = jnp.einsum(
            "hqk,khd->qhd", weights, value_low, preferred_element_type=jnp.float32
        )
        return (mixed_block, (row_max + jnp.log(row_total))[..., 0])

    mixed_out, log_sums = lax.map(attend_block, jnp.arange(block_count))
    mixed_low = mixed_out.reshape(row_count, local_width).astype(jnp.bfloat16)
    attn_part = jnp.dot(mixed_low, w_out, preferred_element_type=jnp.float32)
    attn_total = lax.psum(attn_part.astype(jnp.bfloat16), "tensor").astype(jnp.float32)
    attn_scale = lax.rsqrt(
        jnp.sum(attn_total * attn_total, 1, keepdims=True) / full_width + epsilon
    )
    hidden = whole_x.astype(jnp.float32) + attn_total * attn_scale * gain_attn
    hidden_low = hidden.astype(jnp.bfloat16)
    hidden_cols = lax.dynamic_slice_in_dim(hidden, col_start, narrow, 1)
    gate_proj = jnp.dot(hidden_low, w_gate, preferred_element_type=jnp.float32)
    up_proj = jnp.dot(hidden_low, w_up, preferred_element_type=jnp.float32)
    gate_silu = jax.nn.silu(gate_proj)
    act_low = (gate_silu * up_proj).astype(jnp.bfloat16)
    branch_part = jnp.dot(act_low, w_down, preferred_element_type=jnp.float32)
    branch = lax.psum(branch_part.astype(jnp.bfloat16), "tensor").astype(jnp.float32)
    branch_scale = lax.rsqrt(jnp.sum(branch * branch, 1, keepdims=True) / full_width + epsilon)
    branch_own = lax.dynamic_slice_in_dim(branch, col_start, narrow, 1)
    output = (hidden_cols + branch_own * branch_scale * gain_mlp_cols).astype(jnp.bfloat16)
    dy_full = whole_dy.astype(jnp.float32)
    gained = gain_mlp * dy_full
    row_inner = jnp.sum(gained * branch, 1, keepdims=True)
    branch_low = (
        branch_scale * gained - branch * branch_scale**3 / full_width * row_inner
    ).astype(jnp.bfloat16)
    owner_mask = jnp.arange(full_width) // narrow == tensor_rank
    gain_mlp_part = jnp.where(owner_mask, jnp.sum(dy_full * branch * branch_scale, 0), 0.0)
    down_wgrad = jnp.einsum("tf,td->fd", act_low, branch_low, preferred_element_type=jnp.float32)
    act_grad = jnp.einsum("td,fd->tf", branch_low, w_down, preferred_element_type=jnp.float32)
    sigma = jax.nn.sigmoid(gate_proj)
    gate_low = (act_grad * up_proj * sigma * (1.0 + gate_proj * (1.0 - sigma))).astype(jnp.bfloat16)
    up_low = (act_grad * gate_silu).astype(jnp.bfloat16)
    gate_wgrad = jnp.einsum("td,tf->df", hidden_low, gate_low, preferred_element_type=jnp.float32)
    up_wgrad = jnp.einsum("td,tf->df", hidden_low, up_low, preferred_element_type=jnp.float32)
    hidden_part = jnp.einsum(
        "tf,df->td", gate_low, w_gate, preferred_element_type=jnp.float32
    ) + jnp.einsum("tf,df->td", up_low, w_up, preferred_element_type=jnp.float32)
    hidden_sum, gain_mlp_grad = (
        lax.psum(hidden_part.astype(jnp.bfloat16), "tensor").astype(jnp.float32),
        lax.psum(gain_mlp_part.astype(jnp.bfloat16), "tensor").astype(jnp.float32),
    )
    hidden_grad = dy_full + hidden_sum
    gained_attn = gain_attn * hidden_grad
    attn_inner = jnp.sum(gained_attn * attn_total, 1, keepdims=True)
    attn_low = (
        attn_scale * gained_attn - attn_total * attn_scale**3 / full_width * attn_inner
    ).astype(jnp.bfloat16)
    gain_attn_grad = jnp.sum(hidden_grad * attn_total * attn_scale, 0)
    grad_own = lax.dynamic_slice_in_dim(hidden_grad, col_start, narrow, 1)
    out_wgrad = jnp.einsum("tc,td->cd", mixed_low, attn_low, preferred_element_type=jnp.float32)
    mixed_grad = (
        jnp.einsum("td,cd->tc", attn_low, w_out, preferred_element_type=jnp.float32)
        .astype(jnp.bfloat16)
        .reshape(row_count, heads_here, HD)
    )

    def attend_back(carry, block_index):
        key_acc, value_acc = carry
        row_start = block_index * block_rows
        query_block, scores = scores_for(row_start)
        grad_block = lax.dynamic_slice_in_dim(mixed_grad, row_start, block_rows, 0)
        probs = jnp.exp(scores - log_sums[block_index][..., None])
        probs_low = probs.astype(jnp.bfloat16)
        prob_grad = jnp.einsum(
            "qhd,khd->hqk", grad_block, value_low, preferred_element_type=jnp.float32
        )
        row_dot = jnp.sum(probs * prob_grad, -1, keepdims=True)
        score_low = (probs * (prob_grad - row_dot)).astype(jnp.bfloat16)
        query_part = (
            jnp.einsum("hqk,khd->qhd", score_low, key_rot, preferred_element_type=jnp.float32)
            * score_scale
        )
        key_acc = (
            key_acc
            + jnp.einsum("hqk,qhd->khd", score_low, query_block, preferred_element_type=jnp.float32)
            * score_scale
        )
        value_acc = value_acc + jnp.einsum(
            "hqk,qhd->khd", probs_low, grad_block, preferred_element_type=jnp.float32
        )
        return ((key_acc, value_acc), query_part)

    zero_acc = jnp.zeros((row_count, heads_here, HD), jnp.float32)
    (key_grad, value_grad), query_grad = lax.scan(
        attend_back, (zero_acc, zero_acc), jnp.arange(block_count)
    )
    query_grad = query_grad.reshape(row_count, heads_here, HD)
    query_normed_grad = rotate_back(query_grad, cosine, sine_table).reshape(row_count, local_width)
    key_normed_grad = rotate_back(key_grad, cosine, sine_table).reshape(row_count, local_width)
    gain_query_grad = jnp.sum(query_normed_grad * query_proj * query_scale, 0)
    gain_key_grad = jnp.sum(key_normed_grad * key_proj * key_scale, 0)
    query_gained = gain_query * query_normed_grad
    key_gained = gain_key * key_normed_grad
    query_dot, key_dot = lax.psum(
        (jnp.sum(query_gained * query_proj, 1), jnp.sum(key_gained * key_proj, 1)), "tensor"
    )
    query_low = (
        query_scale * query_gained - query_proj * query_scale**3 / full_width * query_dot[:, None]
    ).astype(jnp.bfloat16)
    key_low = (
        key_scale * key_gained - key_proj * key_scale**3 / full_width * key_dot[:, None]
    ).astype(jnp.bfloat16)
    value_grad_low = value_grad.reshape(row_count, local_width).astype(jnp.bfloat16)
    query_wgrad = jnp.einsum("td,tc->dc", whole_x, query_low, preferred_element_type=jnp.float32)
    key_wgrad = jnp.einsum("td,tc->dc", whole_x, key_low, preferred_element_type=jnp.float32)
    value_wgrad = jnp.einsum(
        "td,tc->dc", whole_x, value_grad_low, preferred_element_type=jnp.float32
    )
    input_part = jnp.einsum("tc,dc->td", query_low, w_query, preferred_element_type=jnp.float32)
    input_part = input_part + jnp.einsum(
        "tc,dc->td", key_low, w_key, preferred_element_type=jnp.float32
    )
    input_part = input_part + jnp.einsum(
        "tc,dc->td", value_grad_low, w_value, preferred_element_type=jnp.float32
    )
    input_grad = (column_sum(input_part) + grad_own).astype(jnp.bfloat16)
    pieces = (
        lax.psum_scatter(
            query_wgrad.astype(jnp.bfloat16), "dp", scatter_dimension=0, tiled=True
        ).astype(jnp.float32),
        lax.psum_scatter(
            key_wgrad.astype(jnp.bfloat16), "dp", scatter_dimension=0, tiled=True
        ).astype(jnp.float32),
        lax.psum_scatter(
            value_wgrad.astype(jnp.bfloat16), "dp", scatter_dimension=0, tiled=True
        ).astype(jnp.float32),
        lax.psum_scatter(
            out_wgrad.astype(jnp.bfloat16), "dp", scatter_dimension=1, tiled=True
        ).astype(jnp.float32),
        lax.psum_scatter(
            gate_wgrad.astype(jnp.bfloat16), "dp", scatter_dimension=0, tiled=True
        ).astype(jnp.float32),
        lax.psum_scatter(
            up_wgrad.astype(jnp.bfloat16), "dp", scatter_dimension=0, tiled=True
        ).astype(jnp.float32),
        lax.psum_scatter(
            down_wgrad.astype(jnp.bfloat16), "dp", scatter_dimension=1, tiled=True
        ).astype(jnp.float32),
        lax.psum_scatter(
            gain_query_grad.astype(jnp.bfloat16), "dp", scatter_dimension=0, tiled=True
        ).astype(jnp.float32),
        lax.psum_scatter(
            gain_key_grad.astype(jnp.bfloat16), "dp", scatter_dimension=0, tiled=True
        ).astype(jnp.float32),
        lax.psum_scatter(
            gain_attn_grad.astype(jnp.bfloat16), "dp", scatter_dimension=0, tiled=True
        ).astype(jnp.float32),
        lax.psum_scatter(
            gain_mlp_grad.astype(jnp.bfloat16), "dp", scatter_dimension=0, tiled=True
        ).astype(jnp.float32),
    )
    summed = (
        lax.all_gather(pieces[0].astype(jnp.bfloat16), "dp", axis=0, tiled=True).astype(
            jnp.float32
        ),
        lax.all_gather(pieces[1].astype(jnp.bfloat16), "dp", axis=0, tiled=True).astype(
            jnp.float32
        ),
        lax.all_gather(pieces[2].astype(jnp.bfloat16), "dp", axis=0, tiled=True).astype(
            jnp.float32
        ),
        lax.all_gather(pieces[3].astype(jnp.bfloat16), "dp", axis=1, tiled=True).astype(
            jnp.float32
        ),
        lax.all_gather(pieces[4].astype(jnp.bfloat16), "dp", axis=0, tiled=True).astype(
            jnp.float32
        ),
        lax.all_gather(pieces[5].astype(jnp.bfloat16), "dp", axis=0, tiled=True).astype(
            jnp.float32
        ),
        lax.all_gather(pieces[6].astype(jnp.bfloat16), "dp", axis=1, tiled=True).astype(
            jnp.float32
        ),
        lax.all_gather(pieces[7].astype(jnp.bfloat16), "dp", axis=0, tiled=True).astype(
            jnp.float32
        ),
        lax.all_gather(pieces[8].astype(jnp.bfloat16), "dp", axis=0, tiled=True).astype(
            jnp.float32
        ),
        lax.all_gather(pieces[9].astype(jnp.bfloat16), "dp", axis=0, tiled=True).astype(
            jnp.float32
        ),
        lax.all_gather(pieces[10].astype(jnp.bfloat16), "dp", axis=0, tiled=True).astype(
            jnp.float32
        ),
    )
    return (
        output,
        input_grad,
        summed[0],
        summed[1],
        summed[2],
        summed[3],
        summed[4],
        summed[5],
        summed[6],
        summed[7],
        summed[8],
        summed[9],
        summed[10],
    )


f32 = jnp.float32
bf16 = jnp.bfloat16

SWAP_Y = [(d, d ^ 1) for d in range(8)]
SWAP_Y_MIDDLE = [(d, d ^ 1) for d in range(2, 6)]
SWAP_Y_END = [(d, d ^ 1) for d in (0, 1, 6, 7)]
Z_IN = [(2 * a + y, 2 * b + y) for a, b in ((0, 1), (3, 2)) for y in (0, 1)]
Z_MID = [(2 * a + y, 2 * b + y) for a, b in ((1, 2), (2, 1)) for y in (0, 1)]
Z_OUT = [(2 * a + y, 2 * b + y) for a, b in ((1, 0), (2, 3)) for y in (0, 1)]
SWAP_CORE = [(t, t ^ 1) for t in range(4)]
SWAP_X = [(t, t ^ 2) for t in range(4)]


def over_dp(value, pairs):
    return lax.ppermute(value, "dp", pairs)


def to_core(value):
    return lax.ppermute(value, "tensor", SWAP_CORE)


def to_x(value):
    return lax.ppermute(value, "tensor", SWAP_X)


def low_add(left, right):
    return (left.astype(f32) + right.astype(f32)).astype(bf16)


def dot(left, right, left_axis=1, right_axis=0):
    return lax.dot_general(
        left, right, (((left_axis,), (right_axis,)), ((), ())), preferred_element_type=f32
    )


def part(value, index, size, axis):
    return lax.dynamic_slice_in_dim(value, index * size, size, axis)


def place_one(target, shape, use_first, first, second, row_block, col_block):
    rows, cols = second.shape
    steps = 4
    tile = rows // steps

    def kernel(spot_ref, first_ref, second_ref, *refs):
        @pl.when(spot_ref[2] == 1)
        def _():
            refs[-1][...] = first_ref[...].astype(f32)

        @pl.when(spot_ref[2] != 1)
        def _():
            refs[-1][...] = second_ref[...].astype(f32)

    spots = jnp.stack(
        [jnp.int32(row_block) * steps, jnp.int32(col_block), use_first.astype(jnp.int32)]
    )
    in_specs = [
        pl.BlockSpec((tile, cols), lambda i, spot: (i * spot[2], 0)),
        pl.BlockSpec((tile, cols), lambda i, spot: (i * (1 - spot[2]), 0)),
    ]
    operands = [spots, first, second]
    aliases = {}
    if target is not None:
        in_specs.append(pl.BlockSpec(memory_space=pl.ANY))
        operands.append(target)
        aliases = {3: 0}
    return pl.pallas_call(
        kernel,
        out_shape=jax.ShapeDtypeStruct(shape, f32),
        grid_spec=pltpu.PrefetchScalarGridSpec(
            num_scalar_prefetch=1,
            grid=(steps,),
            in_specs=in_specs,
            out_specs=pl.BlockSpec((tile, cols), lambda i, spot: (spot[0] + i, spot[1])),
        ),
        input_output_aliases=aliases,
        compiler_params=pltpu.CompilerParams(vmem_limit_bytes=16 << 20),
        cost_estimate=pl.CostEstimate(
            flops=rows * cols, bytes_accessed=6 * rows * cols, transcendentals=0
        ),
        name="place",
    )(*operands)


def place(target, shape, block, row_block, col_block):
    rows, cols = block.shape
    steps = 4
    tile = rows // steps

    def kernel(spot_ref, block_ref, target_ref, out_ref):
        out_ref[...] = block_ref[...].astype(f32)

    spots = jnp.stack([jnp.int32(row_block) * steps, jnp.int32(col_block)])
    return pl.pallas_call(
        kernel,
        out_shape=jax.ShapeDtypeStruct(shape, f32),
        grid_spec=pltpu.PrefetchScalarGridSpec(
            num_scalar_prefetch=1,
            grid=(steps,),
            in_specs=[
                pl.BlockSpec((tile, cols), lambda i, spot: (i, 0)),
                pl.BlockSpec(memory_space=pl.ANY),
            ],
            out_specs=pl.BlockSpec((tile, cols), lambda i, spot: (spot[0] + i, spot[1])),
        ),
        input_output_aliases={2: 0},
        compiler_params=pltpu.CompilerParams(vmem_limit_bytes=16 << 20),
        cost_estimate=pl.CostEstimate(
            flops=rows * cols, bytes_accessed=6 * rows * cols, transcendentals=0
        ),
        name="place",
    )(spots, block, target)


def matmul_call(kernel, steps, ins, outs, scratch=(), flops=0, mib=24):
    moved = sum(a.size * a.dtype.itemsize for a, _, _ in ins)
    moved += sum(math.prod(s) * jnp.dtype(d).itemsize for s, d, _, _ in outs)
    return pl.pallas_call(
        kernel,
        out_shape=[jax.ShapeDtypeStruct(s, d) for s, d, _, _ in outs],
        grid=(steps,),
        in_specs=[pl.BlockSpec(b, m) for _, b, m in ins],
        out_specs=[pl.BlockSpec(b, m) for _, _, b, m in outs],
        scratch_shapes=list(scratch),
        compiler_params=pltpu.CompilerParams(vmem_limit_bytes=mib << 20),
        cost_estimate=pl.CostEstimate(flops=flops, bytes_accessed=moved, transcendentals=0),
    )(*[a for a, _, _ in ins])


def feed(low, w_gate, w_up):
    rows, width = low.shape
    units = w_gate.shape[1]
    tile = min(512, units)

    def kernel(low_ref, gate_w, up_w, gate_ref, up_ref, act_ref):
        gate = dot(low_ref[...], gate_w[...])
        up = dot(low_ref[...], up_w[...])
        gate_ref[...] = gate.astype(bf16)
        up_ref[...] = up.astype(bf16)
        act_ref[...] = (gate * jax.nn.sigmoid(gate) * up).astype(bf16)

    column = lambda n: (0, n)
    return matmul_call(
        kernel,
        units // tile,
        [
            (low, (rows, width), lambda n: (0, 0)),
            (w_gate, (width, tile), column),
            (w_up, (width, tile), column),
        ],
        [((rows, units), bf16, (rows, tile), column)] * 3,
        flops=4 * rows * width * units,
        mib=56,
    )


def unfeed(low, w_down, gate, up):
    rows, width = low.shape
    units = w_down.shape[0]
    tile = min(512, units)

    def kernel(low_ref, down_w, gate_ref, up_ref, dgate_ref, dup_ref):
        grad = dot(low_ref[...], down_w[...], 1, 1)
        gate = gate_ref[...].astype(f32)
        sigma = jax.nn.sigmoid(gate)
        dup_ref[...] = (grad * (gate * sigma)).astype(bf16)
        dgate_ref[...] = (
            grad * up_ref[...].astype(f32) * sigma * (1.0 + gate * (1.0 - sigma))
        ).astype(bf16)

    column = lambda n: (0, n)
    return matmul_call(
        kernel,
        units // tile,
        [
            (low, (rows, width), lambda n: (0, 0)),
            (w_down, (tile, width), lambda n: (n, 0)),
            (gate, (rows, tile), column),
            (up, (rows, tile), column),
        ],
        [((rows, units), bf16, (rows, tile), column)] * 2,
        flops=2 * rows * width * units,
        mib=56,
    )


def unwide(dgate, dup, w_gate, w_up):
    rows, units = dgate.shape
    width = w_gate.shape[0]
    tile = min(512, width)

    def kernel(dgate_ref, dup_ref, gate_w, up_w, upper_ref, lower_ref):
        total = dot(dgate_ref[...], gate_w[...], 1, 1) + dot(dup_ref[...], up_w[...], 1, 1)
        upper_ref[...] = total[: rows // 2].astype(bf16)
        lower_ref[...] = total[rows // 2 :].astype(bf16)

    whole = lambda n: (0, 0)
    row = lambda n: (n, 0)
    column = lambda n: (0, n)
    return matmul_call(
        kernel,
        width // tile,
        [
            (dgate, (rows, units), whole),
            (dup, (rows, units), whole),
            (w_gate, (tile, units), row),
            (w_up, (tile, units), row),
        ],
        [((rows // 2, width), bf16, (rows // 2, tile), column)] * 2,
        flops=4 * rows * width * units,
        mib=56,
    )


def half_turned(values):
    lanes = lax.broadcasted_iota(jnp.int32, values.shape, 1)
    rolled = pltpu.roll(values, HD // 2, 1)
    return jnp.where(lanes < HD // 2, -rolled, rolled)


def as_column(row):
    return jnp.broadcast_to(row, (HD, row.shape[1])).T


def as_row(values):
    return jnp.sum(values.T, 0, keepdims=True)


def project(x, w_query, w_key, w_value):
    rows, width = x.shape
    cols = w_query.shape[1]
    tile = rows // 4

    def kernel(x_ref, q_w, k_w, v_w, q_ref, k_ref, v_ref, sum_ref):
        for which, (weight, result) in enumerate(((q_w, q_ref), (k_w, k_ref))):
            value = dot(x_ref[...], weight[...])
            result[...] = value
            square = value * value
            total = square[:, :HD]
            for start in range(HD, cols, HD):
                total = total + square[:, start : start + HD]
            sum_ref[which : which + 1] = as_row(total)
        v_ref[...] = dot(x_ref[...], v_w[...]).astype(bf16)

    row = lambda i: (i, 0)
    whole = lambda i: (0, 0)
    return matmul_call(
        kernel,
        rows // tile,
        [
            (x, (tile, width), row),
            (w_query, (width, cols), whole),
            (w_key, (width, cols), whole),
            (w_value, (width, cols), whole),
        ],
        [
            ((rows, cols), f32, (tile, cols), row),
            ((rows, cols), f32, (tile, cols), row),
            ((rows, cols), bf16, (tile, cols), row),
            ((2, rows), f32, (2, tile), lambda i: (0, i)),
        ],
        flops=6 * rows * width * cols,
    )


def turn_heads(query, key, squares, full_width, gain_query, gain_key, cosine, sine):
    rows, width = query.shape

    def kernel(q_ref, k_ref, sum_ref, gq_ref, gk_ref, cos_ref, sin_ref, qr_ref, kr_ref):
        scales = lax.rsqrt(sum_ref[...] / full_width + epsilon)
        for value, col, gain, result in ((q_ref, 0, gq_ref, qr_ref), (k_ref, 1, gk_ref, kr_ref)):
            normed = value[...] * as_column(scales[col : col + 1]) * gain[...]
            result[...] = (normed * cos_ref[...] + half_turned(normed) * sin_ref[...]).astype(bf16)

    head = lambda h: (0, h)
    whole = lambda h: (0, 0)
    return matmul_call(
        kernel,
        width // HD,
        [
            (query, (rows, HD), head),
            (key, (rows, HD), head),
            (squares, (2, rows), whole),
            (gain_query[None], (1, HD), head),
            (gain_key[None], (1, HD), head),
            (cosine, (rows, HD), whole),
            (sine, (rows, HD), whole),
        ],
        [((rows, width), bf16, (rows, HD), head)] * 2,
        flops=10 * rows * width,
    )


BLOCK = 256


def key_span(block):
    first = max(0, block - 512 // BLOCK) * BLOCK
    return first, (block + 1) * BLOCK


def attend_heads(query, key, value, docs, blocks):
    width = query.shape[1]
    rows = len(blocks) * BLOCK
    last = blocks[-1] * BLOCK + BLOCK

    def kernel(q_ref, k_ref, v_ref, doc_ref, out_ref):
        for n, block in enumerate(blocks):
            begin, end = key_span(block)
            span = end - begin
            mine = slice(n * BLOCK, (n + 1) * BLOCK)
            own = slice(block * BLOCK, (block + 1) * BLOCK)
            scores = dot(q_ref[mine], k_ref[begin:end], 1, 1) * HD ** (-0.5)
            at_row = block * BLOCK + lax.broadcasted_iota(jnp.int32, (BLOCK, span), 0)
            at_col = begin + lax.broadcasted_iota(jnp.int32, (BLOCK, span), 1)
            doc = jnp.concatenate([as_column(doc_ref[:, own])] * (span // HD), 1)
            allowed = (doc == doc_ref[:, begin:end]) & (at_row >= at_col)
            scores = jnp.where(allowed, scores, -1e30)
            terms = jnp.exp(scores - jnp.max(scores, 1, keepdims=True))
            weights = (terms * (1.0 / jnp.sum(terms, 1, keepdims=True))).astype(bf16)
            out_ref[mine] = dot(weights, v_ref[begin:end]).astype(bf16)

    head = lambda h: (0, h)
    return matmul_call(
        kernel,
        width // HD,
        [
            (query, (rows, HD), lambda h: (blocks[0] // len(blocks), h)),
            (key, (last, HD), head),
            (value, (last, HD), head),
            (docs, docs.shape, lambda h: (0, 0)),
        ],
        [((rows, width), bf16, (rows, HD), head)],
        flops=4 * rows * last * width,
        mib=16,
    )[0]


def unattend_heads(query, key, value, grad, docs, q_proj, k_proj, squares, full_width, gain_query, gain_key, cosine, sine):
    rows, width = query.shape

    def kernel(
        q_ref, k_ref, v_ref, do_ref, doc_ref, qp_ref, kp_ref, sum_ref, gq_ref, gk_ref, cos_ref, sin_ref,
        dq_ref, dk_ref, dv_ref, dots_ref, gain_ref, q_acc, k_acc, v_acc,
    ):
        k_acc[...] = jnp.zeros_like(k_acc)
        v_acc[...] = jnp.zeros_like(v_acc)
        for block in range(rows // BLOCK):
            begin, end = key_span(block)
            span = end - begin
            mine = slice(block * BLOCK, (block + 1) * BLOCK)
            keys = k_ref[begin:end]
            do = do_ref[mine]
            scores = dot(keys, q_ref[mine], 1, 1) * HD ** (-0.5)
            at_key = begin + lax.broadcasted_iota(jnp.int32, (span, BLOCK), 0)
            at_query = block * BLOCK + lax.broadcasted_iota(jnp.int32, (span, BLOCK), 1)
            doc = jnp.concatenate([as_column(doc_ref[:, begin:end])] * (BLOCK // HD), 1)
            allowed = (doc == doc_ref[:, mine]) & (at_query >= at_key)
            scores = jnp.where(allowed, scores, -1e30)
            terms = jnp.exp(scores - jnp.max(scores, 0, keepdims=True))
            probs = terms * (1.0 / jnp.sum(terms, 0, keepdims=True))
            prob_grad = dot(v_ref[begin:end], do, 1, 1)
            inner = jnp.sum(probs * prob_grad, 0, keepdims=True)
            low = (probs * (prob_grad - inner)).astype(bf16)
            q_acc[mine] = dot(low, keys, 0, 0)
            k_acc[begin:end] += dot(low, q_ref[mine])
            v_acc[begin:end] += dot(probs.astype(bf16), do)
        dv_ref[...] = v_acc[...].astype(bf16)
        scales = lax.rsqrt(sum_ref[...] / full_width + epsilon)
        for which, (acc, proj, gain, result) in enumerate(
            ((q_acc, qp_ref, gq_ref, dq_ref), (k_acc, kp_ref, gk_ref, dk_ref))
        ):
            turned = acc[...] * HD ** (-0.5)
            normed = turned * cos_ref[...] - half_turned(turned * sin_ref[...])
            gained = normed * gain[...]
            result[...] = gained
            projected = proj[...]
            gain_ref[which : which + 1] = jnp.sum(
                normed * projected * as_column(scales[which : which + 1]), 0, keepdims=True
            )
            inner = as_row(gained * projected)

            @pl.when(pl.program_id(0) == 0)
            def _():
                dots_ref[which : which + 1] = inner

            @pl.when(pl.program_id(0) > 0)
            def _():
                dots_ref[which : which + 1] += inner

    head = lambda h: (0, h)
    whole = lambda h: (0, 0)
    column = (rows, HD)
    return matmul_call(
        kernel,
        width // HD,
        [
            (query, column, head),
            (key, column, head),
            (value, column, head),
            (grad, column, head),
            (docs, (1, rows), whole),
            (q_proj, column, head),
            (k_proj, column, head),
            (squares, (2, rows), whole),
            (gain_query[None], (1, HD), head),
            (gain_key[None], (1, HD), head),
            (cosine, column, whole),
            (sine, column, whole),
        ],
        [
            ((rows, width), f32, column, head),
            ((rows, width), f32, column, head),
            ((rows, width), bf16, column, head),
            ((2, rows), f32, (2, rows), whole),
            ((2, width), f32, (2, HD), head),
        ],
        scratch=[pltpu.VMEM((rows, HD), f32)] * 3,
        flops=10 * rows * rows * width,
        mib=56,
    )


def unscale(gained, projected, squares, dots, which, full_width):
    rows, cols = gained.shape
    tile = rows // 2

    def kernel(gained_ref, proj_ref, sum_ref, dot_ref, out_ref):
        scale = lax.rsqrt(sum_ref[which : which + 1] / full_width + epsilon)
        inner = scale**3 / full_width * dot_ref[which : which + 1]
        scale, inner = as_column(scale), as_column(inner)
        for start in range(0, cols, HD):
            lanes = slice(start, start + HD)
            out_ref[:, lanes] = (
                scale * gained_ref[:, lanes] - proj_ref[:, lanes] * inner
            ).astype(bf16)

    row = lambda i: (i, 0)
    column = lambda i: (0, i)
    return matmul_call(
        kernel,
        rows // tile,
        [
            (gained, (tile, cols), row),
            (projected, (tile, cols), row),
            (squares, (2, tile), column),
            (dots, (2, tile), column),
        ],
        [((rows, cols), bf16, (tile, cols), row)],
    )[0]


def fast_add(left, right):
    rows, cols = left.shape
    tile = rows // 2

    def kernel(left_ref, right_ref, out_ref):
        out_ref[...] = (left_ref[...].astype(f32) + right_ref[...].astype(f32)).astype(bf16)

    row = lambda i: (i, 0)
    return matmul_call(
        kernel,
        rows // tile,
        [(left, (tile, cols), row), (right, (tile, cols), row)],
        [((rows, cols), bf16, (tile, cols), row)],
        mib=12,
    )[0]


def pick_and_place(target, shape, use_first, first, second, row_block, col_block):
    rows, cols = first.shape
    tile = rows // 4
    steps = 4

    def kernel(spot_ref, first_ref, second_ref, *refs):
        low_ref, wide_ref = refs[-2:]

        @pl.when(spot_ref[2] == 1)
        def _():
            low_ref[...] = first_ref[...]
            wide_ref[...] = first_ref[...].astype(f32)

        @pl.when(spot_ref[2] != 1)
        def _():
            low_ref[...] = second_ref[...]
            wide_ref[...] = second_ref[...].astype(f32)

    spots = jnp.stack(
        [jnp.int32(row_block) * steps, jnp.int32(col_block), use_first.astype(jnp.int32)]
    )
    in_specs = [
        pl.BlockSpec((tile, cols), lambda i, spot: (i * spot[2], 0)),
        pl.BlockSpec((tile, cols), lambda i, spot: (i * (1 - spot[2]), 0)),
    ]
    operands = [spots, first, second]
    aliases = {}
    if target is not None:
        in_specs.append(pl.BlockSpec(memory_space=pl.ANY))
        operands.append(target)
        aliases = {3: 1}
    return pl.pallas_call(
        kernel,
        out_shape=[jax.ShapeDtypeStruct(first.shape, bf16), jax.ShapeDtypeStruct(shape, f32)],
        grid_spec=pltpu.PrefetchScalarGridSpec(
            num_scalar_prefetch=1,
            grid=(steps,),
            in_specs=in_specs,
            out_specs=[
                pl.BlockSpec((tile, cols), lambda i, spot: (i, 0)),
                pl.BlockSpec((tile, cols), lambda i, spot: (spot[0] + i, spot[1])),
            ],
        ),
        input_output_aliases=aliases,
        cost_estimate=pl.CostEstimate(
            flops=rows * cols, bytes_accessed=8 * rows * cols, transcendentals=0
        ),
        name="pick_and_place",
    )(*operands)


ORDER = [
    -3, -2, 1, -4, 6, -8, -7, 5, 11, -12, 206, -207, 13, -14, -9, 15, 16, 17, 18, -19,
    10, 20, -21, 25, 26, -27, 194, -208, 28, -29, 209, 22, -23, -117, 24, 33, 34, -35, -119, 30,
    -31, -118, 36, -37, 32, 41, 42, -43, -120, 54, 38, -39, 44, -45, 121, 40, 114, 166, -167, 46,
    -47, 116, 48, 55, 72, -73, 115, 144, -145, 56, 57, -58, 85, 86, 122, -123, 173, -87, -174, 74,
    -76, 75, 146, -147, 59, -60, 124, 77, -78, 155, -125, -156, 175, -176, 88, -89, 90, 133, 61, 62,
    -63, -134, 168, -169, 79, -80, -81, 51, -52, 177, -178, 91, -92, 157, -158, 148, -149, 179, -82, 170,
    -171, 180, -181, 64, -65, 135, -136, 126, -127, 93, -94, 172, 185, 150, -151, 195, -196, 186, 187, -188,
    159, -160, 210, -211, 128, -129, 152, -153, 189, -190, 197, -198, 95, -96, 137, -138, 191, 193, 232, -233,
    192, 161, -162, 199, -200, 130, -131, 154, 66, -67, 212, -213, 101, 234, -97, 139, -140, -235, 49, -50,
    163, -164, 243, -68, -102, -245, -246, 201, -202, 132, 214, -215, 53, 221, -222, 182, -98, -183, 236, 141,
    184, -237, 244, -69, -142, 165, 203, -204, 223, -224, 216, -217, 103, -105, 104, 247, -248, 250, -251, 70,
    238, 252, -253, -239, 225, -226, 71, 83, 84, 99, 100, 106, -107, 254, 218, -219, 143, 205, 227, -228,
    249, 240, -241, 108, -109, -110, 229, -255, 220, -111, 112, -230, 242, 256, -257, 258, -259, 260, -261, 113,
    262, 231,
]


class Handle:
    def __init__(self, task, index=None):
        self.task, self.index = task, index


class Task:
    def __init__(self, function, inputs, link):
        self.function, self.inputs, self.link, self.values = function, inputs, link, None
        self.handle = Handle(self, 0)


class Plan:
    window = 2

    def __init__(self):
        self.tasks = []

    def add(self, function, inputs, link):
        task = Task(function, inputs, link)
        self.tasks.append(task)
        return task

    def step(self, cost, function, *inputs, outs=1):
        task = self.add(function, inputs, ())
        if outs == 1:
            return task.handle
        return (task.handle, *[Handle(task, k) for k in range(1, outs)])

    def move(self, link, function, value):
        links = {"y": ("y_middle", "y_end")}.get(link, (link,))
        return self.add(function, (value,), links).handle

    def run(self):
        last, sent = None, {}

        def fence(task, extra):
            handles = list(task.inputs) + [h for h in extra if h not in task.inputs]
            values = [h.task.values[h.index] if isinstance(h, Handle) else h for h in handles]
            if extra:
                values = lax.optimization_barrier(tuple(values))
                for handle, fresh in zip(handles, values):
                    if isinstance(handle, Handle):
                        handle.task.values[handle.index] = fresh
            return values[: len(task.inputs)]

        for number in ORDER:
            task = self.tasks[abs(number) - 1]
            extra = [last] if last is not None else []
            for link in task.link:
                earlier = sent.setdefault(link, [])
                if len(earlier) >= self.window and earlier[-self.window] not in extra:
                    extra.append(earlier[-self.window])
                earlier.append(task.handle)
            fenced = fence(task, extra)
            result = task.function(*fenced)
            task.values = list(result) if isinstance(result, (tuple, list)) else [result]
            if number > 0:
                last = task.handle


def in_order(rank, *pieces):
    rows, cols = pieces[0].shape
    tile = rows // 4

    def kernel(rank_ref, *refs):
        for k in range(4):
            start = pl.multiple_of((rank_ref[0] ^ k) * cols, cols)
            refs[4][:, pl.ds(start, cols)] = refs[k][...]

    return pl.pallas_call(
        kernel,
        out_shape=jax.ShapeDtypeStruct((rows, 4 * cols), pieces[0].dtype),
        grid_spec=pltpu.PrefetchScalarGridSpec(
            num_scalar_prefetch=1,
            grid=(rows // tile,),
            in_specs=[pl.BlockSpec((tile, cols), lambda i, rank: (i, 0))] * 4,
            out_specs=pl.BlockSpec((tile, 4 * cols), lambda i, rank: (i, 0)),
        ),
        cost_estimate=pl.CostEstimate(
            flops=rows * cols, bytes_accessed=16 * rows * cols, transcendentals=0
        ),
        name="in_order",
    )(rank[None], *pieces)


def fast_body(
    tokens,
    segments,
    cotangent,
    w_query,
    w_key,
    w_value,
    w_out,
    w_gate,
    w_up,
    w_down,
    gain_query,
    gain_key,
    gain_attn,
    gain_mlp,
):
    full_width = w_query.shape[0]
    row_count, narrow = tokens.shape
    local_width = w_query.shape[1]
    units = w_gate.shape[1]
    rank = lax.axis_index("tensor")
    core = rank % 2
    dp_rank = lax.axis_index("dp")
    y = dp_rank % 2
    z = dp_rank // 2
    z_side = z // 2
    outer = (z == 0) | (z == 3)
    chunks = 2
    chunk = row_count // chunks
    half = chunk // 2

    plan = Plan()
    step = plan.step

    def core_move(value):
        return plan.move("core", to_core, value)

    def x_move(value):
        return plan.move("x", to_x, value)

    def y_move(value):
        return plan.move("y", lambda v: over_dp(v, SWAP_Y), value)

    def y_move_at(where, value):
        pairs = {"middle": SWAP_Y_MIDDLE, "end": SWAP_Y_END}[where]
        return plan.move("y_" + where, lambda v: over_dp(v, pairs), value)

    def z_move(which, value):
        pairs = {"in": Z_IN, "mid": Z_MID, "out": Z_OUT}[which]
        return plan.move(which, lambda v: over_dp(v, pairs), value)

    def gathered(value):
        across = x_move(value)
        pieces = (value, core_move(value), across, core_move(across))
        return across, step(5.0, lambda *p: in_order(rank, *p), *pieces)

    def prepare(value):
        cosine, sine = tables(segments)
        return value, cosine[0], sine[0]

    _, cosine, sine = step(6.0, prepare, tokens, outs=3)
    across, whole_x = gathered(tokens)
    held_dy = step(0.0, lambda v, _: v, cotangent, across)
    _, whole_dy = gathered(held_dy)

    def small_sum(value):
        value = step(0.6, lambda a, b: a + b, value, core_move(value))
        return step(0.6, lambda a, b: a + b, value, x_move(value))

    query_proj, key_proj, value_low, squares = step(
        11.0, lambda x: project(x, w_query, w_key, w_value), whole_x, outs=4
    )
    squares = small_sum(squares)

    query_rot, key_rot = step(
        6.0,
        lambda q, k, s, cos, sin: turn_heads(q, k, s, full_width, gain_query, gain_key, cos, sin),
        query_proj,
        key_proj,
        squares,
        cosine,
        sine,
        outs=2,
    )

    def attend(query, key, value, j):
        per = chunk // BLOCK
        blocks = list(range(j * per, (j + 1) * per))
        block = attend_heads(query, key, value, segments, blocks)
        return jnp.concatenate([part(block, core, half, 0), part(block, 1 - core, half, 0)], 0)

    def own_rows(value, j):
        return lax.dynamic_slice_in_dim(value, j * chunk + core * half, half, 0)

    def halves(value):
        value = value.astype(bf16)
        return value[:half], value[half:]

    def chip_sum(keep, give):
        chip = step(1.8, fast_add, keep, core_move(give))
        return chip, x_move(chip)

    def both(value):
        return step(2.0, lambda a, b: jnp.concatenate([a, b], 0), value, core_move(value))

    mixed, attn_total, attn_scale, hid, own_low, hid_low = [], [], [], [], [], []
    for j in range(chunks):
        block = step(
            8.0 + j,
            lambda q, k, v, j=j: attend(q, k, v, j),
            query_rot,
            key_rot,
            value_low,
        )
        mixed.append(block)
        keep, give = step(3.0, lambda m: halves(dot(m, w_out)), block, outs=2)
        chip, away = chip_sum(keep, give)

        def join(chip, away, x, j=j):
            total = chip.astype(f32) + away.astype(f32)
            scale = lax.rsqrt(jnp.sum(total * total, 1, keepdims=True) / full_width + epsilon)
            hidden = own_rows(x, j).astype(f32) + total * scale * gain_attn
            return total, scale, hidden, hidden.astype(bf16)

        total, scale, hidden, low = step(5.0, join, chip, away, whole_x, outs=4)
        attn_total.append(total)
        attn_scale.append(scale)
        hid.append(hidden)
        own_low.append(low)
        hid_low.append(both(low))

    gate, up, act, out_rows, branch_low, mlp_gains = [], [], [], [], [], []
    for j in range(chunks):
        g, u, a = step(14.5, lambda low: feed(low, w_gate, w_up), hid_low[j], outs=3)
        gate.append(g)
        up.append(u)
        act.append(a)
        keep, give = step(5.0, lambda a: halves(dot(a, w_down)), a, outs=2)
        chip, away = chip_sum(keep, give)

        def finish(chip, away, hidden, dy, j=j):
            branch = chip.astype(f32) + away.astype(f32)
            scale = lax.rsqrt(jnp.sum(branch * branch, 1, keepdims=True) / full_width + epsilon)
            normed = branch * scale
            dy_rows = own_rows(dy, j).astype(f32)
            gained = gain_mlp * dy_rows
            inner = jnp.sum(gained * branch, 1, keepdims=True)
            low = (scale * gained - branch * scale**3 / full_width * inner).astype(bf16)
            return low, (hidden + normed * gain_mlp).astype(bf16), jnp.sum(dy_rows * normed, 0)

        low, rows, gains = step(8.0, finish, chip, away, hid[j], whole_dy, outs=3)
        branch_low.append(both(low))
        out_rows.append(rows)
        mlp_gains.append(gains)

    def own_columns(blocks):
        keeps, comes = [], []
        for block in blocks:
            keep, give = step(
                1.5,
                lambda b: (
                    lax.dynamic_slice_in_dim(b, rank * narrow, narrow, 1),
                    lax.dynamic_slice_in_dim(b, (rank ^ 1) * narrow, narrow, 1),
                ),
                block,
                outs=2,
            )
            keeps.append(keep)
            comes.append(core_move(give))

        def merge(*values):
            pieces = []
            for keep, came in zip(values[:chunks], values[chunks:]):
                pieces += [jnp.where(core == 0, keep, came), jnp.where(core == 0, came, keep)]
            return jnp.concatenate(pieces, 0)

        return step(2.0, merge, *keeps, *comes)

    output = own_columns(out_rows)

    def joined(*values):
        return jnp.concatenate(values, 0)

    def chosen(which):
        return lambda own, came: low_add(
            part(own, which, own.shape[0] // 2, 0), part(came, which, came.shape[0] // 2, 0)
        )

    def half_of(which):
        return lambda own: part(own, which, own.shape[0] // 2, 0)

    def line_sum(own, mib):
        near = step(0.6 + 1.6 * mib, fast_add, own, z_move("in", own))
        total = step(0.6 + 1.6 * mib, fast_add, near, z_move("mid", near))
        return z_move("out", total), total

    def put(target, shape, spots, first, second, mib):
        if target is None:
            run = lambda a, b: pick_and_place(None, shape, outer, a, b, *spots)
            return step(1.0 + 2.2 * mib, run, first, second, outs=2)
        run = lambda a, b, t: pick_and_place(t, shape, outer, a, b, *spots)
        return step(1.0 + 2.2 * mib, run, first, second, target, outs=2)

    def set_down(target, shape, spots, value, mib):
        run = lambda v, t: place(t, shape, v, *spots)
        return step(0.8 + 1.7 * mib, run, value, target)

    def put_only(target, shape, spots, first, second, mib):
        run = lambda a, b, *t: place_one(*(t or (None,)), shape, outer, a, b, *spots)
        rest = () if target is None else (target,)
        return step(0.8 + 1.7 * mib, run, first, second, *rest)

    def sum_middle(own, mib):
        came = z_move("in", own)
        send = step(0.8 * mib, chosen(1 - z_side), own, came)
        keep = step(0.8 * mib, chosen(z_side), own, came)
        keep = step(0.8 * mib, fast_add, keep, z_move("mid", send))
        keep = step(0.8 * mib, fast_add, keep, y_move_at("middle", keep))
        other = z_move("mid", keep)
        return (z_move("out", keep), keep), (z_move("out", other), other)

    def sum_ends(own, mib):
        far = step(0.5 * mib, half_of(1 - z_side), own)
        came = z_move("in", far)
        came = z_move("mid", step(0.8 * mib, fast_add, far, came))
        near = step(0.5 * mib, half_of(z_side), own)
        came = z_move("out", step(0.8 * mib, fast_add, near, came))
        root = step(0.8 * mib, fast_add, near, came)
        root = step(0.8 * mib, fast_add, root, y_move_at("end", root))
        first = z_move("in", root)
        second = z_move("mid", first)
        third = z_move("out", second)
        return (root, first), (third, second)

    quarter = units // 4
    whole_act = step(3.0, joined, *act)
    whole_branch_low = step(3.0, joined, *branch_low)
    down_grad = None
    for k in range(4):
        block = step(
            5.0,
            lambda a, b, k=k: dot(a[:, k * quarter : (k + 1) * quarter], b, 0, 0).astype(bf16),
            whole_act,
            whole_branch_low,
        )
        summed = (sum_middle if k % 2 else sum_ends)(block, 2.0)
        for side, pair in ((z_side, summed[0]), (1 - z_side, summed[1])):
            spot = (2 * k + side, 0)
            down_grad = put_only(down_grad, (units, full_width), spot, *pair, 1.0)

    gate_low, up_low = [], []
    for j in range(chunks):
        g, u = step(
            12.0,
            lambda low, gate, up: unfeed(low, w_down, gate, up),
            branch_low[j],
            gate[j],
            up[j],
            outs=2,
        )
        gate_low.append(g)
        up_low.append(u)

    whole_hid = step(3.0, joined, *hid_low)
    came = [y_move(low) for low in own_low]
    beside = [core_move(c) for c in came]
    neighbour_hid = step(
        3.0, lambda a0, a1, b0, b1: joined(a0, b0, a1, b1), *came, *beside
    )
    mid = units // 2
    piece_cols = mid // 2

    wide = []
    for lows in (gate_low, up_low):
        result = None
        for q in range(2):
            def cut(g0, g1, q=q):
                def columns(which):
                    start = which * mid + q * piece_cols
                    return joined(
                        *[lax.dynamic_slice_in_dim(g, start, piece_cols, 1) for g in (g0, g1)]
                    )

                return columns(y), columns(1 - y)

            keep, give = step(2.5, cut, *lows, outs=2)
            own = step(
                10.0,
                lambda h, k, n, c: (dot(h, k, 0, 0) + dot(n, c, 0, 0)).astype(bf16),
                whole_hid,
                keep,
                neighbour_hid,
                y_move(give),
            )
            shape = (full_width, units)
            piece, result = put(result, shape, (0, 2 * y + q), *line_sum(own, 2.0), 2.0)
            result = set_down(result, shape, (0, 2 * (1 - y) + q), y_move(piece), 2.0)
        wide.append(result)
    gate_grad, up_grad = wide

    hidden_grad, attn_low, attn_gains = [], [], []
    for j in range(chunks):
        keep, give = step(
            14.0,
            lambda g, u: unwide(g, u, w_gate, w_up),
            gate_low[j],
            up_low[j],
            outs=2,
        )
        chip, away = chip_sum(keep, give)

        def unjoin(chip, away, dy, total, scale, j=j):
            grad = own_rows(dy, j).astype(f32) + (chip.astype(f32) + away.astype(f32))
            gained = gain_attn * grad
            inner = jnp.sum(gained * total, 1, keepdims=True)
            low = (scale * gained - total * scale**3 / full_width * inner).astype(bf16)
            return low, grad, jnp.sum(grad * total * scale, 0)

        low, grad, gains = step(
            8.0, unjoin, chip, away, whole_dy, attn_total[j], attn_scale[j], outs=3
        )
        hidden_grad.append(grad)
        attn_gains.append(gains)
        attn_low.append(both(low))
    grad_own = own_columns(hidden_grad)
    whole_attn_low = step(3.0, joined, *attn_low)

    def unmix(low):
        grad = dot(low, w_out, 1, 1).astype(bf16)
        ordered = []
        for j in range(chunks):
            block = grad[j * chunk : (j + 1) * chunk]
            ordered += [part(block, core, half, 0), part(block, 1 - core, half, 0)]
        return jnp.concatenate(ordered, 0)

    mixed_grad = step(6.0, unmix, whole_attn_low)

    query_gained, key_gained, value_grad_low, dots, head_gains = step(
        21.0,
        lambda q, k, v, m, qp, kp, s, cos, sin: unattend_heads(
            q, k, v, m, segments, qp, kp, s, full_width, gain_query, gain_key, cos, sin
        ),
        query_rot,
        key_rot,
        value_low,
        mixed_grad,
        query_proj,
        key_proj,
        squares,
        cosine,
        sine,
        outs=5,
    )
    dots = small_sum(dots)

    def scaled_back(which, gained, projected):
        run = lambda g, p, s, d: unscale(g, p, s, d, which, full_width)
        return step(4.5, run, gained, projected, squares, dots)

    query_low = scaled_back(0, query_gained, query_proj)
    key_low = scaled_back(1, key_gained, key_proj)

    def pair_grad(left, right, shape):
        rows = shape[0] // 2
        give = step(
            3.0, lambda a, b: dot(part(a, 1 - y, rows, 1), b, 0, 0).astype(bf16), left, right
        )
        own = step(
            3.5,
            lambda a, b, c: (dot(part(a, y, rows, 1), b, 0, 0) + c.astype(f32)).astype(bf16),
            left,
            right,
            y_move(give),
        )
        piece, result = put(None, shape, (y, 0), *line_sum(own, 1.0), 1.0)
        return set_down(result, shape, (1 - y, 0), y_move(piece), 1.0)

    whole_mixed = step(1.5, joined, *mixed)
    out_grad = pair_grad(whole_mixed, whole_attn_low, (local_width, full_width))

    x_own = step(2.5, lambda x: part(x, core, row_count // 2, 0), whole_x)
    x_came = y_move(x_own)
    neighbour_x = step(3.0, joined, x_came, core_move(x_came))

    def core_first(value):
        rows = row_count // 2
        return joined(part(value, core, rows, 0), part(value, 1 - core, rows, 0))

    def narrow_grad(low):
        columns = local_width // 2
        keep, give = step(
            1.5, lambda v: (part(v, y, columns, 1), part(v, 1 - y, columns, 1)), low, outs=2
        )
        own = step(
            5.0,
            lambda x, k, n, c: (dot(x, k, 0, 0) + dot(n, core_first(c), 0, 0)).astype(bf16),
            whole_x,
            keep,
            neighbour_x,
            y_move(give),
        )
        shape = (full_width, local_width)
        piece, result = put(None, shape, (0, y), *line_sum(own, 1.0), 1.0)
        return set_down(result, shape, (0, 1 - y), y_move(piece), 1.0)

    value_wgrad = narrow_grad(value_grad_low)
    query_wgrad = narrow_grad(query_low)
    key_wgrad = narrow_grad(key_low)

    def column_part(which):
        def run(query_low, key_low, value_low):
            pieces = []
            for x in (0, 1):
                rows = (2 * x + which) * narrow
                total = 0.0
                for low, weight in ((query_low, w_query), (key_low, w_key), (value_low, w_value)):
                    total = total + dot(
                        low, lax.dynamic_slice_in_dim(weight, rows, narrow, 0), 1, 1
                    )
                pieces.append(total.astype(bf16))
            return pieces

        return run

    lows = (query_low, key_low, value_grad_low)
    give0, give1 = step(7.0, column_part(1 - core), *lows, outs=2)
    keep0, keep1 = step(7.0, column_part(core), *lows, outs=2)
    x_here = rank // 2

    def chip_columns(k0, k1, g0, g1):
        k0, k1 = low_add(k0, g0), low_add(k1, g1)
        first = x_here == 0
        return jnp.where(first, k0, k1), jnp.where(first, k1, k0)

    here, there = step(3.0, chip_columns, keep0, keep1, core_move(give0), core_move(give1), outs=2)
    input_grad = step(
        2.0,
        lambda a, b, c: (a.astype(f32) + b.astype(f32) + c).astype(bf16),
        here,
        x_move(there),
        grad_own,
    )

    wide_gains = step(
        1.0, lambda a, b, c, d: jnp.stack([a + b, c + d]), *mlp_gains, *attn_gains
    )

    def masked(a, b):
        mine = jnp.arange(full_width) // (full_width // 2) == rank // 2
        return jnp.where(mine, a + b, 0.0)

    wide_gains = step(1.0, masked, wide_gains, core_move(wide_gains))
    gains = step(
        1.0,
        lambda a, b, h: jnp.concatenate([(a + b).reshape(-1), h.reshape(-1)]),
        wide_gains,
        x_move(wide_gains),
        head_gains,
    )
    gains = step(0.6, lambda a, b: a + b, gains, y_move(gains))
    gains = step(0.6, lambda a, b: a + b, gains, z_move("in", gains))
    gains = step(0.6, lambda a, b: a + b, gains, z_move("mid", gains))
    gains = step(0.6, lambda a, b: jnp.where(outer, a, b), z_move("out", gains), gains)

    plan.run()
    results = (
        output,
        input_grad,
        query_wgrad,
        key_wgrad,
        value_wgrad,
        out_grad,
        gate_grad,
        up_grad,
        down_grad,
        gains,
    )
    values = [r.task.values[r.index] for r in results]
    gains = values.pop()
    return (
        *values,
        gains[2 * full_width : 2 * full_width + local_width],
        gains[2 * full_width + local_width :],
        gains[full_width : 2 * full_width],
        gains[:full_width],
    )


def solution(mesh):
    in_specs = (
        P("dp", "tensor"),
        P("dp", None),
        P("dp", "tensor"),
        P(None, "tensor"),
        P(None, "tensor"),
        P(None, "tensor"),
        P("tensor", None),
        P(None, "tensor"),
        P(None, "tensor"),
        P("tensor", None),
        P("tensor"),
        P("tensor"),
        P(),
        P(),
    )
    out_specs = (
        P("dp", "tensor"),
        P("dp", "tensor"),
        P(None, "tensor"),
        P(None, "tensor"),
        P(None, "tensor"),
        P("tensor", None),
        P(None, "tensor"),
        P(None, "tensor"),
        P("tensor", None),
        P("tensor"),
        P("tensor"),
        P(),
        P(),
    )
    body = fast_body if dict(mesh.shape) == {"dp": 8, "tensor": 4} else general_body
    return jax.shard_map(body, mesh=mesh, in_specs=in_specs, out_specs=out_specs, check_vma=False)
```

```python
import math

import jax
import jax.numpy as jnp
from jax import lax
from jax.experimental import pallas as pl
from jax.experimental.pallas import tpu as pltpu
from jax.sharding import PartitionSpec as P


HD = 128


epsilon = 1e-06
rope_base = 500000.0


def tables(segments):
    length = segments.shape[-1]
    places = jnp.broadcast_to(jnp.arange(length, dtype=jnp.int32), segments.shape)
    starts = jnp.concatenate(
        [jnp.ones(segments.shape[:-1] + (1,), dtype=bool), segments[..., 1:] != segments[..., :-1]],
        axis=-1,
    )
    firsts = lax.cummax(jnp.where(starts, places, 0), axis=segments.ndim - 1)
    offsets = (places - firsts).astype(jnp.float32)
    freqs = jnp.power(rope_base, -jnp.arange(0, HD, 2).astype(jnp.float32) / HD)
    angles = offsets[..., None] * freqs
    angles = jnp.concatenate([angles, angles], axis=-1)
    return (jnp.cos(angles), jnp.sin(angles))


def rotate(values, cosine, sine_table):
    half_dim = values.shape[-1] // 2
    turned = jnp.concatenate([-values[..., half_dim:], values[..., :half_dim]], axis=-1)
    return values * cosine + turned * sine_table


def rotate_back(gradient, cosine, sine_table):
    half_dim = gradient.shape[-1] // 2
    scaled = gradient * sine_table
    return gradient * cosine + jnp.concatenate(
        [scaled[..., half_dim:], -scaled[..., :half_dim]], axis=-1
    )


def column_sum(partial_value):
    return lax.psum_scatter(
        partial_value.astype(jnp.bfloat16), "tensor", scatter_dimension=1, tiled=True
    ).astype(jnp.float32)


def general_body(
    tokens,
    segments,
    cotangent,
    w_query,
    w_key,
    w_value,
    w_out,
    w_gate,
    w_up,
    w_down,
    gain_query,
    gain_key,
    gain_attn,
    gain_mlp,
):
    full_width = w_query.shape[0]
    row_count = tokens.shape[0]
    narrow = tokens.shape[1]
    local_width = w_query.shape[1]
    heads_here = local_width // HD
    tensor_rank = lax.axis_index("tensor")
    col_start = tensor_rank * narrow
    block_rows = min(512, row_count)
    block_count = row_count // block_rows
    score_scale = HD ** (-0.5)
    cosine, sine_table = tables(segments)
    cosine = cosine[0][:, None, :]
    sine_table = sine_table[0][:, None, :]
    doc_ids = segments[0]
    position = jnp.arange(row_count)
    gain_mlp_cols = lax.dynamic_slice_in_dim(gain_mlp, col_start, narrow, 0)
    whole_x, whole_dy = (
        lax.all_gather(tokens, "tensor", axis=1, tiled=True),
        lax.all_gather(cotangent, "tensor", axis=1, tiled=True),
    )
    query_proj = jnp.dot(whole_x, w_query, preferred_element_type=jnp.float32)
    key_proj = jnp.dot(whole_x, w_key, preferred_element_type=jnp.float32)
    value_proj = jnp.dot(whole_x, w_value, preferred_element_type=jnp.float32)
    query_sq, key_sq = lax.psum(
        (jnp.sum(query_proj * query_proj, 1), jnp.sum(key_proj * key_proj, 1)), "tensor"
    )
    query_scale = lax.rsqrt(query_sq / full_width + epsilon)[:, None]
    key_scale = lax.rsqrt(key_sq / full_width + epsilon)[:, None]
    query_rot = rotate(
        (query_proj * query_scale * gain_query).reshape(row_count, heads_here, HD),
        cosine,
        sine_table,
    ).astype(jnp.bfloat16)
    key_rot = rotate(
        (key_proj * key_scale * gain_key).reshape(row_count, heads_here, HD), cosine, sine_table
    ).astype(jnp.bfloat16)
    value_low = value_proj.astype(jnp.bfloat16).reshape(row_count, heads_here, HD)

    def scores_for(row_start):
        query_block = lax.dynamic_slice_in_dim(query_rot, row_start, block_rows, 0)
        ahead_rows = row_start + jnp.arange(block_rows)
        block_docs = lax.dynamic_slice_in_dim(doc_ids, row_start, block_rows, 0)
        allowed = (block_docs[:, None] == doc_ids[None, :]) & (
            ahead_rows[:, None] >= position[None, :]
        )
        scores = (
            jnp.einsum("qhd,khd->hqk", query_block, key_rot, preferred_element_type=jnp.float32)
            * score_scale
        )
        return (query_block, jnp.where(allowed[None], scores, -1e30))

    def attend_block(block_index):
        _, scores = scores_for(block_index * block_rows)
        row_max = jnp.max(scores, -1, keepdims=True)
        exp_terms = jnp.exp(scores - row_max)
        row_total = jnp.sum(exp_terms, -1, keepdims=True)
        weights = (exp_terms / row_total).astype(jnp.bfloat16)
        mixed_block = jnp.einsum(
            "hqk,khd->qhd", weights, value_low, preferred_element_type=jnp.float32
        )
        return (mixed_block, (row_max + jnp.log(row_total))[..., 0])

    mixed_out, log_sums = lax.map(attend_block, jnp.arange(block_count))
    mixed_low = mixed_out.reshape(row_count, local_width).astype(jnp.bfloat16)
    attn_part = jnp.dot(mixed_low, w_out, preferred_element_type=jnp.float32)
    attn_total = lax.psum(attn_part.astype(jnp.bfloat16), "tensor").astype(jnp.float32)
    attn_scale = lax.rsqrt(
        jnp.sum(attn_total * attn_total, 1, keepdims=True) / full_width + epsilon
    )
    hidden = whole_x.astype(jnp.float32) + attn_total * attn_scale * gain_attn
    hidden_low = hidden.astype(jnp.bfloat16)
    hidden_cols = lax.dynamic_slice_in_dim(hidden, col_start, narrow, 1)
    gate_proj = jnp.dot(hidden_low, w_gate, preferred_element_type=jnp.float32)
    up_proj = jnp.dot(hidden_low, w_up, preferred_element_type=jnp.float32)
    gate_silu = jax.nn.silu(gate_proj)
    act_low = (gate_silu * up_proj).astype(jnp.bfloat16)
    branch_part = jnp.dot(act_low, w_down, preferred_element_type=jnp.float32)
    branch = lax.psum(branch_part.astype(jnp.bfloat16), "tensor").astype(jnp.float32)
    branch_scale = lax.rsqrt(jnp.sum(branch * branch, 1, keepdims=True) / full_width + epsilon)
    branch_own = lax.dynamic_slice_in_dim(branch, col_start, narrow, 1)
    output = (hidden_cols + branch_own * branch_scale * gain_mlp_cols).astype(jnp.bfloat16)
    dy_full = whole_dy.astype(jnp.float32)
    gained = gain_mlp * dy_full
    row_inner = jnp.sum(gained * branch, 1, keepdims=True)
    branch_low = (
        branch_scale * gained - branch * branch_scale**3 / full_width * row_inner
    ).astype(jnp.bfloat16)
    owner_mask = jnp.arange(full_width) // narrow == tensor_rank
    gain_mlp_part = jnp.where(owner_mask, jnp.sum(dy_full * branch * branch_scale, 0), 0.0)
    down_wgrad = jnp.einsum("tf,td->fd", act_low, branch_low, preferred_element_type=jnp.float32)
    act_grad = jnp.einsum("td,fd->tf", branch_low, w_down, preferred_element_type=jnp.float32)
    sigma = jax.nn.sigmoid(gate_proj)
    gate_low = (act_grad * up_proj * sigma * (1.0 + gate_proj * (1.0 - sigma))).astype(jnp.bfloat16)
    up_low = (act_grad * gate_silu).astype(jnp.bfloat16)
    gate_wgrad = jnp.einsum("td,tf->df", hidden_low, gate_low, preferred_element_type=jnp.float32)
    up_wgrad = jnp.einsum("td,tf->df", hidden_low, up_low, preferred_element_type=jnp.float32)
    hidden_part = jnp.einsum(
        "tf,df->td", gate_low, w_gate, preferred_element_type=jnp.float32
    ) + jnp.einsum("tf,df->td", up_low, w_up, preferred_element_type=jnp.float32)
    hidden_sum, gain_mlp_grad = (
        lax.psum(hidden_part.astype(jnp.bfloat16), "tensor").astype(jnp.float32),
        lax.psum(gain_mlp_part.astype(jnp.bfloat16), "tensor").astype(jnp.float32),
    )
    hidden_grad = dy_full + hidden_sum
    gained_attn = gain_attn * hidden_grad
    attn_inner = jnp.sum(gained_attn * attn_total, 1, keepdims=True)
    attn_low = (
        attn_scale * gained_attn - attn_total * attn_scale**3 / full_width * attn_inner
    ).astype(jnp.bfloat16)
    gain_attn_grad = jnp.sum(hidden_grad * attn_total * attn_scale, 0)
    grad_own = lax.dynamic_slice_in_dim(hidden_grad, col_start, narrow, 1)
    out_wgrad = jnp.einsum("tc,td->cd", mixed_low, attn_low, preferred_element_type=jnp.float32)
    mixed_grad = (
        jnp.einsum("td,cd->tc", attn_low, w_out, preferred_element_type=jnp.float32)
        .astype(jnp.bfloat16)
        .reshape(row_count, heads_here, HD)
    )

    def attend_back(carry, block_index):
        key_acc, value_acc = carry
        row_start = block_index * block_rows
        query_block, scores = scores_for(row_start)
        grad_block = lax.dynamic_slice_in_dim(mixed_grad, row_start, block_rows, 0)
        probs = jnp.exp(scores - log_sums[block_index][..., None])
        probs_low = probs.astype(jnp.bfloat16)
        prob_grad = jnp.einsum(
            "qhd,khd->hqk", grad_block, value_low, preferred_element_type=jnp.float32
        )
        row_dot = jnp.sum(probs * prob_grad, -1, keepdims=True)
        score_low = (probs * (prob_grad - row_dot)).astype(jnp.bfloat16)
        query_part = (
            jnp.einsum("hqk,khd->qhd", score_low, key_rot, preferred_element_type=jnp.float32)
            * score_scale
        )
        key_acc = (
            key_acc
            + jnp.einsum("hqk,qhd->khd", score_low, query_block, preferred_element_type=jnp.float32)
            * score_scale
        )
        value_acc = value_acc + jnp.einsum(
            "hqk,qhd->khd", probs_low, grad_block, preferred_element_type=jnp.float32
        )
        return ((key_acc, value_acc), query_part)

    zero_acc = jnp.zeros((row_count, heads_here, HD), jnp.float32)
    (key_grad, value_grad), query_grad = lax.scan(
        attend_back, (zero_acc, zero_acc), jnp.arange(block_count)
    )
    query_grad = query_grad.reshape(row_count, heads_here, HD)
    query_normed_grad = rotate_back(query_grad, cosine, sine_table).reshape(row_count, local_width)
    key_normed_grad = rotate_back(key_grad, cosine, sine_table).reshape(row_count, local_width)
    gain_query_grad = jnp.sum(query_normed_grad * query_proj * query_scale, 0)
    gain_key_grad = jnp.sum(key_normed_grad * key_proj * key_scale, 0)
    query_gained = gain_query * query_normed_grad
    key_gained = gain_key * key_normed_grad
    query_dot, key_dot = lax.psum(
        (jnp.sum(query_gained * query_proj, 1), jnp.sum(key_gained * key_proj, 1)), "tensor"
    )
    query_low = (
        query_scale * query_gained - query_proj * query_scale**3 / full_width * query_dot[:, None]
    ).astype(jnp.bfloat16)
    key_low = (
        key_scale * key_gained - key_proj * key_scale**3 / full_width * key_dot[:, None]
    ).astype(jnp.bfloat16)
    value_grad_low = value_grad.reshape(row_count, local_width).astype(jnp.bfloat16)
    query_wgrad = jnp.einsum("td,tc->dc", whole_x, query_low, preferred_element_type=jnp.float32)
    key_wgrad = jnp.einsum("td,tc->dc", whole_x, key_low, preferred_element_type=jnp.float32)
    value_wgrad = jnp.einsum(
        "td,tc->dc", whole_x, value_grad_low, preferred_element_type=jnp.float32
    )
    input_part = jnp.einsum("tc,dc->td", query_low, w_query, preferred_element_type=jnp.float32)
    input_part = input_part + jnp.einsum(
        "tc,dc->td", key_low, w_key, preferred_element_type=jnp.float32
    )
    input_part = input_part + jnp.einsum(
        "tc,dc->td", value_grad_low, w_value, preferred_element_type=jnp.float32
    )
    input_grad = (column_sum(input_part) + grad_own).astype(jnp.bfloat16)
    pieces = (
        lax.psum_scatter(
            query_wgrad.astype(jnp.bfloat16), "dp", scatter_dimension=0, tiled=True
        ).astype(jnp.float32),
        lax.psum_scatter(
            key_wgrad.astype(jnp.bfloat16), "dp", scatter_dimension=0, tiled=True
        ).astype(jnp.float32),
        lax.psum_scatter(
            value_wgrad.astype(jnp.bfloat16), "dp", scatter_dimension=0, tiled=True
        ).astype(jnp.float32),
        lax.psum_scatter(
            out_wgrad.astype(jnp.bfloat16), "dp", scatter_dimension=1, tiled=True
        ).astype(jnp.float32),
        lax.psum_scatter(
            gate_wgrad.astype(jnp.bfloat16), "dp", scatter_dimension=0, tiled=True
        ).astype(jnp.float32),
        lax.psum_scatter(
            up_wgrad.astype(jnp.bfloat16), "dp", scatter_dimension=0, tiled=True
        ).astype(jnp.float32),
        lax.psum_scatter(
            down_wgrad.astype(jnp.bfloat16), "dp", scatter_dimension=1, tiled=True
        ).astype(jnp.float32),
        lax.psum_scatter(
            gain_query_grad.astype(jnp.bfloat16), "dp", scatter_dimension=0, tiled=True
        ).astype(jnp.float32),
        lax.psum_scatter(
            gain_key_grad.astype(jnp.bfloat16), "dp", scatter_dimension=0, tiled=True
        ).astype(jnp.float32),
        lax.psum_scatter(
            gain_attn_grad.astype(jnp.bfloat16), "dp", scatter_dimension=0, tiled=True
        ).astype(jnp.float32),
        lax.psum_scatter(
            gain_mlp_grad.astype(jnp.bfloat16), "dp", scatter_dimension=0, tiled=True
        ).astype(jnp.float32),
    )
    summed = (
        lax.all_gather(pieces[0].astype(jnp.bfloat16), "dp", axis=0, tiled=True).astype(
            jnp.float32
        ),
        lax.all_gather(pieces[1].astype(jnp.bfloat16), "dp", axis=0, tiled=True).astype(
            jnp.float32
        ),
        lax.all_gather(pieces[2].astype(jnp.bfloat16), "dp", axis=0, tiled=True).astype(
            jnp.float32
        ),
        lax.all_gather(pieces[3].astype(jnp.bfloat16), "dp", axis=1, tiled=True).astype(
            jnp.float32
        ),
        lax.all_gather(pieces[4].astype(jnp.bfloat16), "dp", axis=0, tiled=True).astype(
            jnp.float32
        ),
        lax.all_gather(pieces[5].astype(jnp.bfloat16), "dp", axis=0, tiled=True).astype(
            jnp.float32
        ),
        lax.all_gather(pieces[6].astype(jnp.bfloat16), "dp", axis=1, tiled=True).astype(
            jnp.float32
        ),
        lax.all_gather(pieces[7].astype(jnp.bfloat16), "dp", axis=0, tiled=True).astype(
            jnp.float32
        ),
        lax.all_gather(pieces[8].astype(jnp.bfloat16), "dp", axis=0, tiled=True).astype(
            jnp.float32
        ),
        lax.all_gather(pieces[9].astype(jnp.bfloat16), "dp", axis=0, tiled=True).astype(
            jnp.float32
        ),
        lax.all_gather(pieces[10].astype(jnp.bfloat16), "dp", axis=0, tiled=True).astype(
            jnp.float32
        ),
    )
    return (
        output,
        input_grad,
        summed[0],
        summed[1],
        summed[2],
        summed[3],
        summed[4],
        summed[5],
        summed[6],
        summed[7],
        summed[8],
        summed[9],
        summed[10],
    )


f32 = jnp.float32
bf16 = jnp.bfloat16

SWAP_Y = [(d, d ^ 1) for d in range(8)]
SWAP_Y_MIDDLE = [(d, d ^ 1) for d in range(2, 6)]
SWAP_Y_END = [(d, d ^ 1) for d in (0, 1, 6, 7)]
Z_IN = [(2 * a + y, 2 * b + y) for a, b in ((0, 1), (3, 2)) for y in (0, 1)]
Z_MID = [(2 * a + y, 2 * b + y) for a, b in ((1, 2), (2, 1)) for y in (0, 1)]
Z_OUT = [(2 * a + y, 2 * b + y) for a, b in ((1, 0), (2, 3)) for y in (0, 1)]
SWAP_CORE = [(t, t ^ 1) for t in range(4)]
SWAP_X = [(t, t ^ 2) for t in range(4)]


def over_dp(value, pairs):
    return lax.ppermute(value, "dp", pairs)


def to_core(value):
    return lax.ppermute(value, "tensor", SWAP_CORE)


def to_x(value):
    return lax.ppermute(value, "tensor", SWAP_X)


def low_add(left, right):
    return (left.astype(f32) + right.astype(f32)).astype(bf16)


def dot(left, right, left_axis=1, right_axis=0):
    return lax.dot_general(
        left, right, (((left_axis,), (right_axis,)), ((), ())), preferred_element_type=f32
    )


def part(value, index, size, axis):
    return lax.dynamic_slice_in_dim(value, index * size, size, axis)


def place_one(target, shape, use_first, first, second, row_block, col_block):
    rows, cols = second.shape
    steps = 2
    tile = rows // steps

    def kernel(spot_ref, first_ref, second_ref, *refs):
        @pl.when(spot_ref[2] == 1)
        def _():
            refs[-1][...] = first_ref[...].astype(f32)

        @pl.when(spot_ref[2] != 1)
        def _():
            refs[-1][...] = second_ref[...].astype(f32)

    spots = jnp.stack(
        [jnp.int32(row_block) * steps, jnp.int32(col_block), use_first.astype(jnp.int32)]
    )
    in_specs = [
        pl.BlockSpec((tile, cols), lambda i, spot: (i * spot[2], 0)),
        pl.BlockSpec((tile, cols), lambda i, spot: (i * (1 - spot[2]), 0)),
    ]
    operands = [spots, first, second]
    aliases = {}
    if target is not None:
        in_specs.append(pl.BlockSpec(memory_space=pl.ANY))
        operands.append(target)
        aliases = {3: 0}
    return pl.pallas_call(
        kernel,
        out_shape=jax.ShapeDtypeStruct(shape, f32),
        grid_spec=pltpu.PrefetchScalarGridSpec(
            num_scalar_prefetch=1,
            grid=(steps,),
            in_specs=in_specs,
            out_specs=pl.BlockSpec((tile, cols), lambda i, spot: (spot[0] + i, spot[1])),
        ),
        input_output_aliases=aliases,
        compiler_params=pltpu.CompilerParams(vmem_limit_bytes=16 << 20),
        cost_estimate=pl.CostEstimate(
            flops=rows * cols, bytes_accessed=6 * rows * cols, transcendentals=0
        ),
        name="place",
    )(*operands)


def place(target, shape, block, row_block, col_block):
    rows, cols = block.shape
    steps = 2
    tile = rows // steps

    def kernel(spot_ref, block_ref, target_ref, out_ref):
        out_ref[...] = block_ref[...].astype(f32)

    spots = jnp.stack([jnp.int32(row_block) * steps, jnp.int32(col_block)])
    return pl.pallas_call(
        kernel,
        out_shape=jax.ShapeDtypeStruct(shape, f32),
        grid_spec=pltpu.PrefetchScalarGridSpec(
            num_scalar_prefetch=1,
            grid=(steps,),
            in_specs=[
                pl.BlockSpec((tile, cols), lambda i, spot: (i, 0)),
                pl.BlockSpec(memory_space=pl.ANY),
            ],
            out_specs=pl.BlockSpec((tile, cols), lambda i, spot: (spot[0] + i, spot[1])),
        ),
        input_output_aliases={2: 0},
        compiler_params=pltpu.CompilerParams(vmem_limit_bytes=16 << 20),
        cost_estimate=pl.CostEstimate(
            flops=rows * cols, bytes_accessed=6 * rows * cols, transcendentals=0
        ),
        name="place",
    )(spots, block, target)


def matmul_call(kernel, steps, ins, outs, scratch=(), flops=0, mib=24, scalars=None):
    moved = sum(a.size * a.dtype.itemsize for a, _, _ in ins)
    moved += sum(math.prod(s) * jnp.dtype(d).itemsize for s, d, _, _ in outs)
    ahead = () if scalars is None else (scalars,)
    return pl.pallas_call(
        kernel,
        out_shape=[jax.ShapeDtypeStruct(s, d) for s, d, _, _ in outs],
        grid_spec=pltpu.PrefetchScalarGridSpec(
            num_scalar_prefetch=len(ahead),
            grid=(steps,),
            in_specs=[pl.BlockSpec(b, m) for _, b, m in ins],
            out_specs=[pl.BlockSpec(b, m) for _, _, b, m in outs],
            scratch_shapes=list(scratch),
        ),
        compiler_params=pltpu.CompilerParams(vmem_limit_bytes=mib << 20),
        cost_estimate=pl.CostEstimate(flops=flops, bytes_accessed=moved, transcendentals=0),
    )(*ahead, *[a for a, _, _ in ins])


def feed(low, w_gate, w_up):
    rows, width = low.shape
    units = w_gate.shape[1]
    tile = min(512, units)

    def kernel(low_ref, gate_w, up_w, gate_ref, up_ref, act_ref):
        gate = dot(low_ref[...], gate_w[...])
        up = dot(low_ref[...], up_w[...])
        gate_ref[...] = gate.astype(bf16)
        up_ref[...] = up.astype(bf16)
        act_ref[...] = (gate * jax.nn.sigmoid(gate) * up).astype(bf16)

    column = lambda n: (0, n)
    return matmul_call(
        kernel,
        units // tile,
        [
            (low, (rows, width), lambda n: (0, 0)),
            (w_gate, (width, tile), column),
            (w_up, (width, tile), column),
        ],
        [((rows, units), bf16, (rows, tile), column)] * 3,
        flops=4 * rows * width * units,
        mib=56,
    )


def unfeed(low, w_down, gate, up, y):
    rows, width = low.shape
    units = w_down.shape[0]
    tile = units // 4

    def kernel(_, low_ref, down_w, gate_ref, up_ref, *outs):
        grad = dot(low_ref[...], down_w[...], 1, 1)
        gate = gate_ref[...].astype(f32)
        sigma = jax.nn.sigmoid(gate)
        dup = (grad * (gate * sigma)).astype(bf16)
        dgate = (grad * up_ref[...].astype(f32) * sigma * (1.0 + gate * (1.0 - sigma))).astype(bf16)

        @pl.when(pl.program_id(0) < 2)
        def _():
            outs[0][...], outs[1][...] = dgate, dup

        @pl.when(pl.program_id(0) >= 2)
        def _():
            outs[2][...], outs[3][...] = dgate, dup

    def unit(n, y):
        return jnp.where(n < 2, 2 * (1 - y[0]) + n, 2 * y[0] + n - 2)

    column = lambda n, y: (0, unit(n, y))
    give = ((rows, units // 2), bf16, (rows, tile), lambda n, y: (0, jnp.minimum(n, 1)))
    keep = ((rows, units // 2), bf16, (rows, tile), lambda n, y: (0, jnp.maximum(n - 2, 0)))
    return matmul_call(
        kernel,
        4,
        [
            (low, (rows, width), lambda n, y: (0, 0)),
            (w_down, (tile, width), lambda n, y: (unit(n, y), 0)),
            (gate, (rows, tile), column),
            (up, (rows, tile), column),
        ],
        [give, give, keep, keep],
        flops=2 * rows * width * units,
        mib=56,
        scalars=y[None],
    )


def unwide(give_gate, give_up, keep_gate, keep_up, w_gate, w_up, y):
    rows, part_units = keep_gate.shape
    width, units = w_gate.shape
    tile = min(512, width)

    def kernel(_, give_g, give_u, keep_g, keep_u, give_gw, give_uw, keep_gw, keep_uw, upper_ref, lower_ref):
        total = dot(give_g[...], give_gw[...], 1, 1) + dot(give_u[...], give_uw[...], 1, 1)
        total += dot(keep_g[...], keep_gw[...], 1, 1) + dot(keep_u[...], keep_uw[...], 1, 1)
        upper_ref[...] = total[: rows // 2].astype(bf16)
        lower_ref[...] = total[rows // 2 :].astype(bf16)

    whole = lambda n, y: (0, 0)
    column = lambda n, y: (0, n)
    other = lambda n, y: (n, 1 - y[0])
    mine = lambda n, y: (n, y[0])
    lows = [(v, (rows, part_units), whole) for v in (give_gate, give_up, keep_gate, keep_up)]
    weights = [(w, (tile, part_units), m) for m in (other, mine) for w in (w_gate, w_up)]
    return matmul_call(
        kernel,
        width // tile,
        lows + weights,
        [((rows // 2, width), bf16, (rows // 2, tile), column)] * 2,
        flops=4 * rows * width * units,
        mib=56,
        scalars=y[None],
    )


def wide_grad(hid0, hid1, near0, next0, near1, next1, own0, own1, came0, came1):
    rows, cols = own0.shape
    width = hid0.shape[1]
    tile = min(512, width)
    half = rows // 2

    def kernel(h0, h1, n0, x0, n1, x1, o0, o1, c0, c1, left_ref, right_ref):
        total = dot(h0[...], o0[...], 0, 0) + dot(h1[...], o1[...], 0, 0)
        total += dot(n0[...], c0[:half], 0, 0) + dot(x0[...], c0[half:], 0, 0)
        total += dot(n1[...], c1[:half], 0, 0) + dot(x1[...], c1[half:], 0, 0)
        left_ref[...] = total[:, : cols // 2].astype(bf16)
        right_ref[...] = total[:, cols // 2 :].astype(bf16)

    lefts = (hid0, hid1, near0, next0, near1, next1)
    return matmul_call(
        kernel,
        width // tile,
        [(v, (v.shape[0], tile), lambda n: (0, n)) for v in lefts]
        + [(v, v.shape, lambda n: (0, 0)) for v in (own0, own1, came0, came1)],
        [((width, cols // 2), bf16, (tile, cols // 2), lambda n: (n, 0))] * 2,
        flops=8 * rows * width * cols,
        mib=56,
    )


def down_grad_rows(act0, act1, low0, low1, which):
    rows, units = act0.shape
    width = low0.shape[1]
    tile = units // 8

    def kernel(_, a0, a1, b0, b1, *outs):
        total = (dot(a0[...], b0[...], 0, 0) + dot(a1[...], b1[...], 0, 0)).astype(bf16)
        for n, out in enumerate(outs):
            @pl.when(pl.program_id(0) == n)
            def _(out=out):
                out[...] = total

    whole = lambda n, which: (0, 0)
    return matmul_call(
        kernel,
        4,
        [(a, (rows, tile), lambda n, which: (0, which[n])) for a in (act0, act1)]
        + [(b, (rows, width), whole) for b in (low0, low1)],
        [((tile, width), bf16, (tile, width), whole)] * 4,
        flops=4 * rows * width * units,
        mib=56,
        scalars=which,
    )


def input_columns(lows, weights, core):
    rows, cols = lows[0].shape
    narrow = weights[0].shape[0] // 4

    def kernel(_, a0, a1, a2, w0, w1, w2, give_ref, keep_ref):
        total = dot(a0[...], w0[...], 1, 1) + dot(a1[...], w1[...], 1, 1) + dot(a2[...], w2[...], 1, 1)
        total = total.astype(bf16)

        @pl.when(pl.program_id(0) < 2)
        def _():
            give_ref[0] = total

        @pl.when(pl.program_id(0) >= 2)
        def _():
            keep_ref[0] = total

    def block(n, core):
        return (jnp.where(n < 2, 2 * n + 1 - core[0], 2 * (n - 2) + core[0]), 0)

    return matmul_call(
        kernel,
        4,
        [(a, (rows, cols), lambda n, core: (0, 0)) for a in lows]
        + [(w, (narrow, cols), block) for w in weights],
        [
            ((2, rows, narrow), bf16, (1, rows, narrow), lambda n, core: (jnp.minimum(n, 1), 0, 0)),
            ((2, rows, narrow), bf16, (1, rows, narrow), lambda n, core: (jnp.maximum(n - 2, 0), 0, 0)),
        ],
        flops=24 * rows * cols * narrow,
        mib=56,
        scalars=core[None],
    )


def join_rows(chip, away, x, block, gain):
    rows, width = chip.shape
    tile = rows // 2

    def kernel(_, chip_ref, away_ref, x_ref, gain_ref, low_ref):
        total = chip_ref[...].astype(f32) + away_ref[...].astype(f32)
        scale = lax.rsqrt(jnp.sum(total * total, 1, keepdims=True) / width + epsilon)
        low_ref[...] = (x_ref[...].astype(f32) + total * scale * gain_ref[...]).astype(bf16)

    row = lambda i, b: (i, 0)
    return matmul_call(
        kernel,
        2,
        [
            (chip, (tile, width), row),
            (away, (tile, width), row),
            (x, (tile, width), lambda i, b: (2 * b[0] + i, 0)),
            (gain[None], (1, width), lambda i, b: (0, 0)),
        ],
        [((rows, width), bf16, (tile, width), row)],
        scalars=block[None],
    )[0]


def norm_back_rows(sums, grads, columns, base, block, rank, gain):
    rows, width = sums[0].shape
    narrow = columns[0].shape[1]
    tile = rows // 2
    kind = f32 if base is None else bf16
    extra = grads if base is None else (base,)

    def kernel(spot, *refs):
        first, second = refs[:2]
        more = refs[2 : 2 + len(extra)]
        pieces = refs[2 + len(extra) : 6 + len(extra)]
        gain_ref, low_ref, own_ref, give_ref, grad_ref = refs[6 + len(extra) :]
        lanes = [pl.ds(pl.multiple_of((spot[1] ^ k) * narrow, narrow), narrow) for k in range(4)]
        square = jnp.zeros((tile, 1), f32)
        inner = jnp.zeros((tile, 1), f32)

        def terms(k):
            total = first[:, lanes[k]].astype(f32) + second[:, lanes[k]].astype(f32)
            grad = pieces[k][...].astype(f32)
            if base is None:
                grad += more[0][:, lanes[k]].astype(f32) + more[1][:, lanes[k]].astype(f32)
            return total, grad

        for k in range(4):
            total, grad = terms(k)
            square += jnp.sum(total * total, 1, keepdims=True)
            inner += jnp.sum(grad * gain_ref[:, lanes[k]] * total, 1, keepdims=True)
        scale = lax.rsqrt(square / width + epsilon)
        back = scale * scale * scale / width * inner
        for k in range(4):
            total, grad = terms(k)
            gained = grad * gain_ref[:, lanes[k]]
            low_ref[:, lanes[k]] = (scale * gained - total * back).astype(bf16)
            normed = total * scale
            if k < 2:
                if base is None:
                    value = grad
                else:
                    value = more[0][:, lanes[k]].astype(f32) + normed * gain_ref[:, lanes[k]]
                (own_ref, give_ref)[k][...] = value.astype(kind)
            part_sum = jnp.sum(grad * normed, 0, keepdims=True)

            @pl.when(pl.program_id(0) == 0)
            def _():
                grad_ref[:, lanes[k]] = part_sum

            @pl.when(pl.program_id(0) > 0)
            def _():
                grad_ref[:, lanes[k]] += part_sum

    row = lambda i, s: (i, 0)
    whole = lambda i, s: (0, 0)
    return matmul_call(
        kernel,
        2,
        [(v, (tile, width), row) for v in (*sums, *extra)]
        + [(v, (tile, narrow), lambda i, s: (2 * s[0] + i, 0)) for v in columns]
        + [(gain[None], (1, width), whole)],
        [
            ((rows, width), bf16, (tile, width), row),
            ((rows, narrow), kind, (tile, narrow), row),
            ((rows, narrow), kind, (tile, narrow), row),
            ((1, width), f32, (1, width), whole),
        ],
        scalars=jnp.stack([block, rank]),
    )


def narrow_grads(x, beside, lows, came, y):
    rows, width = x.shape
    cols = came[0].shape[1]
    tile = min(512, width)

    def kernel(_, x_ref, beside_ref, *refs):
        for low, other, out in zip(refs[:3], refs[3:6], refs[6:]):
            total = dot(x_ref[...], low[...], 0, 0) + dot(beside_ref[...], other[...], 0, 0)
            out[...] = total.astype(bf16)

    column = lambda n, y: (0, n)
    return matmul_call(
        kernel,
        width // tile,
        [(v, (rows, tile), column) for v in (x, beside)]
        + [(v, (rows, cols), lambda n, y: (0, y[0])) for v in lows]
        + [(v, (rows, cols), lambda n, y: (0, 0)) for v in came],
        [((width, cols), bf16, (tile, cols), lambda n, y: (n, 0))] * 3,
        flops=12 * rows * width * cols,
        mib=56,
        scalars=y[None],
    )


def half_turned(values):
    lanes = lax.broadcasted_iota(jnp.int32, values.shape, 1)
    rolled = pltpu.roll(values, HD // 2, 1)
    return jnp.where(lanes < HD // 2, -rolled, rolled)


def as_column(row):
    return jnp.broadcast_to(row, (HD, row.shape[1])).T


def as_row(values):
    return jnp.sum(values.T, 0, keepdims=True)


def project(x, w_query, w_key, w_value):
    rows, width = x.shape
    cols = w_query.shape[1]
    tile = rows // 4

    def kernel(x_ref, q_w, k_w, v_w, q_ref, k_ref, v_ref, sum_ref):
        for which, (weight, result) in enumerate(((q_w, q_ref), (k_w, k_ref))):
            value = dot(x_ref[...], weight[...])
            result[...] = value
            square = value * value
            total = square[:, :HD]
            for start in range(HD, cols, HD):
                total = total + square[:, start : start + HD]
            sum_ref[which : which + 1] = as_row(total)
        v_ref[...] = dot(x_ref[...], v_w[...]).astype(bf16)

    row = lambda i: (i, 0)
    whole = lambda i: (0, 0)
    return matmul_call(
        kernel,
        rows // tile,
        [
            (x, (tile, width), row),
            (w_query, (width, cols), whole),
            (w_key, (width, cols), whole),
            (w_value, (width, cols), whole),
        ],
        [
            ((rows, cols), f32, (tile, cols), row),
            ((rows, cols), f32, (tile, cols), row),
            ((rows, cols), bf16, (tile, cols), row),
            ((2, rows), f32, (2, tile), lambda i: (0, i)),
        ],
        flops=6 * rows * width * cols,
        mib=56,
    )


def turn_heads(query, key, squares, full_width, gain_query, gain_key, cosine, sine):
    rows, width = query.shape

    def kernel(q_ref, k_ref, sum_ref, gq_ref, gk_ref, cos_ref, sin_ref, qr_ref, kr_ref):
        scales = lax.rsqrt(sum_ref[...] / full_width + epsilon)
        for value, col, gain, result in ((q_ref, 0, gq_ref, qr_ref), (k_ref, 1, gk_ref, kr_ref)):
            normed = value[...] * as_column(scales[col : col + 1]) * gain[...]
            result[...] = (normed * cos_ref[...] + half_turned(normed) * sin_ref[...]).astype(bf16)

    head = lambda h: (0, h)
    whole = lambda h: (0, 0)
    return matmul_call(
        kernel,
        width // HD,
        [
            (query, (rows, HD), head),
            (key, (rows, HD), head),
            (squares, (2, rows), whole),
            (gain_query[None], (1, HD), head),
            (gain_key[None], (1, HD), head),
            (cosine, (rows, HD), whole),
            (sine, (rows, HD), whole),
        ],
        [((rows, width), bf16, (rows, HD), head)] * 2,
        flops=10 * rows * width,
    )


BLOCK = 256


def key_span(block):
    first = max(0, block - 512 // BLOCK) * BLOCK
    return first, (block + 1) * BLOCK


def attend_heads(query, key, value, docs, blocks):
    width = query.shape[1]
    rows = len(blocks) * BLOCK
    last = blocks[-1] * BLOCK + BLOCK

    def kernel(q_ref, k_ref, v_ref, doc_ref, out_ref):
        for n, block in enumerate(blocks):
            begin, end = key_span(block)
            span = end - begin
            mine = slice(n * BLOCK, (n + 1) * BLOCK)
            own = slice(block * BLOCK, (block + 1) * BLOCK)
            scores = dot(q_ref[mine], k_ref[begin:end], 1, 1) * HD ** (-0.5)
            at_row = block * BLOCK + lax.broadcasted_iota(jnp.int32, (BLOCK, span), 0)
            at_col = begin + lax.broadcasted_iota(jnp.int32, (BLOCK, span), 1)
            doc = jnp.concatenate([as_column(doc_ref[:, own])] * (span // HD), 1)
            allowed = (doc == doc_ref[:, begin:end]) & (at_row >= at_col)
            scores = jnp.where(allowed, scores, -1e30)
            terms = jnp.exp(scores - jnp.max(scores, 1, keepdims=True))
            weights = (terms * (1.0 / jnp.sum(terms, 1, keepdims=True))).astype(bf16)
            out_ref[mine] = dot(weights, v_ref[begin:end]).astype(bf16)

    head = lambda h: (0, h)
    return matmul_call(
        kernel,
        width // HD,
        [
            (query, (rows, HD), lambda h: (blocks[0] // len(blocks), h)),
            (key, (last, HD), head),
            (value, (last, HD), head),
            (docs, docs.shape, lambda h: (0, 0)),
        ],
        [((rows, width), bf16, (rows, HD), head)],
        flops=4 * rows * last * width,
        mib=16,
    )[0]


def unattend_heads(query, key, value, grad, docs, q_proj, k_proj, squares, full_width, gain_query, gain_key, cosine, sine):
    rows, width = query.shape

    def kernel(
        q_ref, k_ref, v_ref, do_ref, doc_ref, qp_ref, kp_ref, sum_ref, gq_ref, gk_ref, cos_ref, sin_ref,
        dq_ref, dk_ref, dv_ref, dots_ref, gain_ref, q_acc, k_acc, v_acc,
    ):
        k_acc[...] = jnp.zeros_like(k_acc)
        v_acc[...] = jnp.zeros_like(v_acc)
        for block in range(rows // BLOCK):
            begin, end = key_span(block)
            span = end - begin
            mine = slice(block * BLOCK, (block + 1) * BLOCK)
            keys = k_ref[begin:end]
            do = do_ref[mine]
            scores = dot(keys, q_ref[mine], 1, 1) * HD ** (-0.5)
            at_key = begin + lax.broadcasted_iota(jnp.int32, (span, BLOCK), 0)
            at_query = block * BLOCK + lax.broadcasted_iota(jnp.int32, (span, BLOCK), 1)
            doc = jnp.concatenate([as_column(doc_ref[:, begin:end])] * (BLOCK // HD), 1)
            allowed = (doc == doc_ref[:, mine]) & (at_query >= at_key)
            scores = jnp.where(allowed, scores, -1e30)
            terms = jnp.exp(scores - jnp.max(scores, 0, keepdims=True))
            probs = terms * (1.0 / jnp.sum(terms, 0, keepdims=True))
            prob_grad = dot(v_ref[begin:end], do, 1, 1)
            inner = jnp.sum(probs * prob_grad, 0, keepdims=True)
            low = (probs * (prob_grad - inner)).astype(bf16)
            q_acc[mine] = dot(low, keys, 0, 0)
            k_acc[begin:end] += dot(low, q_ref[mine])
            v_acc[begin:end] += dot(probs.astype(bf16), do)
        dv_ref[...] = v_acc[...].astype(bf16)
        scales = lax.rsqrt(sum_ref[...] / full_width + epsilon)
        for which, (acc, proj, gain, result) in enumerate(
            ((q_acc, qp_ref, gq_ref, dq_ref), (k_acc, kp_ref, gk_ref, dk_ref))
        ):
            turned = acc[...] * HD ** (-0.5)
            normed = turned * cos_ref[...] - half_turned(turned * sin_ref[...])
            gained = normed * gain[...]
            result[...] = gained
            projected = proj[...]
            gain_ref[which : which + 1] = jnp.sum(
                normed * projected * as_column(scales[which : which + 1]), 0, keepdims=True
            )
            inner = as_row(gained * projected)

            @pl.when(pl.program_id(0) == 0)
            def _():
                dots_ref[which : which + 1] = inner

            @pl.when(pl.program_id(0) > 0)
            def _():
                dots_ref[which : which + 1] += inner

    head = lambda h: (0, h)
    whole = lambda h: (0, 0)
    column = (rows, HD)
    return matmul_call(
        kernel,
        width // HD,
        [
            (query, column, head),
            (key, column, head),
            (value, column, head),
            (grad, column, head),
            (docs, (1, rows), whole),
            (q_proj, column, head),
            (k_proj, column, head),
            (squares, (2, rows), whole),
            (gain_query[None], (1, HD), head),
            (gain_key[None], (1, HD), head),
            (cosine, column, whole),
            (sine, column, whole),
        ],
        [
            ((rows, width), f32, column, head),
            ((rows, width), f32, column, head),
            ((rows, width), bf16, column, head),
            ((2, rows), f32, (2, rows), whole),
            ((2, width), f32, (2, HD), head),
        ],
        scratch=[pltpu.VMEM((rows, HD), f32)] * 3,
        flops=10 * rows * rows * width,
        mib=56,
    )


def unscale(gained, projected, squares, dots, which, full_width, y):
    rows, cols = gained.shape
    tile = rows // 2

    def kernel(y_ref, gained_ref, proj_ref, sum_ref, dot_ref, out_ref, give_ref):
        scale = lax.rsqrt(sum_ref[which : which + 1] / full_width + epsilon)
        inner = scale**3 / full_width * dot_ref[which : which + 1]
        scale, inner = as_column(scale), as_column(inner)
        for start in range(0, cols, HD):
            lanes = slice(start, start + HD)
            out_ref[:, lanes] = (
                scale * gained_ref[:, lanes] - proj_ref[:, lanes] * inner
            ).astype(bf16)
        other = pl.multiple_of((1 - y_ref[0]) * (cols // 2), cols // 2)
        give_ref[...] = out_ref[:, pl.ds(other, cols // 2)]

    row = lambda i, y: (i, 0)
    column = lambda i, y: (0, i)
    return matmul_call(
        kernel,
        rows // tile,
        [
            (gained, (tile, cols), row),
            (projected, (tile, cols), row),
            (squares, (2, tile), column),
            (dots, (2, tile), column),
        ],
        [
            ((rows, cols), bf16, (tile, cols), row),
            ((rows, cols // 2), bf16, (tile, cols // 2), row),
        ],
        scalars=y[None],
    )


def fast_add(left, right):
    rows, cols = left.shape
    tile = rows // 2

    def kernel(left_ref, right_ref, out_ref):
        out_ref[...] = (left_ref[...].astype(f32) + right_ref[...].astype(f32)).astype(bf16)

    row = lambda i: (i, 0)
    return matmul_call(
        kernel,
        rows // tile,
        [(left, (tile, cols), row), (right, (tile, cols), row)],
        [((rows, cols), bf16, (tile, cols), row)],
        mib=12,
    )[0]


def pick_and_place(target, shape, use_first, first, second, row_block, col_block):
    rows, cols = first.shape
    tile = rows // 2
    steps = 2

    def kernel(spot_ref, first_ref, second_ref, *refs):
        low_ref, wide_ref = refs[-2:]

        @pl.when(spot_ref[2] == 1)
        def _():
            low_ref[...] = first_ref[...]
            wide_ref[...] = first_ref[...].astype(f32)

        @pl.when(spot_ref[2] != 1)
        def _():
            low_ref[...] = second_ref[...]
            wide_ref[...] = second_ref[...].astype(f32)

    spots = jnp.stack(
        [jnp.int32(row_block) * steps, jnp.int32(col_block), use_first.astype(jnp.int32)]
    )
    in_specs = [
        pl.BlockSpec((tile, cols), lambda i, spot: (i * spot[2], 0)),
        pl.BlockSpec((tile, cols), lambda i, spot: (i * (1 - spot[2]), 0)),
    ]
    operands = [spots, first, second]
    aliases = {}
    if target is not None:
        in_specs.append(pl.BlockSpec(memory_space=pl.ANY))
        operands.append(target)
        aliases = {3: 1}
    return pl.pallas_call(
        kernel,
        out_shape=[jax.ShapeDtypeStruct(first.shape, bf16), jax.ShapeDtypeStruct(shape, f32)],
        grid_spec=pltpu.PrefetchScalarGridSpec(
            num_scalar_prefetch=1,
            grid=(steps,),
            in_specs=in_specs,
            out_specs=[
                pl.BlockSpec((tile, cols), lambda i, spot: (i, 0)),
                pl.BlockSpec((tile, cols), lambda i, spot: (spot[0] + i, spot[1])),
            ],
        ),
        input_output_aliases=aliases,
        cost_estimate=pl.CostEstimate(
            flops=rows * cols, bytes_accessed=8 * rows * cols, transcendentals=0
        ),
        name="pick_and_place",
    )(*operands)


ORDER = [
    -2, -3, -6, 1, -4, -12, -11, 7, -9, 5, 15, -16, 17, -18, -8, 19, 20, 21, 22, -23,
    -13, 24, -25, 29, -10, 30, 14, -31, 175, 32, -33, 26, -27, -106, 28, 37, 38, -39, -108, 34,
    -35, -107, 40, -41, 36, 46, 47, -48, -109, 42, -43, -45, 49, -50, 44, 104, -129, 148, -110, -149,
    51, -52, -54, 150, -151, 53, 105, -130, 56, -57, 156, -157, -111, 80, -81, 58, -59, 131, -132, -94,
    158, -159, -70, 82, 60, -61, 152, -154, -153, -83, 155, 112, -113, 62, 160, -162, -161, 84, 133, -134,
    163, 165, 166, -63, -85, -140, 167, 114, -115, 174, -187, 135, -168, -136, 86, -87, 169, -170, 71, 220,
    -221, 171, 176, -121, 222, -223, 164, -177, 224, 141, -142, 172, -188, 116, -117, 88, 137, -138, 178, -179,
    173, 215, 122, -123, -216, 143, -72, -144, 118, -225, 64, 180, -181, -119, 95, -96, -189, 139, 73, 217,
    -218, 226, -227, 124, -125, -65, 145, 97, 228, -229, -74, 230, 182, -183, 219, -89, -146, 120, -66, 68,
    190, -207, -98, 75, 126, -67, -191, -127, -76, 55, -199, 208, -209, 184, -185, -90, 99, 69, 147, 192,
    210, -211, 77, -78, 200, 128, -193, -201, -91, 212, -213, 186, 194, -195, 79, 92, 202, -203, 196, -197,
    93, -100, 214, 204, -205, -231, 198, 101, -102, 206, 232, 103,
]


class Handle:
    def __init__(self, task, index=None):
        self.task, self.index = task, index


class Task:
    def __init__(self, function, inputs, link):
        self.function, self.inputs, self.link, self.values = function, inputs, link, None
        self.handle = Handle(self, 0)


class Plan:
    window = 2

    def __init__(self):
        self.tasks = []

    def add(self, function, inputs, link):
        task = Task(function, inputs, link)
        self.tasks.append(task)
        return task

    def step(self, cost, function, *inputs, outs=1):
        task = self.add(function, inputs, ())
        if outs == 1:
            return task.handle
        return (task.handle, *[Handle(task, k) for k in range(1, outs)])

    def move(self, link, function, value):
        links = {"y": ("y_middle", "y_end")}.get(link, (link,))
        return self.add(function, (value,), links).handle

    def run(self):
        last, sent = None, {}

        def fence(task, extra):
            handles = list(task.inputs) + [h for h in extra if h not in task.inputs]
            values = [h.task.values[h.index] if isinstance(h, Handle) else h for h in handles]
            if extra:
                values = lax.optimization_barrier(tuple(values))
                for handle, fresh in zip(handles, values):
                    if isinstance(handle, Handle):
                        handle.task.values[handle.index] = fresh
            return values[: len(task.inputs)]

        for number in ORDER:
            task = self.tasks[abs(number) - 1]
            extra = [last] if last is not None else []
            for link in task.link:
                earlier = sent.setdefault(link, [])
                if len(earlier) >= self.window and earlier[-self.window] not in extra:
                    extra.append(earlier[-self.window])
                earlier.append(task.handle)
            fenced = fence(task, extra)
            result = task.function(*fenced)
            task.values = list(result) if isinstance(result, (tuple, list)) else [result]
            if number > 0:
                last = task.handle


def in_order(rank, *pieces):
    rows, cols = pieces[0].shape
    tile = rows // 2

    def kernel(rank_ref, *refs):
        for k in range(4):
            start = pl.multiple_of((rank_ref[0] ^ k) * cols, cols)
            refs[4][:, pl.ds(start, cols)] = refs[k][...]

    return pl.pallas_call(
        kernel,
        out_shape=jax.ShapeDtypeStruct((rows, 4 * cols), pieces[0].dtype),
        grid_spec=pltpu.PrefetchScalarGridSpec(
            num_scalar_prefetch=1,
            grid=(rows // tile,),
            in_specs=[pl.BlockSpec((tile, cols), lambda i, rank: (i, 0))] * 4,
            out_specs=pl.BlockSpec((tile, 4 * cols), lambda i, rank: (i, 0)),
        ),
        compiler_params=pltpu.CompilerParams(vmem_limit_bytes=24 << 20),
        cost_estimate=pl.CostEstimate(
            flops=rows * cols, bytes_accessed=16 * rows * cols, transcendentals=0
        ),
        name="in_order",
    )(rank[None], *pieces)


def fast_body(
    tokens,
    segments,
    cotangent,
    w_query,
    w_key,
    w_value,
    w_out,
    w_gate,
    w_up,
    w_down,
    gain_query,
    gain_key,
    gain_attn,
    gain_mlp,
):
    full_width = w_query.shape[0]
    row_count, _ = tokens.shape
    local_width = w_query.shape[1]
    units = w_gate.shape[1]
    rank = lax.axis_index("tensor")
    core = rank % 2
    dp_rank = lax.axis_index("dp")
    y = dp_rank % 2
    z = dp_rank // 2
    z_side = z // 2
    outer = (z == 0) | (z == 3)
    chunks = 2
    chunk = row_count // chunks
    half = chunk // 2

    plan = Plan()
    step = plan.step

    def core_move(value):
        return plan.move("core", to_core, value)

    def x_move(value):
        return plan.move("x", to_x, value)

    def y_move(value):
        return plan.move("y", lambda v: over_dp(v, SWAP_Y), value)

    def y_move_at(where, value):
        pairs = {"middle": SWAP_Y_MIDDLE, "end": SWAP_Y_END}[where]
        return plan.move("y_" + where, lambda v: over_dp(v, pairs), value)

    def z_move(which, value):
        pairs = {"in": Z_IN, "mid": Z_MID, "out": Z_OUT}[which]
        return plan.move(which, lambda v: over_dp(v, pairs), value)

    def gathered(value):
        across = x_move(value)
        return value, core_move(value), across, core_move(across)

    def ordered(pieces):
        return step(4.9, lambda *p: in_order(rank, *p), *pieces)

    def prepare(value):
        cosine, sine = tables(segments)
        return value, cosine[0], sine[0]

    _, cosine, sine = step(6.0, prepare, tokens, outs=3)
    x_pieces = gathered(tokens)
    whole_x = ordered(x_pieces)
    near_tokens = y_move(tokens)
    dy_pieces = gathered(step(0.0, lambda v, _: v, cotangent, x_pieces[2]))
    neighbour_x = ordered(gathered(near_tokens))

    def small_sum(value):
        value = step(0.2, lambda a, b: a + b, value, core_move(value))
        return step(0.2, lambda a, b: a + b, value, x_move(value))

    query_proj, key_proj, value_low, squares = step(
        11.0, lambda x: project(x, w_query, w_key, w_value), whole_x, outs=4
    )
    squares = small_sum(squares)

    query_rot, key_rot = step(
        5.5,
        lambda q, k, s, cos, sin: turn_heads(q, k, s, full_width, gain_query, gain_key, cos, sin),
        query_proj,
        key_proj,
        squares,
        cosine,
        sine,
        outs=2,
    )

    def attend(query, key, value, j):
        per = chunk // BLOCK
        blocks = list(range(j * per, (j + 1) * per))
        block = attend_heads(query, key, value, segments, blocks)
        return jnp.concatenate([part(block, core, half, 0), part(block, 1 - core, half, 0)], 0)

    def halves(value):
        value = value.astype(bf16)
        return value[:half], value[half:]

    def chip_sum(keep, give):
        chip = step(1.8, fast_add, keep, core_move(give))
        return chip, x_move(chip)

    def both(value):
        return step(1.7, lambda a, b: jnp.concatenate([a, b], 0), value, core_move(value))

    mixed, attn_sums, own_low, hid_low = [], [], [], []
    for j in range(chunks):
        block = step(
            5.5 + j,
            lambda q, k, v, j=j: attend(q, k, v, j),
            query_rot,
            key_rot,
            value_low,
        )
        mixed.append(block)
        keep, give = step(2.6, lambda m: halves(dot(m, w_out)), block, outs=2)
        chip, away = chip_sum(keep, give)

        low = step(
            3.6,
            lambda a, b, x, j=j: join_rows(a, b, x, 2 * j + core, gain_attn),
            chip,
            away,
            whole_x,
        )
        attn_sums.append((chip, away))
        own_low.append(low)
        hid_low.append(both(low))

    gate, up, act, outs, branch_low, mlp_gains = [], [], [], [], [], []
    for j in range(chunks):
        g, u, a = step(14.5, lambda low: feed(low, w_gate, w_up), hid_low[j], outs=3)
        gate.append(g)
        up.append(u)
        act.append(a)
        keep, give = step(9.3, lambda a: halves(dot(a, w_down)), a, outs=2)
        chip, away = chip_sum(keep, give)

        low, own, give, gains = step(
            4.8,
            lambda a, b, h, *dy, j=j: norm_back_rows((a, b), (), dy, h, 2 * j + core, rank, gain_mlp),
            chip,
            away,
            own_low[j],
            *dy_pieces,
            outs=4,
        )
        branch_low.append(both(low))
        outs.append((own, core_move(give)))
        mlp_gains.append(gains)

    def own_columns(pairs):
        def merge(*values):
            pieces = []
            for keep, came in zip(values[::2], values[1::2]):
                pieces += [jnp.where(core == 0, keep, came), jnp.where(core == 0, came, keep)]
            return jnp.concatenate(pieces, 0)

        return step(3.5, merge, *[v for pair in pairs for v in pair])

    output = own_columns(outs)

    def joined(*values):
        return jnp.concatenate(values, 0)

    def line_sum(own, mib):
        near = step(0.6 + 1.6 * mib, fast_add, own, z_move("in", own))
        total = step(0.6 + 1.6 * mib, fast_add, near, z_move("mid", near))
        return z_move("out", total), total

    def put(target, shape, spots, first, second, mib):
        if target is None:
            run = lambda a, b: pick_and_place(None, shape, outer, a, b, *spots)
            return step(2.2 + 1.4 * mib, run, first, second, outs=2)
        run = lambda a, b, t: pick_and_place(t, shape, outer, a, b, *spots)
        return step(2.2 + 1.4 * mib, run, first, second, target, outs=2)

    def set_down(target, shape, spots, value, mib):
        run = lambda v, t: place(t, shape, v, *spots)
        return step(2.3 + 0.9 * mib, run, value, target)

    def put_only(target, shape, spots, first, second, mib):
        run = lambda a, b, *t: place_one(*(t or (None,)), shape, outer, a, b, *spots)
        rest = () if target is None else (target,)
        return step(2.3 + 0.9 * mib, run, first, second, *rest)

    def sum_ends(far, near, mib):
        came = z_move("in", far)
        came = z_move("mid", step(2.3 * mib, fast_add, far, came))
        came = z_move("out", step(2.3 * mib, fast_add, near, came))
        root = step(2.3 * mib, fast_add, near, came)
        root = step(2.3 * mib, fast_add, root, y_move_at("end", root))
        first = z_move("in", root)
        second = z_move("mid", first)
        third = z_move("out", second)
        return (root, first), (third, second)

    down_grad, shape = None, (units, full_width)
    for k in (0, 2):
        which = jnp.stack([2 * k + 1 - z_side, 2 * k + z_side, 2 * k + 3 - y, 2 * k + 2 + y])
        far, near, give, keep = step(
            8.5,
            lambda *v, which=which: down_grad_rows(*v, which),
            *act,
            *branch_low,
            outs=4,
        )
        summed = sum_ends(far, near, 1.0)
        for side, pair in ((z_side, summed[0]), (1 - z_side, summed[1])):
            down_grad = put_only(down_grad, shape, (2 * k + side, 0), *pair, 1.0)
        own = step(2.3, fast_add, keep, y_move(give))
        piece, down_grad = put(down_grad, shape, (2 * k + 2 + y, 0), *line_sum(own, 1.0), 1.0)
        spot = (2 * k + 3 - y, 0)
        down_grad = set_down(down_grad, shape, spot, y_move(piece), 1.0)

    lows = []
    for j in range(chunks):
        lows.append(
            step(
                12.0,
                lambda low, gate, up: unfeed(low, w_down, gate, up, y),
                branch_low[j],
                gate[j],
                up[j],
                outs=4,
            )
        )

    near = [y_move(low) for low in own_low]
    beside = [core_move(n) for n in near]
    wide = []
    for which in range(2):
        came = [y_move(low[which]) for low in lows]
        pieces = step(
            14.5,
            wide_grad,
            *hid_low,
            near[0],
            beside[0],
            near[1],
            beside[1],
            *[low[2 + which] for low in lows],
            *came,
            outs=2,
        )
        result, shape = None, (full_width, units)
        for q, own in enumerate(pieces):
            piece, result = put(result, shape, (0, 2 * y + q), *line_sum(own, 2.0), 2.0)
            result = set_down(result, shape, (0, 2 * (1 - y) + q), y_move(piece), 2.0)
        wide.append(result)
    gate_grad, up_grad = wide

    hidden_grad, attn_low, attn_gains = [], [], []
    for j in range(chunks):
        keep, give = step(
            14.0,
            lambda *v: unwide(*v, w_gate, w_up, y),
            *lows[j],
            outs=2,
        )
        chip, away = chip_sum(keep, give)

        low, own, give, gains = step(
            5.5,
            lambda a, b, c, d, *dy, j=j: norm_back_rows(
                (a, b), (c, d), dy, None, 2 * j + core, rank, gain_attn
            ),
            *attn_sums[j],
            chip,
            away,
            *dy_pieces,
            outs=4,
        )
        hidden_grad.append((own, core_move(give)))
        attn_gains.append(gains)
        attn_low.append(both(low))
    grad_own = own_columns(hidden_grad)
    whole_attn_low = step(3.0, joined, *attn_low)

    def unmix(low):
        grad = dot(low, w_out, 1, 1).astype(bf16)
        ordered = []
        for j in range(chunks):
            block = grad[j * chunk : (j + 1) * chunk]
            ordered += [part(block, core, half, 0), part(block, 1 - core, half, 0)]
        return jnp.concatenate(ordered, 0)

    mixed_grad = step(6.0, unmix, whole_attn_low)

    query_gained, key_gained, value_grad_low, dots, head_gains = step(
        19.5,
        lambda q, k, v, m, qp, kp, s, cos, sin: unattend_heads(
            q, k, v, m, segments, qp, kp, s, full_width, gain_query, gain_key, cos, sin
        ),
        query_rot,
        key_rot,
        value_low,
        mixed_grad,
        query_proj,
        key_proj,
        squares,
        cosine,
        sine,
        outs=5,
    )
    dots = small_sum(dots)

    def scaled_back(which, gained, projected):
        run = lambda g, p, s, d: unscale(g, p, s, d, which, full_width, y)
        return step(3.5, run, gained, projected, squares, dots, outs=2)

    query_low, query_give = scaled_back(0, query_gained, query_proj)
    key_low, key_give = scaled_back(1, key_gained, key_proj)
    value_give = step(
        1.0, lambda v: part(v, 1 - y, local_width // 2, 1), value_grad_low
    )

    def pair_grad(left, right, shape):
        rows = shape[0] // 2
        give = step(
            4.8, lambda a, b: dot(part(a, 1 - y, rows, 1), b, 0, 0).astype(bf16), left, right
        )
        own = step(
            4.8,
            lambda a, b, c: (dot(part(a, y, rows, 1), b, 0, 0) + c.astype(f32)).astype(bf16),
            left,
            right,
            y_move(give),
        )
        piece, result = put(None, shape, (y, 0), *line_sum(own, 1.0), 1.0)
        return set_down(result, shape, (1 - y, 0), y_move(piece), 1.0)

    whole_mixed = step(1.5, joined, *mixed)
    out_grad = pair_grad(whole_mixed, whole_attn_low, (local_width, full_width))

    came = [y_move(give) for give in (value_give, query_give, key_give)]
    pieces = step(
        11.0,
        lambda x, n, v, q, k, cv, cq, ck: narrow_grads(x, n, (v, q, k), (cv, cq, ck), y),
        whole_x,
        neighbour_x,
        value_grad_low,
        query_low,
        key_low,
        *came,
        outs=3,
    )
    narrow_results = []
    for own in pieces:
        shape = (full_width, local_width)
        piece, result = put(None, shape, (0, y), *line_sum(own, 1.0), 1.0)
        narrow_results.append(set_down(result, shape, (0, 1 - y), y_move(piece), 1.0))
    value_wgrad, query_wgrad, key_wgrad = narrow_results

    give, keep = step(
        10.0,
        lambda *v: input_columns(v, (w_query, w_key, w_value), core),
        query_low,
        key_low,
        value_grad_low,
        outs=2,
    )
    x_here = rank // 2

    def chip_columns(keep, came):
        total = low_add(keep, came)
        return (
            lax.dynamic_index_in_dim(total, x_here, 0, False),
            lax.dynamic_index_in_dim(total, 1 - x_here, 0, False),
        )

    here, there = step(3.5, chip_columns, keep, core_move(give), outs=2)
    input_grad = step(
        2.0,
        lambda a, b, c: (a.astype(f32) + b.astype(f32) + c).astype(bf16),
        here,
        x_move(there),
        grad_own,
    )

    wide_gains = step(
        0.3, lambda a, b, c, d: joined(a + b, c + d), *mlp_gains, *attn_gains
    )

    def masked(a, b):
        mine = jnp.arange(full_width) // (full_width // 2) == rank // 2
        return jnp.where(mine, a + b, 0.0)

    wide_gains = step(0.3, masked, wide_gains, core_move(wide_gains))
    gains = step(
        1.0,
        lambda a, b, h: jnp.concatenate([(a + b).reshape(-1), h.reshape(-1)]),
        wide_gains,
        x_move(wide_gains),
        head_gains,
    )
    gains = step(0.2, lambda a, b: a + b, gains, y_move(gains))
    gains = step(0.2, lambda a, b: a + b, gains, z_move("in", gains))
    gains = step(0.2, lambda a, b: a + b, gains, z_move("mid", gains))
    gains = step(0.2, lambda a, b: jnp.where(outer, a, b), z_move("out", gains), gains)

    plan.run()
    results = (
        output,
        input_grad,
        query_wgrad,
        key_wgrad,
        value_wgrad,
        out_grad,
        gate_grad,
        up_grad,
        down_grad,
        gains,
    )
    values = [r.task.values[r.index] for r in results]
    gains = values.pop()
    return (
        *values,
        gains[2 * full_width : 2 * full_width + local_width],
        gains[2 * full_width + local_width :],
        gains[full_width : 2 * full_width],
        gains[:full_width],
    )


def solution(mesh):
    in_specs = (
        P("dp", "tensor"),
        P("dp", None),
        P("dp", "tensor"),
        P(None, "tensor"),
        P(None, "tensor"),
        P(None, "tensor"),
        P("tensor", None),
        P(None, "tensor"),
        P(None, "tensor"),
        P("tensor", None),
        P("tensor"),
        P("tensor"),
        P(),
        P(),
    )
    out_specs = (
        P("dp", "tensor"),
        P("dp", "tensor"),
        P(None, "tensor"),
        P(None, "tensor"),
        P(None, "tensor"),
        P("tensor", None),
        P(None, "tensor"),
        P(None, "tensor"),
        P("tensor", None),
        P("tensor"),
        P("tensor"),
        P(),
        P(),
    )
    body = fast_body if dict(mesh.shape) == {"dp": 8, "tensor": 4} else general_body
    return jax.shard_map(body, mesh=mesh, in_specs=in_specs, out_specs=out_specs, check_vma=False)
```

```python
import math

import jax
import jax.numpy as jnp
from jax import lax
from jax.experimental import pallas as pl
from jax.experimental.pallas import tpu as pltpu
from jax.sharding import PartitionSpec as P


HD = 128


epsilon = 1e-06
rope_base = 500000.0


def tables(segments):
    length = segments.shape[-1]
    places = jnp.broadcast_to(jnp.arange(length, dtype=jnp.int32), segments.shape)
    starts = jnp.concatenate(
        [jnp.ones(segments.shape[:-1] + (1,), dtype=bool), segments[..., 1:] != segments[..., :-1]],
        axis=-1,
    )
    firsts = lax.cummax(jnp.where(starts, places, 0), axis=segments.ndim - 1)
    offsets = (places - firsts).astype(jnp.float32)
    freqs = jnp.power(rope_base, -jnp.arange(0, HD, 2).astype(jnp.float32) / HD)
    angles = offsets[..., None] * freqs
    angles = jnp.concatenate([angles, angles], axis=-1)
    return (jnp.cos(angles), jnp.sin(angles))


def rotate(values, cosine, sine_table):
    half_dim = values.shape[-1] // 2
    turned = jnp.concatenate([-values[..., half_dim:], values[..., :half_dim]], axis=-1)
    return values * cosine + turned * sine_table


def rotate_back(gradient, cosine, sine_table):
    half_dim = gradient.shape[-1] // 2
    scaled = gradient * sine_table
    return gradient * cosine + jnp.concatenate(
        [scaled[..., half_dim:], -scaled[..., :half_dim]], axis=-1
    )


def column_sum(partial_value):
    return lax.psum_scatter(
        partial_value.astype(jnp.bfloat16), "tensor", scatter_dimension=1, tiled=True
    ).astype(jnp.float32)


def general_body(
    tokens,
    segments,
    cotangent,
    w_query,
    w_key,
    w_value,
    w_out,
    w_gate,
    w_up,
    w_down,
    gain_query,
    gain_key,
    gain_attn,
    gain_mlp,
):
    full_width = w_query.shape[0]
    row_count = tokens.shape[0]
    narrow = tokens.shape[1]
    local_width = w_query.shape[1]
    heads_here = local_width // HD
    tensor_rank = lax.axis_index("tensor")
    col_start = tensor_rank * narrow
    block_rows = min(512, row_count)
    block_count = row_count // block_rows
    score_scale = HD ** (-0.5)
    cosine, sine_table = tables(segments)
    cosine = cosine[0][:, None, :]
    sine_table = sine_table[0][:, None, :]
    doc_ids = segments[0]
    position = jnp.arange(row_count)
    gain_mlp_cols = lax.dynamic_slice_in_dim(gain_mlp, col_start, narrow, 0)
    whole_x, whole_dy = (
        lax.all_gather(tokens, "tensor", axis=1, tiled=True),
        lax.all_gather(cotangent, "tensor", axis=1, tiled=True),
    )
    query_proj = jnp.dot(whole_x, w_query, preferred_element_type=jnp.float32)
    key_proj = jnp.dot(whole_x, w_key, preferred_element_type=jnp.float32)
    value_proj = jnp.dot(whole_x, w_value, preferred_element_type=jnp.float32)
    query_sq, key_sq = lax.psum(
        (jnp.sum(query_proj * query_proj, 1), jnp.sum(key_proj * key_proj, 1)), "tensor"
    )
    query_scale = lax.rsqrt(query_sq / full_width + epsilon)[:, None]
    key_scale = lax.rsqrt(key_sq / full_width + epsilon)[:, None]
    query_rot = rotate(
        (query_proj * query_scale * gain_query).reshape(row_count, heads_here, HD),
        cosine,
        sine_table,
    ).astype(jnp.bfloat16)
    key_rot = rotate(
        (key_proj * key_scale * gain_key).reshape(row_count, heads_here, HD), cosine, sine_table
    ).astype(jnp.bfloat16)
    value_low = value_proj.astype(jnp.bfloat16).reshape(row_count, heads_here, HD)

    def scores_for(row_start):
        query_block = lax.dynamic_slice_in_dim(query_rot, row_start, block_rows, 0)
        ahead_rows = row_start + jnp.arange(block_rows)
        block_docs = lax.dynamic_slice_in_dim(doc_ids, row_start, block_rows, 0)
        allowed = (block_docs[:, None] == doc_ids[None, :]) & (
            ahead_rows[:, None] >= position[None, :]
        )
        scores = (
            jnp.einsum("qhd,khd->hqk", query_block, key_rot, preferred_element_type=jnp.float32)
            * score_scale
        )
        return (query_block, jnp.where(allowed[None], scores, -1e30))

    def attend_block(block_index):
        _, scores = scores_for(block_index * block_rows)
        row_max = jnp.max(scores, -1, keepdims=True)
        exp_terms = jnp.exp(scores - row_max)
        row_total = jnp.sum(exp_terms, -1, keepdims=True)
        weights = (exp_terms / row_total).astype(jnp.bfloat16)
        mixed_block = jnp.einsum(
            "hqk,khd->qhd", weights, value_low, preferred_element_type=jnp.float32
        )
        return (mixed_block, (row_max + jnp.log(row_total))[..., 0])

    mixed_out, log_sums = lax.map(attend_block, jnp.arange(block_count))
    mixed_low = mixed_out.reshape(row_count, local_width).astype(jnp.bfloat16)
    attn_part = jnp.dot(mixed_low, w_out, preferred_element_type=jnp.float32)
    attn_total = lax.psum(attn_part.astype(jnp.bfloat16), "tensor").astype(jnp.float32)
    attn_scale = lax.rsqrt(
        jnp.sum(attn_total * attn_total, 1, keepdims=True) / full_width + epsilon
    )
    hidden = whole_x.astype(jnp.float32) + attn_total * attn_scale * gain_attn
    hidden_low = hidden.astype(jnp.bfloat16)
    hidden_cols = lax.dynamic_slice_in_dim(hidden, col_start, narrow, 1)
    gate_proj = jnp.dot(hidden_low, w_gate, preferred_element_type=jnp.float32)
    up_proj = jnp.dot(hidden_low, w_up, preferred_element_type=jnp.float32)
    gate_silu = jax.nn.silu(gate_proj)
    act_low = (gate_silu * up_proj).astype(jnp.bfloat16)
    branch_part = jnp.dot(act_low, w_down, preferred_element_type=jnp.float32)
    branch = lax.psum(branch_part.astype(jnp.bfloat16), "tensor").astype(jnp.float32)
    branch_scale = lax.rsqrt(jnp.sum(branch * branch, 1, keepdims=True) / full_width + epsilon)
    branch_own = lax.dynamic_slice_in_dim(branch, col_start, narrow, 1)
    output = (hidden_cols + branch_own * branch_scale * gain_mlp_cols).astype(jnp.bfloat16)
    dy_full = whole_dy.astype(jnp.float32)
    gained = gain_mlp * dy_full
    row_inner = jnp.sum(gained * branch, 1, keepdims=True)
    branch_low = (
        branch_scale * gained - branch * branch_scale**3 / full_width * row_inner
    ).astype(jnp.bfloat16)
    owner_mask = jnp.arange(full_width) // narrow == tensor_rank
    gain_mlp_part = jnp.where(owner_mask, jnp.sum(dy_full * branch * branch_scale, 0), 0.0)
    down_wgrad = jnp.einsum("tf,td->fd", act_low, branch_low, preferred_element_type=jnp.float32)
    act_grad = jnp.einsum("td,fd->tf", branch_low, w_down, preferred_element_type=jnp.float32)
    sigma = jax.nn.sigmoid(gate_proj)
    gate_low = (act_grad * up_proj * sigma * (1.0 + gate_proj * (1.0 - sigma))).astype(jnp.bfloat16)
    up_low = (act_grad * gate_silu).astype(jnp.bfloat16)
    gate_wgrad = jnp.einsum("td,tf->df", hidden_low, gate_low, preferred_element_type=jnp.float32)
    up_wgrad = jnp.einsum("td,tf->df", hidden_low, up_low, preferred_element_type=jnp.float32)
    hidden_part = jnp.einsum(
        "tf,df->td", gate_low, w_gate, preferred_element_type=jnp.float32
    ) + jnp.einsum("tf,df->td", up_low, w_up, preferred_element_type=jnp.float32)
    hidden_sum, gain_mlp_grad = (
        lax.psum(hidden_part.astype(jnp.bfloat16), "tensor").astype(jnp.float32),
        lax.psum(gain_mlp_part.astype(jnp.bfloat16), "tensor").astype(jnp.float32),
    )
    hidden_grad = dy_full + hidden_sum
    gained_attn = gain_attn * hidden_grad
    attn_inner = jnp.sum(gained_attn * attn_total, 1, keepdims=True)
    attn_low = (
        attn_scale * gained_attn - attn_total * attn_scale**3 / full_width * attn_inner
    ).astype(jnp.bfloat16)
    gain_attn_grad = jnp.sum(hidden_grad * attn_total * attn_scale, 0)
    grad_own = lax.dynamic_slice_in_dim(hidden_grad, col_start, narrow, 1)
    out_wgrad = jnp.einsum("tc,td->cd", mixed_low, attn_low, preferred_element_type=jnp.float32)
    mixed_grad = (
        jnp.einsum("td,cd->tc", attn_low, w_out, preferred_element_type=jnp.float32)
        .astype(jnp.bfloat16)
        .reshape(row_count, heads_here, HD)
    )

    def attend_back(carry, block_index):
        key_acc, value_acc = carry
        row_start = block_index * block_rows
        query_block, scores = scores_for(row_start)
        grad_block = lax.dynamic_slice_in_dim(mixed_grad, row_start, block_rows, 0)
        probs = jnp.exp(scores - log_sums[block_index][..., None])
        probs_low = probs.astype(jnp.bfloat16)
        prob_grad = jnp.einsum(
            "qhd,khd->hqk", grad_block, value_low, preferred_element_type=jnp.float32
        )
        row_dot = jnp.sum(probs * prob_grad, -1, keepdims=True)
        score_low = (probs * (prob_grad - row_dot)).astype(jnp.bfloat16)
        query_part = (
            jnp.einsum("hqk,khd->qhd", score_low, key_rot, preferred_element_type=jnp.float32)
            * score_scale
        )
        key_acc = (
            key_acc
            + jnp.einsum("hqk,qhd->khd", score_low, query_block, preferred_element_type=jnp.float32)
            * score_scale
        )
        value_acc = value_acc + jnp.einsum(
            "hqk,qhd->khd", probs_low, grad_block, preferred_element_type=jnp.float32
        )
        return ((key_acc, value_acc), query_part)

    zero_acc = jnp.zeros((row_count, heads_here, HD), jnp.float32)
    (key_grad, value_grad), query_grad = lax.scan(
        attend_back, (zero_acc, zero_acc), jnp.arange(block_count)
    )
    query_grad = query_grad.reshape(row_count, heads_here, HD)
    query_normed_grad = rotate_back(query_grad, cosine, sine_table).reshape(row_count, local_width)
    key_normed_grad = rotate_back(key_grad, cosine, sine_table).reshape(row_count, local_width)
    gain_query_grad = jnp.sum(query_normed_grad * query_proj * query_scale, 0)
    gain_key_grad = jnp.sum(key_normed_grad * key_proj * key_scale, 0)
    query_gained = gain_query * query_normed_grad
    key_gained = gain_key * key_normed_grad
    query_dot, key_dot = lax.psum(
        (jnp.sum(query_gained * query_proj, 1), jnp.sum(key_gained * key_proj, 1)), "tensor"
    )
    query_low = (
        query_scale * query_gained - query_proj * query_scale**3 / full_width * query_dot[:, None]
    ).astype(jnp.bfloat16)
    key_low = (
        key_scale * key_gained - key_proj * key_scale**3 / full_width * key_dot[:, None]
    ).astype(jnp.bfloat16)
    value_grad_low = value_grad.reshape(row_count, local_width).astype(jnp.bfloat16)
    query_wgrad = jnp.einsum("td,tc->dc", whole_x, query_low, preferred_element_type=jnp.float32)
    key_wgrad = jnp.einsum("td,tc->dc", whole_x, key_low, preferred_element_type=jnp.float32)
    value_wgrad = jnp.einsum(
        "td,tc->dc", whole_x, value_grad_low, preferred_element_type=jnp.float32
    )
    input_part = jnp.einsum("tc,dc->td", query_low, w_query, preferred_element_type=jnp.float32)
    input_part = input_part + jnp.einsum(
        "tc,dc->td", key_low, w_key, preferred_element_type=jnp.float32
    )
    input_part = input_part + jnp.einsum(
        "tc,dc->td", value_grad_low, w_value, preferred_element_type=jnp.float32
    )
    input_grad = (column_sum(input_part) + grad_own).astype(jnp.bfloat16)
    pieces = (
        lax.psum_scatter(
            query_wgrad.astype(jnp.bfloat16), "dp", scatter_dimension=0, tiled=True
        ).astype(jnp.float32),
        lax.psum_scatter(
            key_wgrad.astype(jnp.bfloat16), "dp", scatter_dimension=0, tiled=True
        ).astype(jnp.float32),
        lax.psum_scatter(
            value_wgrad.astype(jnp.bfloat16), "dp", scatter_dimension=0, tiled=True
        ).astype(jnp.float32),
        lax.psum_scatter(
            out_wgrad.astype(jnp.bfloat16), "dp", scatter_dimension=1, tiled=True
        ).astype(jnp.float32),
        lax.psum_scatter(
            gate_wgrad.astype(jnp.bfloat16), "dp", scatter_dimension=0, tiled=True
        ).astype(jnp.float32),
        lax.psum_scatter(
            up_wgrad.astype(jnp.bfloat16), "dp", scatter_dimension=0, tiled=True
        ).astype(jnp.float32),
        lax.psum_scatter(
            down_wgrad.astype(jnp.bfloat16), "dp", scatter_dimension=1, tiled=True
        ).astype(jnp.float32),
        lax.psum_scatter(
            gain_query_grad.astype(jnp.bfloat16), "dp", scatter_dimension=0, tiled=True
        ).astype(jnp.float32),
        lax.psum_scatter(
            gain_key_grad.astype(jnp.bfloat16), "dp", scatter_dimension=0, tiled=True
        ).astype(jnp.float32),
        lax.psum_scatter(
            gain_attn_grad.astype(jnp.bfloat16), "dp", scatter_dimension=0, tiled=True
        ).astype(jnp.float32),
        lax.psum_scatter(
            gain_mlp_grad.astype(jnp.bfloat16), "dp", scatter_dimension=0, tiled=True
        ).astype(jnp.float32),
    )
    summed = (
        lax.all_gather(pieces[0].astype(jnp.bfloat16), "dp", axis=0, tiled=True).astype(
            jnp.float32
        ),
        lax.all_gather(pieces[1].astype(jnp.bfloat16), "dp", axis=0, tiled=True).astype(
            jnp.float32
        ),
        lax.all_gather(pieces[2].astype(jnp.bfloat16), "dp", axis=0, tiled=True).astype(
            jnp.float32
        ),
        lax.all_gather(pieces[3].astype(jnp.bfloat16), "dp", axis=1, tiled=True).astype(
            jnp.float32
        ),
        lax.all_gather(pieces[4].astype(jnp.bfloat16), "dp", axis=0, tiled=True).astype(
            jnp.float32
        ),
        lax.all_gather(pieces[5].astype(jnp.bfloat16), "dp", axis=0, tiled=True).astype(
            jnp.float32
        ),
        lax.all_gather(pieces[6].astype(jnp.bfloat16), "dp", axis=1, tiled=True).astype(
            jnp.float32
        ),
        lax.all_gather(pieces[7].astype(jnp.bfloat16), "dp", axis=0, tiled=True).astype(
            jnp.float32
        ),
        lax.all_gather(pieces[8].astype(jnp.bfloat16), "dp", axis=0, tiled=True).astype(
            jnp.float32
        ),
        lax.all_gather(pieces[9].astype(jnp.bfloat16), "dp", axis=0, tiled=True).astype(
            jnp.float32
        ),
        lax.all_gather(pieces[10].astype(jnp.bfloat16), "dp", axis=0, tiled=True).astype(
            jnp.float32
        ),
    )
    return (
        output,
        input_grad,
        summed[0],
        summed[1],
        summed[2],
        summed[3],
        summed[4],
        summed[5],
        summed[6],
        summed[7],
        summed[8],
        summed[9],
        summed[10],
    )


f32 = jnp.float32
bf16 = jnp.bfloat16

SWAP_Y = [(d, d ^ 1) for d in range(8)]
SWAP_Y_MIDDLE = [(d, d ^ 1) for d in range(2, 6)]
SWAP_Y_END = [(d, d ^ 1) for d in (0, 1, 6, 7)]
Z_IN = [(2 * a + y, 2 * b + y) for a, b in ((0, 1), (3, 2)) for y in (0, 1)]
Z_MID = [(2 * a + y, 2 * b + y) for a, b in ((1, 2), (2, 1)) for y in (0, 1)]
Z_OUT = [(2 * a + y, 2 * b + y) for a, b in ((1, 0), (2, 3)) for y in (0, 1)]
SWAP_CORE = [(t, t ^ 1) for t in range(4)]
SWAP_X = [(t, t ^ 2) for t in range(4)]


def over_dp(value, pairs):
    return lax.ppermute(value, "dp", pairs)


def to_core(value):
    return lax.ppermute(value, "tensor", SWAP_CORE)


def to_x(value):
    return lax.ppermute(value, "tensor", SWAP_X)


def low_add(left, right):
    return (left.astype(f32) + right.astype(f32)).astype(bf16)


def dot(left, right, left_axis=1, right_axis=0):
    return lax.dot_general(
        left, right, (((left_axis,), (right_axis,)), ((), ())), preferred_element_type=f32
    )


def part(value, index, size, axis):
    return lax.dynamic_slice_in_dim(value, index * size, size, axis)


def place_one(target, shape, use_first, first, second, row_block, col_block):
    rows, cols = second.shape
    steps = 2
    tile = rows // steps

    def kernel(spot_ref, first_ref, second_ref, *refs):
        @pl.when(spot_ref[2] == 1)
        def _():
            refs[-1][...] = first_ref[...].astype(f32)

        @pl.when(spot_ref[2] != 1)
        def _():
            refs[-1][...] = second_ref[...].astype(f32)

    spots = jnp.stack(
        [jnp.int32(row_block) * steps, jnp.int32(col_block), use_first.astype(jnp.int32)]
    )
    in_specs = [
        pl.BlockSpec((tile, cols), lambda i, spot: (i * spot[2], 0)),
        pl.BlockSpec((tile, cols), lambda i, spot: (i * (1 - spot[2]), 0)),
    ]
    operands = [spots, first, second]
    aliases = {}
    if target is not None:
        in_specs.append(pl.BlockSpec(memory_space=pl.ANY))
        operands.append(target)
        aliases = {3: 0}
    return pl.pallas_call(
        kernel,
        out_shape=jax.ShapeDtypeStruct(shape, f32),
        grid_spec=pltpu.PrefetchScalarGridSpec(
            num_scalar_prefetch=1,
            grid=(steps,),
            in_specs=in_specs,
            out_specs=pl.BlockSpec((tile, cols), lambda i, spot: (spot[0] + i, spot[1])),
        ),
        input_output_aliases=aliases,
        compiler_params=pltpu.CompilerParams(vmem_limit_bytes=16 << 20),
        cost_estimate=pl.CostEstimate(
            flops=rows * cols, bytes_accessed=6 * rows * cols, transcendentals=0
        ),
        name="place",
    )(*operands)


def place(target, shape, block, row_block, col_block):
    rows, cols = block.shape
    steps = 2
    tile = rows // steps

    def kernel(spot_ref, block_ref, target_ref, out_ref):
        out_ref[...] = block_ref[...].astype(f32)

    spots = jnp.stack([jnp.int32(row_block) * steps, jnp.int32(col_block)])
    return pl.pallas_call(
        kernel,
        out_shape=jax.ShapeDtypeStruct(shape, f32),
        grid_spec=pltpu.PrefetchScalarGridSpec(
            num_scalar_prefetch=1,
            grid=(steps,),
            in_specs=[
                pl.BlockSpec((tile, cols), lambda i, spot: (i, 0)),
                pl.BlockSpec(memory_space=pl.ANY),
            ],
            out_specs=pl.BlockSpec((tile, cols), lambda i, spot: (spot[0] + i, spot[1])),
        ),
        input_output_aliases={2: 0},
        compiler_params=pltpu.CompilerParams(vmem_limit_bytes=16 << 20),
        cost_estimate=pl.CostEstimate(
            flops=rows * cols, bytes_accessed=6 * rows * cols, transcendentals=0
        ),
        name="place",
    )(spots, block, target)


def matmul_call(kernel, steps, ins, outs, scratch=(), flops=0, mib=24, scalars=None):
    moved = sum(a.size * a.dtype.itemsize for a, _, _ in ins)
    moved += sum(math.prod(s) * jnp.dtype(d).itemsize for s, d, _, _ in outs)
    ahead = () if scalars is None else (scalars,)
    return pl.pallas_call(
        kernel,
        out_shape=[jax.ShapeDtypeStruct(s, d) for s, d, _, _ in outs],
        grid_spec=pltpu.PrefetchScalarGridSpec(
            num_scalar_prefetch=len(ahead),
            grid=(steps,),
            in_specs=[pl.BlockSpec(b, m) for _, b, m in ins],
            out_specs=[pl.BlockSpec(b, m) for _, _, b, m in outs],
            scratch_shapes=list(scratch),
        ),
        compiler_params=pltpu.CompilerParams(vmem_limit_bytes=mib << 20),
        cost_estimate=pl.CostEstimate(flops=flops, bytes_accessed=moved, transcendentals=0),
    )(*ahead, *[a for a, _, _ in ins])


def feed(own, other, w_gate, w_up, w_down):
    half, width = own.shape
    rows = 2 * half
    units = w_gate.shape[1]
    tile = min(512, units)
    steps = units // tile

    def kernel(own_in, other_in, gate_w, up_w, down_w, gate_ref, up_ref, act_ref, own_ref, other_ref, low_ref, sum_ref):
        step = pl.program_id(0)

        @pl.when(step == 0)
        def _():
            low_ref[:half] = own_in[...]
            low_ref[half:] = other_in[...]

        gate = dot(low_ref[...], gate_w[...])
        up = dot(low_ref[...], up_w[...])
        gate_ref[...] = gate.astype(bf16)
        up_ref[...] = up.astype(bf16)
        act = (gate * jax.nn.sigmoid(gate) * up).astype(bf16)
        act_ref[...] = act
        term = dot(act, down_w[...])

        @pl.when(step == 0)
        def _():
            sum_ref[...] = term

        @pl.when((step > 0) & (step < steps - 1))
        def _():
            sum_ref[...] += term

        @pl.when(step == steps - 1)
        def _():
            own_ref[...] = (sum_ref[:half] + term[:half]).astype(bf16)
            other_ref[...] = (sum_ref[half:] + term[half:]).astype(bf16)

    column = lambda n: (0, n)
    whole = lambda n: (0, 0)
    return matmul_call(
        kernel,
        steps,
        [
            (own, (half, width), whole),
            (other, (half, width), whole),
            (w_gate, (width, tile), column),
            (w_up, (width, tile), column),
            (w_down, (tile, width), lambda n: (n, 0)),
        ],
        [((rows, units), bf16, (rows, tile), column)] * 3 + [((half, width), bf16, (half, width), whole)] * 2,
        scratch=[pltpu.VMEM((rows, width), bf16), pltpu.VMEM((rows, width), f32)],
        flops=6 * rows * width * units,
        mib=58,
    )


def unfeed(own, other, w_down, gate, up, y):
    half, width = own.shape
    rows = 2 * half
    units = w_down.shape[0]
    tile = units // 4

    def kernel(_, own_in, other_in, down_w, gate_ref, up_ref, *outs):
        *outs, low_ref = outs

        @pl.when(pl.program_id(0) == 0)
        def _():
            low_ref[:half] = own_in[...]
            low_ref[half:] = other_in[...]

        grad = dot(low_ref[...], down_w[...], 1, 1)
        gate = gate_ref[...].astype(f32)
        sigma = jax.nn.sigmoid(gate)
        dup = (grad * (gate * sigma)).astype(bf16)
        dgate = (grad * up_ref[...].astype(f32) * sigma * (1.0 + gate * (1.0 - sigma))).astype(bf16)

        @pl.when(pl.program_id(0) < 2)
        def _():
            outs[0][...], outs[1][...] = dgate, dup

        @pl.when(pl.program_id(0) >= 2)
        def _():
            outs[2][...], outs[3][...] = dgate, dup

    def unit(n, y):
        return jnp.where(n < 2, 2 * (1 - y[0]) + n, 2 * y[0] + n - 2)

    column = lambda n, y: (0, unit(n, y))
    give = ((rows, units // 2), bf16, (rows, tile), lambda n, y: (0, jnp.minimum(n, 1)))
    keep = ((rows, units // 2), bf16, (rows, tile), lambda n, y: (0, jnp.maximum(n - 2, 0)))
    return matmul_call(
        kernel,
        4,
        [
            (own, (half, width), lambda n, y: (0, 0)),
            (other, (half, width), lambda n, y: (0, 0)),
            (w_down, (tile, width), lambda n, y: (unit(n, y), 0)),
            (gate, (rows, tile), column),
            (up, (rows, tile), column),
        ],
        [give, give, keep, keep],
        scratch=[pltpu.VMEM((rows, width), bf16)],
        flops=2 * rows * width * units,
        mib=56,
        scalars=y[None],
    )


def unwide(give_gate, give_up, keep_gate, keep_up, w_gate, w_up, y):
    rows, part_units = keep_gate.shape
    width, units = w_gate.shape
    tile = min(512, width)

    def kernel(_, give_g, give_u, keep_g, keep_u, give_gw, give_uw, keep_gw, keep_uw, upper_ref, lower_ref):
        total = dot(give_g[...], give_gw[...], 1, 1) + dot(give_u[...], give_uw[...], 1, 1)
        total += dot(keep_g[...], keep_gw[...], 1, 1) + dot(keep_u[...], keep_uw[...], 1, 1)
        upper_ref[...] = total[: rows // 2].astype(bf16)
        lower_ref[...] = total[rows // 2 :].astype(bf16)

    whole = lambda n, y: (0, 0)
    column = lambda n, y: (0, n)
    other = lambda n, y: (n, 1 - y[0])
    mine = lambda n, y: (n, y[0])
    lows = [(v, (rows, part_units), whole) for v in (give_gate, give_up, keep_gate, keep_up)]
    weights = [(w, (tile, part_units), m) for m in (other, mine) for w in (w_gate, w_up)]
    return matmul_call(
        kernel,
        width // tile,
        lows + weights,
        [((rows // 2, width), bf16, (rows // 2, tile), column)] * 2,
        flops=4 * rows * width * units,
        mib=56,
        scalars=y[None],
    )


def wide_grad(hids, nears, own0, own1, came0, came1):
    rows, cols = own0.shape
    width = hids[0].shape[1]
    tile = min(512, width)
    half = rows // 2

    def kernel(*refs):
        lefts, (o0, o1, c0, c1), (left_ref, right_ref) = refs[:8], refs[8:12], refs[12:]
        total = jnp.zeros((tile, cols), f32)
        for n, low in enumerate((o0, o1, c0, c1)):
            total += dot(lefts[2 * n][...], low[:half], 0, 0)
            total += dot(lefts[2 * n + 1][...], low[half:], 0, 0)
        left_ref[...] = total[:, : cols // 2].astype(bf16)
        right_ref[...] = total[:, cols // 2 :].astype(bf16)

    return matmul_call(
        kernel,
        width // tile,
        [(v, (half, tile), lambda n: (0, n)) for v in (*hids, *nears)]
        + [(v, v.shape, lambda n: (0, 0)) for v in (own0, own1, came0, came1)],
        [((width, cols // 2), bf16, (tile, cols // 2), lambda n: (n, 0))] * 2,
        flops=8 * rows * width * cols,
        mib=56,
    )


def down_grad_rows(acts, lows, which):
    rows, units = acts[0].shape
    half, width = lows[0].shape
    tile = units // 8

    def kernel(_, a0, a1, b0, b1, b2, b3, *outs):
        total = dot(a0[:half], b0[...], 0, 0) + dot(a0[half:], b1[...], 0, 0)
        total += dot(a1[:half], b2[...], 0, 0) + dot(a1[half:], b3[...], 0, 0)
        total = total.astype(bf16)
        for n, out in enumerate(outs):
            @pl.when(pl.program_id(0) == n)
            def _(out=out):
                out[...] = total

    whole = lambda n, which: (0, 0)
    return matmul_call(
        kernel,
        4,
        [(a, (rows, tile), lambda n, which: (0, which[n])) for a in acts]
        + [(b, (half, width), whole) for b in lows],
        [((tile, width), bf16, (tile, width), whole)] * 4,
        flops=4 * rows * width * units,
        mib=56,
        scalars=which,
    )


def input_columns(lows, weights, core):
    rows, cols = lows[0].shape
    narrow = weights[0].shape[0] // 4

    def kernel(_, a0, a1, a2, w0, w1, w2, give_ref, keep_ref):
        total = dot(a0[...], w0[...], 1, 1) + dot(a1[...], w1[...], 1, 1) + dot(a2[...], w2[...], 1, 1)
        total = total.astype(bf16)

        @pl.when(pl.program_id(0) < 2)
        def _():
            give_ref[0] = total

        @pl.when(pl.program_id(0) >= 2)
        def _():
            keep_ref[0] = total

    def block(n, core):
        return (jnp.where(n < 2, 2 * n + 1 - core[0], 2 * (n - 2) + core[0]), 0)

    return matmul_call(
        kernel,
        4,
        [(a, (rows, cols), lambda n, core: (0, 0)) for a in lows]
        + [(w, (narrow, cols), block) for w in weights],
        [
            ((2, rows, narrow), bf16, (1, rows, narrow), lambda n, core: (jnp.minimum(n, 1), 0, 0)),
            ((2, rows, narrow), bf16, (1, rows, narrow), lambda n, core: (jnp.maximum(n - 2, 0), 0, 0)),
        ],
        flops=24 * rows * cols * narrow,
        mib=56,
        scalars=core[None],
    )


def join_rows(chip, away, x, block, gain):
    rows, width = chip.shape
    tile = rows // 2

    def kernel(_, chip_ref, away_ref, x_ref, gain_ref, low_ref):
        total = chip_ref[...].astype(f32) + away_ref[...].astype(f32)
        scale = lax.rsqrt(jnp.sum(total * total, 1, keepdims=True) / width + epsilon)
        low_ref[...] = (x_ref[...].astype(f32) + total * scale * gain_ref[...]).astype(bf16)

    row = lambda i, b: (i, 0)
    return matmul_call(
        kernel,
        2,
        [
            (chip, (tile, width), row),
            (away, (tile, width), row),
            (x, (tile, width), lambda i, b: (2 * b[0] + i, 0)),
            (gain[None], (1, width), lambda i, b: (0, 0)),
        ],
        [((rows, width), bf16, (tile, width), row)],
        mib=56,
        scalars=block[None],
    )[0]


def norm_back_rows(sums, grads, columns, base, block, rank, gain):
    rows, width = sums[0].shape
    narrow = columns[0].shape[1]
    tile = rows // 2
    kind = f32 if base is None else bf16
    extra = grads if base is None else (base,)

    def kernel(spot, *refs):
        first, second = refs[:2]
        more = refs[2 : 2 + len(extra)]
        pieces = refs[2 + len(extra) : 6 + len(extra)]
        gain_ref, low_ref, own_ref, give_ref, grad_ref = refs[6 + len(extra) :]
        lanes = [pl.ds(pl.multiple_of((spot[1] ^ k) * narrow, narrow), narrow) for k in range(4)]
        square = jnp.zeros((tile, 1), f32)
        inner = jnp.zeros((tile, 1), f32)

        def terms(k):
            total = first[:, lanes[k]].astype(f32) + second[:, lanes[k]].astype(f32)
            grad = pieces[k][...].astype(f32)
            if base is None:
                grad += more[0][:, lanes[k]].astype(f32) + more[1][:, lanes[k]].astype(f32)
            return total, grad

        for k in range(4):
            total, grad = terms(k)
            square += jnp.sum(total * total, 1, keepdims=True)
            inner += jnp.sum(grad * gain_ref[:, lanes[k]] * total, 1, keepdims=True)
        scale = lax.rsqrt(square / width + epsilon)
        back = scale * scale * scale / width * inner
        for k in range(4):
            total, grad = terms(k)
            gained = grad * gain_ref[:, lanes[k]]
            low_ref[:, lanes[k]] = (scale * gained - total * back).astype(bf16)
            normed = total * scale
            if k < 2:
                if base is None:
                    value = grad
                else:
                    value = more[0][:, lanes[k]].astype(f32) + normed * gain_ref[:, lanes[k]]
                (own_ref, give_ref)[k][...] = value.astype(kind)
            part_sum = jnp.sum(grad * normed, 0, keepdims=True)

            @pl.when(pl.program_id(0) == 0)
            def _():
                grad_ref[:, lanes[k]] = part_sum

            @pl.when(pl.program_id(0) > 0)
            def _():
                grad_ref[:, lanes[k]] += part_sum

    row = lambda i, s: (i, 0)
    whole = lambda i, s: (0, 0)
    return matmul_call(
        kernel,
        2,
        [(v, (tile, width), row) for v in (*sums, *extra)]
        + [(v, (tile, narrow), lambda i, s: (2 * s[0] + i, 0)) for v in columns]
        + [(gain[None], (1, width), whole)],
        [
            ((rows, width), bf16, (tile, width), row),
            ((rows, narrow), kind, (tile, narrow), row),
            ((rows, narrow), kind, (tile, narrow), row),
            ((1, width), f32, (1, width), whole),
        ],
        scalars=jnp.stack([block, rank]),
    )


def narrow_grads(x0, x1, beside, lows, came, y):
    half, width = x0.shape
    rows = 2 * half
    cols = came[0].shape[1]
    tile = min(512, width)

    def kernel(_, x0_ref, x1_ref, beside_ref, *refs):
        for low, other, out in zip(refs[:3], refs[3:6], refs[6:]):
            total = dot(x0_ref[...], low[:half], 0, 0) + dot(x1_ref[...], low[half:], 0, 0)
            total += dot(beside_ref[...], other[...], 0, 0)
            out[...] = total.astype(bf16)

    column = lambda n, y: (0, n)
    return matmul_call(
        kernel,
        width // tile,
        [(v, (v.shape[0], tile), column) for v in (x0, x1, beside)]
        + [(v, (rows, cols), lambda n, y: (0, y[0])) for v in lows]
        + [(v, (rows, cols), lambda n, y: (0, 0)) for v in came],
        [((width, cols), bf16, (tile, cols), lambda n, y: (n, 0))] * 3,
        flops=12 * rows * width * cols,
        mib=56,
        scalars=y[None],
    )


def half_turned(values):
    lanes = lax.broadcasted_iota(jnp.int32, values.shape, 1)
    rolled = pltpu.roll(values, HD // 2, 1)
    return jnp.where(lanes < HD // 2, -rolled, rolled)


def as_column(row):
    return jnp.broadcast_to(row, (HD, row.shape[1])).T


def as_row(values):
    return jnp.sum(values.T, 0, keepdims=True)


def project(x, w_query, w_key, w_value):
    rows, width = x.shape
    cols = w_query.shape[1]
    tile = rows // 2

    def kernel(x_ref, q_w, k_w, v_w, q_ref, k_ref, v_ref, sum_ref):
        for which, (weight, result) in enumerate(((q_w, q_ref), (k_w, k_ref))):
            value = dot(x_ref[...], weight[...])
            result[...] = value
            square = value * value
            total = square[:, :HD]
            for start in range(HD, cols, HD):
                total = total + square[:, start : start + HD]
            sum_ref[which : which + 1] = as_row(total)
        v_ref[...] = dot(x_ref[...], v_w[...]).astype(bf16)

    row = lambda i: (i, 0)
    whole = lambda i: (0, 0)
    return matmul_call(
        kernel,
        rows // tile,
        [
            (x, (tile, width), row),
            (w_query, (width, cols), whole),
            (w_key, (width, cols), whole),
            (w_value, (width, cols), whole),
        ],
        [
            ((rows, cols), f32, (tile, cols), row),
            ((rows, cols), f32, (tile, cols), row),
            ((rows, cols), bf16, (tile, cols), row),
            ((2, rows), f32, (2, tile), lambda i: (0, i)),
        ],
        flops=6 * rows * width * cols,
        mib=56,
    )


def turn_heads(query, key, squares, full_width, gain_query, gain_key, cosine, sine, block):
    rows, width = query.shape

    def kernel(q_ref, k_ref, sum_ref, gq_ref, gk_ref, cos_ref, sin_ref, qr_ref, kr_ref):
        scales = lax.rsqrt(sum_ref[...] / full_width + epsilon)
        for value, col, gain, result in ((q_ref, 0, gq_ref, qr_ref), (k_ref, 1, gk_ref, kr_ref)):
            normed = value[...] * as_column(scales[col : col + 1]) * gain[...]
            result[...] = (normed * cos_ref[...] + half_turned(normed) * sin_ref[...]).astype(bf16)

    head = lambda h: (0, h)
    whole = lambda h: (0, 0)
    return matmul_call(
        kernel,
        width // HD,
        [
            (query, (rows, HD), head),
            (key, (rows, HD), head),
            (squares, (2, rows), whole),
            (gain_query[None], (1, HD), head),
            (gain_key[None], (1, HD), head),
            (cosine, (rows, HD), lambda h: (block, 0)),
            (sine, (rows, HD), lambda h: (block, 0)),
        ],
        [((rows, width), bf16, (rows, HD), head)] * 2,
        flops=10 * rows * width,
        mib=56,
    )


BLOCK = 256


def key_span(block):
    first = max(0, block - 512 // BLOCK) * BLOCK
    return first, (block + 1) * BLOCK


def attend_heads(query, key, value, docs, blocks):
    width = query.shape[1]
    rows = len(blocks) * BLOCK
    last = blocks[-1] * BLOCK + BLOCK

    def kernel(q_ref, k_ref, v_ref, doc_ref, out_ref):
        for n, block in enumerate(blocks):
            begin, end = key_span(block)
            span = end - begin
            mine = slice(n * BLOCK, (n + 1) * BLOCK)
            own = slice(block * BLOCK, (block + 1) * BLOCK)
            scores = dot(q_ref[mine], k_ref[begin:end], 1, 1) * HD ** (-0.5)
            at_row = block * BLOCK + lax.broadcasted_iota(jnp.int32, (BLOCK, span), 0)
            at_col = begin + lax.broadcasted_iota(jnp.int32, (BLOCK, span), 1)
            doc = jnp.concatenate([as_column(doc_ref[:, own])] * (span // HD), 1)
            allowed = (doc == doc_ref[:, begin:end]) & (at_row >= at_col)
            scores = jnp.where(allowed, scores, -1e30)
            terms = jnp.exp(scores - jnp.max(scores, 1, keepdims=True))
            weights = (terms * (1.0 / jnp.sum(terms, 1, keepdims=True))).astype(bf16)
            out_ref[mine] = dot(weights, v_ref[begin:end]).astype(bf16)

    head = lambda h: (0, h)
    return matmul_call(
        kernel,
        width // HD,
        [
            (query, (rows, HD), head),
            (key, (last, HD), head),
            (value, (last, HD), head),
            (docs, docs.shape, lambda h: (0, 0)),
        ],
        [((rows, width), bf16, (rows, HD), head)],
        flops=4 * rows * last * width,
        mib=16,
    )[0]


def unattend_heads(query, key, value, grad, docs, q_proj, k_proj, squares, full_width, gain_query, gain_key, cosine, sine):
    rows, width = query.shape

    def kernel(
        q_ref, k_ref, v_ref, do_ref, doc_ref, qp_ref, kp_ref, sum_ref, gq_ref, gk_ref, cos_ref, sin_ref,
        dq_ref, dk_ref, dv_ref, dots_ref, gain_ref, q_acc, k_acc, v_acc,
    ):
        k_acc[...] = jnp.zeros_like(k_acc)
        v_acc[...] = jnp.zeros_like(v_acc)
        for block in range(rows // BLOCK):
            begin, end = key_span(block)
            span = end - begin
            mine = slice(block * BLOCK, (block + 1) * BLOCK)
            keys = k_ref[begin:end]
            do = do_ref[mine]
            scores = dot(keys, q_ref[mine], 1, 1) * HD ** (-0.5)
            at_key = begin + lax.broadcasted_iota(jnp.int32, (span, BLOCK), 0)
            at_query = block * BLOCK + lax.broadcasted_iota(jnp.int32, (span, BLOCK), 1)
            doc = jnp.concatenate([as_column(doc_ref[:, begin:end])] * (BLOCK // HD), 1)
            allowed = (doc == doc_ref[:, mine]) & (at_query >= at_key)
            scores = jnp.where(allowed, scores, -1e30)
            terms = jnp.exp(scores - jnp.max(scores, 0, keepdims=True))
            probs = terms * (1.0 / jnp.sum(terms, 0, keepdims=True))
            prob_grad = dot(v_ref[begin:end], do, 1, 1)
            inner = jnp.sum(probs * prob_grad, 0, keepdims=True)
            low = (probs * (prob_grad - inner)).astype(bf16)
            q_acc[mine] = dot(low, keys, 0, 0)
            k_acc[begin:end] += dot(low, q_ref[mine])
            v_acc[begin:end] += dot(probs.astype(bf16), do)
        dv_ref[...] = v_acc[...].astype(bf16)
        scales = lax.rsqrt(sum_ref[...] / full_width + epsilon)
        for which, (acc, proj, gain, result) in enumerate(
            ((q_acc, qp_ref, gq_ref, dq_ref), (k_acc, kp_ref, gk_ref, dk_ref))
        ):
            turned = acc[...] * HD ** (-0.5)
            normed = turned * cos_ref[...] - half_turned(turned * sin_ref[...])
            gained = normed * gain[...]
            result[...] = gained
            projected = proj[...]
            gain_ref[which : which + 1] = jnp.sum(
                normed * projected * as_column(scales[which : which + 1]), 0, keepdims=True
            )
            inner = as_row(gained * projected)

            @pl.when(pl.program_id(0) == 0)
            def _():
                dots_ref[which : which + 1] = inner

            @pl.when(pl.program_id(0) > 0)
            def _():
                dots_ref[which : which + 1] += inner

    head = lambda h: (0, h)
    whole = lambda h: (0, 0)
    column = (rows, HD)
    return matmul_call(
        kernel,
        width // HD,
        [
            (query, column, head),
            (key, column, head),
            (value, column, head),
            (grad, column, head),
            (docs, (1, rows), whole),
            (q_proj, column, head),
            (k_proj, column, head),
            (squares, (2, rows), whole),
            (gain_query[None], (1, HD), head),
            (gain_key[None], (1, HD), head),
            (cosine, column, whole),
            (sine, column, whole),
        ],
        [
            ((rows, width), f32, column, head),
            ((rows, width), f32, column, head),
            ((rows, width), bf16, column, head),
            ((2, rows), f32, (2, rows), whole),
            ((2, width), f32, (2, HD), head),
        ],
        scratch=[pltpu.VMEM((rows, HD), f32)] * 3,
        flops=10 * rows * rows * width,
        mib=56,
    )


def unscale(gained, projected, squares, dots, which, full_width, y):
    rows, cols = gained.shape
    tile = rows // 2

    def kernel(y_ref, gained_ref, proj_ref, sum_ref, dot_ref, out_ref, give_ref):
        scale = lax.rsqrt(sum_ref[which : which + 1] / full_width + epsilon)
        inner = scale**3 / full_width * dot_ref[which : which + 1]
        scale, inner = as_column(scale), as_column(inner)
        for start in range(0, cols, HD):
            lanes = slice(start, start + HD)
            out_ref[:, lanes] = (
                scale * gained_ref[:, lanes] - proj_ref[:, lanes] * inner
            ).astype(bf16)
        other = pl.multiple_of((1 - y_ref[0]) * (cols // 2), cols // 2)
        give_ref[...] = out_ref[:, pl.ds(other, cols // 2)]

    row = lambda i, y: (i, 0)
    column = lambda i, y: (0, i)
    return matmul_call(
        kernel,
        rows // tile,
        [
            (gained, (tile, cols), row),
            (projected, (tile, cols), row),
            (squares, (2, tile), column),
            (dots, (2, tile), column),
        ],
        [
            ((rows, cols), bf16, (tile, cols), row),
            ((rows, cols // 2), bf16, (tile, cols // 2), row),
        ],
        scalars=y[None],
    )


def fast_add(left, right, mib=12):
    rows, cols = left.shape
    tile = rows // 2

    def kernel(left_ref, right_ref, out_ref):
        out_ref[...] = (left_ref[...].astype(f32) + right_ref[...].astype(f32)).astype(bf16)

    row = lambda i: (i, 0)
    return matmul_call(
        kernel,
        rows // tile,
        [(left, (tile, cols), row), (right, (tile, cols), row)],
        [((rows, cols), bf16, (tile, cols), row)],
        mib=mib,
    )[0]


def pick_and_place(target, shape, use_first, first, second, row_block, col_block):
    rows, cols = first.shape
    tile = rows // 2
    steps = 2

    def kernel(spot_ref, first_ref, second_ref, *refs):
        low_ref, wide_ref = refs[-2:]

        @pl.when(spot_ref[2] == 1)
        def _():
            low_ref[...] = first_ref[...]
            wide_ref[...] = first_ref[...].astype(f32)

        @pl.when(spot_ref[2] != 1)
        def _():
            low_ref[...] = second_ref[...]
            wide_ref[...] = second_ref[...].astype(f32)

    spots = jnp.stack(
        [jnp.int32(row_block) * steps, jnp.int32(col_block), use_first.astype(jnp.int32)]
    )
    in_specs = [
        pl.BlockSpec((tile, cols), lambda i, spot: (i * spot[2], 0)),
        pl.BlockSpec((tile, cols), lambda i, spot: (i * (1 - spot[2]), 0)),
    ]
    operands = [spots, first, second]
    aliases = {}
    if target is not None:
        in_specs.append(pl.BlockSpec(memory_space=pl.ANY))
        operands.append(target)
        aliases = {3: 1}
    return pl.pallas_call(
        kernel,
        out_shape=[jax.ShapeDtypeStruct(first.shape, bf16), jax.ShapeDtypeStruct(shape, f32)],
        grid_spec=pltpu.PrefetchScalarGridSpec(
            num_scalar_prefetch=1,
            grid=(steps,),
            in_specs=in_specs,
            out_specs=[
                pl.BlockSpec((tile, cols), lambda i, spot: (i, 0)),
                pl.BlockSpec((tile, cols), lambda i, spot: (spot[0] + i, spot[1])),
            ],
        ),
        input_output_aliases=aliases,
        cost_estimate=pl.CostEstimate(
            flops=rows * cols, bytes_accessed=8 * rows * cols, transcendentals=0
        ),
        name="pick_and_place",
    )(*operands)


ORDER = [
    -2, -3, -11, 1, -4, 6, -8, -7, 5, 12, -13, -9, 14, -15, 10, 18, -19, 16, 17, 30,
    31, -32, 25, 20, -21, 33, -34, 22, 23, 24, 37, 38, -39, 188, 29, 40, -41, 44, -45, -46,
    35, -36, -121, 28, 48, -49, -122, 42, -43, -123, 50, -51, 55, -56, -47, 27, -124, 57, 52, -58,
    -53, -54, 26, 119, -125, -144, 163, -164, 59, -60, -61, 62, -63, 165, -64, 68, -69, -82, 120, -166,
    -126, -65, -145, 170, -71, -171, 70, -73, 172, -173, 167, -169, -168, 95, -96, -106, 83, -84, 146, -147,
    72, 174, -176, 74, -75, 85, 107, -108, -86, 127, 76, -78, -77, -128, 87, -88, 109, -110, -155, 148,
    -149, 178, 189, -190, -79, 179, 180, 129, -130, 187, -200, 150, -151, 111, -136, -112, -175, -181, 182, -183,
    97, 184, 185, -201, 186, 228, -202, -229, 156, -157, 131, -132, 152, -153, 66, 203, -212, 230, -231, 137,
    -138, -204, 158, -159, 133, -134, 233, -234, 213, 235, -236, 154, 237, 191, -192, -214, 80, 205, -220, -238,
    -206, 139, -140, 160, -161, 193, 135, -194, 89, 239, -240, 215, -98, -216, 241, 221, 177, 232, -242, 81,
    207, 141, -142, -90, 99, 162, -222, 195, -196, 113, -114, 243, -244, 217, -218, -91, 223, -208, 245, 197,
    -100, 143, -115, -92, -198, 93, 209, 219, 101, -102, -210, 94, 67, -224, 199, -116, 103, -104, 211, 225,
    -226, 105, 117, 118, 227,
]


class Handle:
    def __init__(self, task, index=None):
        self.task, self.index = task, index


class Task:
    def __init__(self, function, inputs, link):
        self.function, self.inputs, self.link, self.values = function, inputs, link, None
        self.handle = Handle(self, 0)


class Plan:
    window = 2

    def __init__(self):
        self.tasks = []

    def add(self, function, inputs, link):
        task = Task(function, inputs, link)
        self.tasks.append(task)
        return task

    def step(self, cost, function, *inputs, outs=1):
        task = self.add(function, inputs, ())
        if outs == 1:
            return task.handle
        return (task.handle, *[Handle(task, k) for k in range(1, outs)])

    def move(self, link, function, value):
        links = {"y": ("y_middle", "y_end")}.get(link, (link,))
        return self.add(function, (value,), links).handle

    def run(self):
        last, sent = None, {}

        def fence(task, extra):
            handles = list(task.inputs) + [h for h in extra if h not in task.inputs]
            values = [h.task.values[h.index] if isinstance(h, Handle) else h for h in handles]
            if extra:
                values = lax.optimization_barrier(tuple(values))
                for handle, fresh in zip(handles, values):
                    if isinstance(handle, Handle):
                        handle.task.values[handle.index] = fresh
            return values[: len(task.inputs)]

        for number in ORDER:
            task = self.tasks[abs(number) - 1]
            extra = [last] if last is not None else []
            for link in task.link:
                earlier = sent.setdefault(link, [])
                if len(earlier) >= self.window and earlier[-self.window] not in extra:
                    extra.append(earlier[-self.window])
                earlier.append(task.handle)
            fenced = fence(task, extra)
            result = task.function(*fenced)
            task.values = list(result) if isinstance(result, (tuple, list)) else [result]
            if number > 0:
                last = task.handle


def in_order(rank, *pieces):
    rows, cols = pieces[0].shape
    tile = rows // 2

    def kernel(rank_ref, *refs):
        for k in range(4):
            start = pl.multiple_of((rank_ref[0] ^ k) * cols, cols)
            refs[4][:, pl.ds(start, cols)] = refs[k][...]

    return pl.pallas_call(
        kernel,
        out_shape=jax.ShapeDtypeStruct((rows, 4 * cols), pieces[0].dtype),
        grid_spec=pltpu.PrefetchScalarGridSpec(
            num_scalar_prefetch=1,
            grid=(rows // tile,),
            in_specs=[pl.BlockSpec((tile, cols), lambda i, rank: (i, 0))] * 4,
            out_specs=pl.BlockSpec((tile, 4 * cols), lambda i, rank: (i, 0)),
        ),
        compiler_params=pltpu.CompilerParams(vmem_limit_bytes=56 << 20),
        cost_estimate=pl.CostEstimate(
            flops=rows * cols, bytes_accessed=16 * rows * cols, transcendentals=0
        ),
        name="in_order",
    )(rank[None], *pieces)


def fast_body(
    tokens,
    segments,
    cotangent,
    w_query,
    w_key,
    w_value,
    w_out,
    w_gate,
    w_up,
    w_down,
    gain_query,
    gain_key,
    gain_attn,
    gain_mlp,
):
    full_width = w_query.shape[0]
    row_count, _ = tokens.shape
    local_width = w_query.shape[1]
    units = w_gate.shape[1]
    rank = lax.axis_index("tensor")
    core = rank % 2
    dp_rank = lax.axis_index("dp")
    y = dp_rank % 2
    z = dp_rank // 2
    z_side = z // 2
    outer = (z == 0) | (z == 3)
    chunks = 2
    chunk = row_count // chunks
    half = chunk // 2

    plan = Plan()
    step = plan.step

    def core_move(value):
        return plan.move("core", to_core, value)

    def x_move(value):
        return plan.move("x", to_x, value)

    def y_move(value):
        return plan.move("y", lambda v: over_dp(v, SWAP_Y), value)

    def y_move_at(where, value):
        pairs = {"middle": SWAP_Y_MIDDLE, "end": SWAP_Y_END}[where]
        return plan.move("y_" + where, lambda v: over_dp(v, pairs), value)

    def z_move(which, value):
        pairs = {"in": Z_IN, "mid": Z_MID, "out": Z_OUT}[which]
        return plan.move(which, lambda v: over_dp(v, pairs), value)

    def gathered(value):
        across = x_move(value)
        return value, core_move(value), across, core_move(across)

    def ordered(pieces, cost):
        return step(cost, lambda *p: in_order(rank, *p), *pieces)

    def prepare(value):
        cosine, sine = tables(segments)
        return value, cosine[0], sine[0]

    _, cosine, sine = step(5.0, prepare, tokens, outs=3)
    parts = [tokens[j * chunk : (j + 1) * chunk] for j in range(chunks)]
    x_rows, across = [], None
    for value in parts:
        if across is not None:
            value = step(0.0, lambda v, _: v, value, across)
        pieces = gathered(value)
        across = pieces[2]
        x_rows.append(ordered(pieces, 2.9))
    near_tokens = y_move(tokens)

    def small_sum(value):
        value = step(0.6, lambda a, b: a + b, value, core_move(value))
        return step(0.6, lambda a, b: a + b, value, x_move(value))

    def joined(*values):
        return jnp.concatenate(values, 0)

    query_parts, key_parts, value_parts, rot_query, rot_key, square_parts = [], [], [], [], [], []
    for j in range(chunks):
        q, k, v, squares = step(
            8.0, lambda x: project(x, w_query, w_key, w_value), x_rows[j], outs=4
        )
        squares = small_sum(squares)
        qr, kr = step(
            4.0,
            lambda q, k, s, cos, sin, j=j: turn_heads(
                q, k, s, full_width, gain_query, gain_key, cos, sin, j
            ),
            q,
            k,
            squares,
            cosine,
            sine,
            outs=2,
        )
        query_parts.append(q)
        key_parts.append(k)
        value_parts.append(v)
        rot_query.append(qr)
        rot_key.append(kr)
        square_parts.append(squares)
    key_rot = step(1.5, joined, *rot_key)
    value_low = step(1.5, joined, *value_parts)
    query_rot = step(1.5, joined, *rot_query)
    query_proj = step(2.8, joined, *query_parts)
    key_proj = step(2.8, joined, *key_parts)
    squares = step(0.5, lambda a, b: jnp.concatenate([a, b], 1), *square_parts)

    def attend(query, key, value, j):
        per = chunk // BLOCK
        blocks = list(range(j * per, (j + 1) * per))
        block = attend_heads(query, key, value, segments, blocks)
        return jnp.concatenate([part(block, core, half, 0), part(block, 1 - core, half, 0)], 0)

    def halves(value):
        value = value.astype(bf16)
        return value[:half], value[half:]

    def chip_sum(keep, give):
        chip = step(2.4, lambda a, b: fast_add(a, b, 12), keep, core_move(give))
        return chip, x_move(chip)

    mixed, attn_sums, own_low, hid = [], [], [], []
    for j in range(chunks):
        block = step(
            5.0 + j,
            lambda q, k, v, j=j: attend(q, k, v, j),
            rot_query[j],
            *((rot_key[0], value_parts[0]) if j == 0 else (key_rot, value_low)),
        )
        mixed.append(block)
        keep, give = step(2.0, lambda m: halves(dot(m, w_out)), block, outs=2)
        chip, away = chip_sum(keep, give)

        low = step(
            3.8,
            lambda a, b, x: join_rows(a, b, x, core, gain_attn),
            chip,
            away,
            x_rows[j],
        )
        attn_sums.append((chip, away))
        own_low.append(low)
        hid += [low, core_move(low)]

    dy_pieces = gathered(step(0.0, lambda v, _: v, cotangent, chip))

    gate, up, act, outs, branch_low, mlp_gains = [], [], [], [], [], []
    for j in range(chunks):
        g, u, a, keep, give = step(
            21.6, lambda a, b: feed(a, b, w_gate, w_up, w_down), *hid[2 * j : 2 * j + 2], outs=5
        )
        gate.append(g)
        up.append(u)
        act.append(a)
        chip, away = chip_sum(keep, give)

        low, own, give, gains = step(
            4.3,
            lambda a, b, h, *dy, j=j: norm_back_rows((a, b), (), dy, h, 2 * j + core, rank, gain_mlp),
            chip,
            away,
            own_low[j],
            *dy_pieces,
            outs=4,
        )
        branch_low += [low, core_move(low)]
        outs.append((own, core_move(give)))
        mlp_gains.append(gains)

    held_tokens = step(0.0, lambda v, _: v, near_tokens, branch_low[2 * chunks - 2])
    neighbour_x = ordered(gathered(held_tokens), 4.5)

    def own_columns(pairs):
        def merge(*values):
            pieces = []
            for keep, came in zip(values[::2], values[1::2]):
                pieces += [jnp.where(core == 0, keep, came), jnp.where(core == 0, came, keep)]
            return jnp.concatenate(pieces, 0)

        return step(2.8, merge, *[v for pair in pairs for v in pair])

    output = own_columns(outs)

    def line_sum(own, mib):
        near = step(0.5 + 1.6 * mib, fast_add, own, z_move("in", own))
        total = step(0.5 + 1.6 * mib, fast_add, near, z_move("mid", near))
        return z_move("out", total), total

    def put(target, shape, spots, first, second, mib):
        if target is None:
            run = lambda a, b: pick_and_place(None, shape, outer, a, b, *spots)
            return step(2.4 + 1.4 * mib, run, first, second, outs=2)
        run = lambda a, b, t: pick_and_place(t, shape, outer, a, b, *spots)
        return step(2.4 + 1.4 * mib, run, first, second, target, outs=2)

    def set_down(target, shape, spots, value, mib):
        run = lambda v, t: place(t, shape, v, *spots)
        return step(1.9 + 0.9 * mib, run, value, target)

    def put_only(target, shape, spots, first, second, mib):
        run = lambda a, b, *t: place_one(*(t or (None,)), shape, outer, a, b, *spots)
        rest = () if target is None else (target,)
        return step(2.3 + 0.9 * mib, run, first, second, *rest)

    def sum_ends(far, near, mib):
        came = z_move("in", far)
        came = z_move("mid", step(2.1 * mib, fast_add, far, came))
        came = z_move("out", step(2.1 * mib, fast_add, near, came))
        root = step(2.1 * mib, fast_add, near, came)
        root = step(2.1 * mib, fast_add, root, y_move_at("end", root))
        first = z_move("in", root)
        second = z_move("mid", first)
        third = z_move("out", second)
        return (root, first), (third, second)

    def sum_middle(far, near, mib):
        send = step(2.1 * mib, fast_add, far, z_move("in", far))
        keep = step(2.1 * mib, fast_add, near, z_move("in", near))
        keep = step(2.1 * mib, fast_add, keep, z_move("mid", send))
        keep = step(2.1 * mib, fast_add, keep, y_move_at("middle", keep))
        other = z_move("mid", keep)
        return (z_move("out", keep), keep), (z_move("out", other), other)

    down_grad, shape = None, (units, full_width)

    def place_z(target, k, sums):
        for side, pair in ((z_side, sums[0]), (1 - z_side, sums[1])):
            target = put_only(target, shape, (2 * k + side, 0), *pair, 1.0)
        return target

    kinds = (2, 1, 0, 1)
    for k in (0, 2):
        sides = [y if kinds[k + n] == 0 else z_side for n in range(2)]
        which = jnp.stack(
            [2 * k + 1 - sides[0], 2 * k + sides[0], 2 * k + 3 - sides[1], 2 * k + 2 + sides[1]]
        )
        blocks = step(
            11.0,
            lambda *v, which=which: down_grad_rows(v[:chunks], v[chunks:], which),
            *act,
            *branch_low,
            outs=4,
        )
        for n in range(2):
            far, near = blocks[2 * n : 2 * n + 2]
            if kinds[k + n] == 1:
                down_grad = place_z(down_grad, k + n, sum_ends(far, near, 1.0))
                continue
            if kinds[k + n] == 2:
                down_grad = place_z(down_grad, k + n, sum_middle(far, near, 1.0))
                continue
            own = step(2.1, fast_add, near, y_move(far))
            spot = 2 * (k + n)
            piece, down_grad = put(down_grad, shape, (spot + y, 0), *line_sum(own, 1.0), 1.0)
            down_grad = set_down(down_grad, shape, (spot + 1 - y, 0), y_move(piece), 1.0)

    lows = []
    for j in range(chunks):
        lows.append(
            step(
                11.6,
                lambda a, b, gate, up: unfeed(a, b, w_down, gate, up, y),
                *branch_low[2 * j : 2 * j + 2],
                gate[j],
                up[j],
                outs=4,
            )
        )

    near = []
    for low in own_low:
        came = y_move(low)
        near += [came, core_move(came)]
    wide = []
    for which in range(2):
        pieces = step(
            13.8,
            lambda *v: wide_grad(v[:4], v[4:8], *v[8:]),
            *hid,
            *near,
            *[low[2 + which] for low in lows],
            *[y_move(low[which]) for low in lows],
            outs=2,
        )
        result, shape = None, (full_width, units)
        for q, own in enumerate(pieces):
            piece, result = put(result, shape, (0, 2 * y + q), *line_sum(own, 2.0), 2.0)
            result = set_down(result, shape, (0, 2 * (1 - y) + q), y_move(piece), 2.0)
        wide.append(result)
    gate_grad, up_grad = wide

    hidden_grad, attn_low, attn_gains = [], [], []
    for j in range(chunks):
        keep, give = step(
            14.3,
            lambda *v: unwide(*v, w_gate, w_up, y),
            *lows[j],
            outs=2,
        )
        chip, away = chip_sum(keep, give)

        low, own, give, gains = step(
            4.6,
            lambda a, b, c, d, *dy, j=j: norm_back_rows(
                (a, b), (c, d), dy, None, 2 * j + core, rank, gain_attn
            ),
            *attn_sums[j],
            chip,
            away,
            *dy_pieces,
            outs=4,
        )
        hidden_grad.append((own, core_move(give)))
        attn_gains.append(gains)
        attn_low += [low, core_move(low)]
    grad_own = own_columns(hidden_grad)
    whole_attn_low = step(3.0, joined, *attn_low)

    def unmix(low):
        grad = dot(low, w_out, 1, 1).astype(bf16)
        ordered = []
        for j in range(chunks):
            block = grad[j * chunk : (j + 1) * chunk]
            ordered += [part(block, core, half, 0), part(block, 1 - core, half, 0)]
        return jnp.concatenate(ordered, 0)

    mixed_grad = step(4.0, unmix, whole_attn_low)

    query_gained, key_gained, value_grad_low, dots, head_gains = step(
        19.5,
        lambda q, k, v, m, qp, kp, s, cos, sin: unattend_heads(
            q, k, v, m, segments, qp, kp, s, full_width, gain_query, gain_key, cos, sin
        ),
        query_rot,
        key_rot,
        value_low,
        mixed_grad,
        query_proj,
        key_proj,
        squares,
        cosine,
        sine,
        outs=5,
    )
    dots = small_sum(dots)

    def scaled_back(which, gained, projected):
        run = lambda g, p, s, d: unscale(g, p, s, d, which, full_width, y)
        return step(2.0, run, gained, projected, squares, dots, outs=2)

    query_low, query_give = scaled_back(0, query_gained, query_proj)
    key_low, key_give = scaled_back(1, key_gained, key_proj)
    value_give = step(
        1.0, lambda v: part(v, 1 - y, local_width // 2, 1), value_grad_low
    )

    def pair_grad(left, right, shape):
        rows = shape[0] // 2
        give = step(
            4.7, lambda a, b: dot(part(a, 1 - y, rows, 1), b, 0, 0).astype(bf16), left, right
        )
        own = step(
            4.8,
            lambda a, b, c: (dot(part(a, y, rows, 1), b, 0, 0) + c.astype(f32)).astype(bf16),
            left,
            right,
            y_move(give),
        )
        piece, result = put(None, shape, (y, 0), *line_sum(own, 1.0), 1.0)
        return set_down(result, shape, (1 - y, 0), y_move(piece), 1.0)

    whole_mixed = step(1.5, joined, *mixed)
    out_grad = pair_grad(whole_mixed, whole_attn_low, (local_width, full_width))

    came = [y_move(give) for give in (value_give, query_give, key_give)]
    pieces = step(
        11.0,
        lambda x0, x1, n, v, q, k, cv, cq, ck: narrow_grads(
            x0, x1, n, (v, q, k), (cv, cq, ck), y
        ),
        *x_rows,
        neighbour_x,
        value_grad_low,
        query_low,
        key_low,
        *came,
        outs=3,
    )
    narrow_results = []
    for own in pieces:
        shape = (full_width, local_width)
        piece, result = put(None, shape, (0, y), *line_sum(own, 1.0), 1.0)
        narrow_results.append(set_down(result, shape, (0, 1 - y), y_move(piece), 1.0))
    value_wgrad, query_wgrad, key_wgrad = narrow_results

    give, keep = step(
        11.7,
        lambda *v: input_columns(v, (w_query, w_key, w_value), core),
        query_low,
        key_low,
        value_grad_low,
        outs=2,
    )
    x_here = rank // 2

    def chip_columns(keep, came):
        total = low_add(keep, came)
        return (
            lax.dynamic_index_in_dim(total, x_here, 0, False),
            lax.dynamic_index_in_dim(total, 1 - x_here, 0, False),
        )

    here, there = step(3.5, chip_columns, keep, core_move(give), outs=2)
    input_grad = step(
        2.0,
        lambda a, b, c: (a.astype(f32) + b.astype(f32) + c).astype(bf16),
        here,
        x_move(there),
        grad_own,
    )

    wide_gains = step(
        0.3, lambda a, b, c, d: joined(a + b, c + d), *mlp_gains, *attn_gains
    )

    def masked(a, b):
        mine = jnp.arange(full_width) // (full_width // 2) == rank // 2
        return jnp.where(mine, a + b, 0.0)

    wide_gains = step(0.3, masked, wide_gains, core_move(wide_gains))
    gains = step(
        1.0,
        lambda a, b, h: jnp.concatenate([(a + b).reshape(-1), h.reshape(-1)]),
        wide_gains,
        x_move(wide_gains),
        head_gains,
    )
    gains = step(0.2, lambda a, b: a + b, gains, y_move(gains))
    gains = step(0.2, lambda a, b: a + b, gains, z_move("in", gains))
    gains = step(0.2, lambda a, b: a + b, gains, z_move("mid", gains))
    gains = step(0.2, lambda a, b: jnp.where(outer, a, b), z_move("out", gains), gains)

    plan.run()
    results = (
        output,
        input_grad,
        query_wgrad,
        key_wgrad,
        value_wgrad,
        out_grad,
        gate_grad,
        up_grad,
        down_grad,
        gains,
    )
    values = [r.task.values[r.index] for r in results]
    gains = values.pop()
    return (
        *values,
        gains[2 * full_width : 2 * full_width + local_width],
        gains[2 * full_width + local_width :],
        gains[full_width : 2 * full_width],
        gains[:full_width],
    )


def solution(mesh):
    in_specs = (
        P("dp", "tensor"),
        P("dp", None),
        P("dp", "tensor"),
        P(None, "tensor"),
        P(None, "tensor"),
        P(None, "tensor"),
        P("tensor", None),
        P(None, "tensor"),
        P(None, "tensor"),
        P("tensor", None),
        P("tensor"),
        P("tensor"),
        P(),
        P(),
    )
    out_specs = (
        P("dp", "tensor"),
        P("dp", "tensor"),
        P(None, "tensor"),
        P(None, "tensor"),
        P(None, "tensor"),
        P("tensor", None),
        P(None, "tensor"),
        P(None, "tensor"),
        P("tensor", None),
        P("tensor"),
        P("tensor"),
        P(),
        P(),
    )
    body = fast_body if dict(mesh.shape) == {"dp": 8, "tensor": 4} else general_body
    return jax.shard_map(body, mesh=mesh, in_specs=in_specs, out_specs=out_specs, check_vma=False)
```
